256 devices in a mesh: seq: 64 (over y, z, core), pool: 4 (over x).
Axes of the slice: x: 4, y: 4, z: 8, core: 2. Of those that a mesh axis runs over, the one named last changes fastest.
Arguments:
- query_rows: bfloat16 [32768, 4096], P('seq', 'pool'), may hold values from -6 to 6
- key_rows: bfloat16 [32768, 4096], P('seq', 'pool'), may hold values from -6 to 6
- value_rows: bfloat16 [32768, 4096], P('seq', 'pool'), may hold values from -6 to 6
- log_decay: float32 [32, 32768], P('pool', 'seq'), may hold values from -0.7 to 0
- residual: bfloat16 [32768, 4096], P(('seq', 'pool')), may hold values from -6 to 6
- out_weight: bfloat16 [4096, 4096], P('pool', 'seq'), may hold values from -0.09375 to 0.09375
- norm_gain: float32 [4096], replicated, may hold values from 0.5 to 1.5
- kv_weight: bfloat16 [4096, 1024], P('seq'), may hold values from -0.09375 to 0.09375
- block_table: int32 [256, 2], P(('seq', 'pool')), may hold values from 0 to 3, as said below
Outputs:
- page_cache: bfloat16 [64, 4, 2, 128, 1024], P('seq', 'pool')
The draws below stay inside these ranges and needn't reach their ends.
Inputs may be any that keep to these rules, and one draw needn't show every extreme that they name: `block_table`: column 0 is a page's pool device, column 1 its slot there. The pages of one index of seq go to pool devices of that same index, no two to the same device and slot; one pool device receives exactly 2 of them, each other at most 2, and all 1 pages of some device go to that one.
All inputs are finite; a program needn't handle non-finite values.
Results may differ from the reference program's by a relative error of at most 0.0056.
Values may be sent and summed in bfloat16 or wider, within the bound.
A program may use at most 128 MiB of HBM per device.

```python
import jax
import jax.numpy as jnp
from jax import lax

D = 4096
RETENTION_HEADS = 32
HD = 128
PAGE = 128
BLK = 512
TOK_DEV = 512
PROMPT_TOKENS = 32768
KVW = 1024
PAGES_DEV = 1
SLOTS = 2
NPAGES = 256
N_SEQ = 64
N_POOL = 4


def draw_log_decay(key, part):
    parallel_lanes = jax.random.split(key, 7)
    slow_share = 0.5
    slow_heads = jax.random.uniform(parallel_lanes[0], (RETENTION_HEADS,)) < slow_share
    fast_rate = jnp.exp(jax.random.uniform(parallel_lanes[1], (RETENTION_HEADS,), minval=jnp.log(1.0 / 50.0), maxval=jnp.log(1.0 / 30.0)))
    slow_rate = jnp.exp(jax.random.uniform(parallel_lanes[2], (RETENTION_HEADS,), minval=jnp.log(0.03), maxval=jnp.log(0.25))) / PROMPT_TOKENS
    base_rate = jnp.where(slow_heads, slow_rate, fast_rate)
    block_factor = jnp.exp(jax.random.uniform(parallel_lanes[3], (RETENTION_HEADS, N_SEQ), minval=jnp.log(0.5), maxval=jnp.log(2.0)))
    block_factor = jnp.repeat(block_factor, TOK_DEV, axis=1)
    jitter = jax.random.uniform(parallel_lanes[4], (RETENTION_HEADS, PROMPT_TOKENS), minval=0.5, maxval=1.5)
    decay_speed = base_rate[:, None] * block_factor * jitter
    token_positions = jnp.arange(PROMPT_TOKENS, dtype=jnp.int32)
    spike_locations = jax.random.randint(parallel_lanes[5], (RETENTION_HEADS, 2), 0, PROMPT_TOKENS)
    spike_events = jnp.any(token_positions[None, :, None] == spike_locations[:, None, :], axis=-1)
    spike_keep_mask = jax.random.uniform(parallel_lanes[6], (RETENTION_HEADS, PROMPT_TOKENS), minval=0.5, maxval=0.8)
    return jnp.where(spike_events, jnp.log(spike_keep_mask), -decay_speed).astype(jnp.float32)


def draw_block_table(key, part):
    group_pages = PAGES_DEV * N_POOL

    def one_group(group_key):
        parallel_lanes = jax.random.split(group_key, 6)
        heavy = jax.random.randint(parallel_lanes[0], (), 0, N_POOL)
        source = jax.random.randint(parallel_lanes[1], (), 0, N_POOL)
        page_ids = jnp.arange(group_pages, dtype=jnp.int32)
        shuffled = jax.random.permutation(parallel_lanes[2], group_pages)
        ranking_score = jnp.where(page_ids // PAGES_DEV == source, -1, shuffled)
        ranking = jnp.argsort(jnp.argsort(ranking_score, stable=True), stable=True)
        to_heavy = ranking < SLOTS
        others = (heavy + 1 + jax.random.randint(parallel_lanes[3], (group_pages,), 0, N_POOL - 1)) % N_POOL
        owners = jnp.where(to_heavy, heavy, others).astype(jnp.int32)
        order = jax.random.permutation(parallel_lanes[4], group_pages)
        same_owner = owners[:, None] == owners[None, :]
        earlier = order[None, :] < order[:, None]
        place_rank = jnp.sum(jnp.logical_and(same_owner, earlier).astype(jnp.int32), axis=1)
        shifts = jax.random.randint(parallel_lanes[5], (N_POOL,), 0, SLOTS)
        slot_ids = (place_rank + shifts[owners]) % SLOTS
        return jnp.stack([owners, slot_ids.astype(jnp.int32)], axis=1)
    tables = jax.vmap(one_group)(jax.random.split(key, N_SEQ))
    return tables.reshape(NPAGES, 2).astype(jnp.int32)


def steps_of(stream_key, extent, pieces, least, top_value):
    factor_of = 1.0
    for axis_at, shards_of in pieces:
        draws = jax.random.uniform(jax.random.fold_in(jax.random.fold_in(stream_key, 6), axis_at), (shards_of,), jnp.float32, least / len(pieces), top_value / len(pieces))
        factor_of = factor_of * jnp.repeat(jnp.exp(draws), extent[axis_at] // shards_of).reshape((-1,) + (1,) * (len(extent) - 1 - axis_at))
    return factor_of


def centred(key, extent, width, reach, cuts=(), kind=jnp.bfloat16):
    values = width * jax.random.normal(key, extent, jnp.float32)
    if cuts:
        values = values * steps_of(key, extent, cuts, -0.22, 0.18)
    return jnp.clip(values, -reach, reach).astype(kind)


def setup_inputs(seed: int = 0) -> dict:
    seeds = jax.random.split(jax.random.key(seed), 10)
    query_rows = centred(seeds[0], (PROMPT_TOKENS, RETENTION_HEADS * HD), 1.0, 6.0, ((0, 64), (1, 4)))
    key_rows = centred(seeds[1], (PROMPT_TOKENS, RETENTION_HEADS * HD), 1.0, 6.0, ((0, 64), (1, 4)))
    value_rows = centred(seeds[2], (PROMPT_TOKENS, RETENTION_HEADS * HD), 1.0, 6.0, ((0, 64), (1, 4)))
    log_decay = draw_log_decay(jax.random.fold_in(seeds[9], 71), 0)
    residual = centred(seeds[4], (PROMPT_TOKENS, D), 1.0, 6.0, ((0, 256),))
    out_weight = centred(seeds[5], (RETENTION_HEADS * HD, D), D ** -0.5, 0.09375, ((0, 4), (1, 64)))
    norm_gain = jnp.clip(1.0 + 0.1 * jax.random.normal(seeds[6], (D,), jnp.float32), 0.5, 1.5)
    kv_weight = centred(seeds[7], (D, KVW), D ** -0.5, 0.09375, ((0, 64),))
    block_table = draw_block_table(jax.random.fold_in(seeds[9], 71), 0)
    return {"query_rows": query_rows, "key_rows": key_rows, "value_rows": value_rows, "log_decay": log_decay, "residual": residual, "out_weight": out_weight, "norm_gain": norm_gain, "kv_weight": kv_weight, "block_table": block_table}


def retention(query_rows, key_rows, value_rows, log_decay):
    block_count = PROMPT_TOKENS // BLK

    def split_heads(matrix):
        return matrix.reshape(block_count, BLK, RETENTION_HEADS, HD).transpose(0, 2, 1, 3)
    queries = split_heads(query_rows)
    key_heads = split_heads(key_rows)
    value_heads = split_heads(value_rows)
    decays = log_decay.reshape(RETENTION_HEADS, block_count, BLK).transpose(1, 0, 2)
    lower_mask = jnp.tril(jnp.ones((BLK, BLK), dtype=bool))

    def advance(carried, inputs):
        query_blk, key_blk, value_blk, decay_blk = inputs
        cumulative = jnp.cumsum(decay_blk, axis=1)
        block_total = cumulative[:, -1]
        log_gap = jnp.where(lower_mask[None], cumulative[:, :, None] - cumulative[:, None, :], 0.0)
        products = jnp.einsum('hid,hjd->hij', query_blk.astype(jnp.float32), key_blk.astype(jnp.float32))
        scores = jnp.where(lower_mask[None], products * jnp.exp(log_gap), 0.0).astype(jnp.bfloat16)
        inner = jnp.einsum('hij,hjd->hid', scores.astype(jnp.float32), value_blk.astype(jnp.float32))
        outer = jnp.einsum('hid,hde->hie', query_blk.astype(jnp.float32), carried, precision=lax.Precision.HIGHEST) * jnp.exp(cumulative)[:, :, None]
        weighted = (key_blk.astype(jnp.float32) * jnp.exp(block_total[:, None] - cumulative)[:, :, None]).astype(jnp.bfloat16)
        update = jnp.einsum('hjd,hje->hde', weighted.astype(jnp.float32), value_blk.astype(jnp.float32))
        carried = jnp.exp(block_total)[:, None, None] * carried + update
        return (carried, inner + outer)
    initial = jnp.zeros((RETENTION_HEADS, HD, HD), dtype=jnp.float32)
    _, retained = lax.scan(advance, initial, (queries, key_heads, value_heads, decays))
    scaled = retained * lax.rsqrt(lax.optimization_barrier(jnp.mean(retained * retained, axis=-1, keepdims=True)) + 1e-05)
    return scaled.transpose(0, 2, 1, 3).reshape(PROMPT_TOKENS, RETENTION_HEADS * HD).astype(jnp.bfloat16)

def reference(query_rows, key_rows, value_rows, log_decay, residual, out_weight, norm_gain, kv_weight, block_table):
    mixed = retention(query_rows, key_rows, value_rows, log_decay)

    def finish(pair):
        mixed_blk, resid_blk = pair
        hidden = resid_blk.astype(jnp.float32) + jnp.dot(mixed_blk, out_weight, preferred_element_type=jnp.float32)
        normed = (hidden * lax.rsqrt(lax.optimization_barrier(jnp.mean(hidden * hidden, axis=-1, keepdims=True)) + 1e-05) * norm_gain).astype(jnp.bfloat16)
        return jnp.dot(normed, kv_weight, preferred_element_type=jnp.float32).astype(jnp.bfloat16)
    kv_all = lax.map(finish, (mixed.reshape(N_SEQ, TOK_DEV, RETENTION_HEADS * HD), residual.reshape(N_SEQ, TOK_DEV, D)))
    pages = kv_all.reshape(N_SEQ, TOK_DEV // PAGE, PAGE, KVW)
    table = block_table.reshape(N_SEQ, TOK_DEV // PAGE, 2)
    group = jnp.broadcast_to(jnp.arange(N_SEQ, dtype=jnp.int32)[:, None], (N_SEQ, TOK_DEV // PAGE))
    page_cache = jnp.zeros((N_SEQ, N_POOL, SLOTS, PAGE, KVW), dtype=jnp.bfloat16)
    page_cache = page_cache.at[group, table[..., 0], table[..., 1]].set(pages)
    return page_cache
```

```python
import jax
import jax.numpy as jnp
from jax import lax
from jax.experimental import pallas as pl
from jax.experimental.pallas import tpu as pltpu
from jax.sharding import PartitionSpec as P

NY, NZ, NX = 4, 8, 4
HEADS = 8
HD = 128
BLK = 512
PAGE = 128
D = 4096
KVW = 1024
CH = 8
CW = D // CH
DW = CW // 2
NT = 4
TW = KVW // NT
F32 = jnp.float32
BF16 = jnp.bfloat16
MESH = pl.DeviceIdType.MESH
NT_DIMS = (((1,), (1,)), ((), ()))
TN_DIMS = (((0,), (0,)), ((), ()))
HIGH = lax.Precision.HIGHEST


def kernel(
    wt, kw, q_hbm, k_hbm, v_hbm, ld, res_hbm, gain, tbl,
    pages, tables,
    gw, gk, q_s, k_s, v_s, res_s, crow, ccol, a_s, a_r, u_s, inner, mixed,
    ub_s, ub_r, st_s, st_r, sr_s, sr_r, se_s, se_r, sf_s, sf_r, state,
    part, rs_s, rs_r, hid, norm, pg, tb,
    ld_sem, w_zs, w_ys, w_fs, w_ps, w_r, w_p,
    k_zs, k_ys, k_fs, k_ps, k_r, k_h, k_p,
    s1_s, s1_r, s2_s, s2_r, s3_s, s3_r, s4_s, s4_r, s5_s, s5_r,
    rs_ss, rs_rs, g_s, g_f, g_r, t_s, t_r,
):
    me = lax.axis_index("seq")
    x = lax.axis_index("pool")
    y = lax.div(me, 16)
    z = lax.rem(lax.div(me, 2), 8)
    c = lax.rem(me, 2)

    def at(yy, zz, cc):
        return (yy * NZ + zz) * 2 + cc

    def mod(value, size):
        return lax.rem(value + size, size)

    up = (at(mod(y + 1, NY), z, c), x)
    down = (at(mod(y - 1, NY), z, c), x)
    ahead = (at(y, mod(z + 1, NZ), c), x)
    behind = (at(y, mod(z - 1, NZ), c), x)
    partner = (at(y, z, 1 - c), x)
    right = (me, mod(x + 1, NX))
    left = (me, mod(x - 1, NX))

    def send(src, dst, ssem, rsem, device):
        copy = pltpu.make_async_remote_copy(
            src_ref=src, dst_ref=dst, send_sem=ssem, recv_sem=rsem,
            device_id=device, device_id_type=MESH,
        )
        return copy

    def arrive(ref, rsem):
        send(ref, ref, rsem, rsem, partner).wait_recv()

    def sent(ref, ssem):
        send(ref, ref, ssem, ssem, partner).wait_send()

    peers = [partner]
    peers += [(at(y, mod(z + m, NZ), c), x) for m in range(1, NZ)]
    peers += [(at(mod(y + m, NY), z, c), x) for m in range(1, NY)]
    peers += [(me, mod(x + m, NX)) for m in range(1, NX)]
    barrier = pltpu.get_barrier_semaphore()
    for peer in peers:
        pl.semaphore_signal(barrier, inc=1, device_id=peer, device_id_type=MESH)
    loads = [
        pltpu.make_async_copy(k_hbm, k_s, ld_sem.at[0]),
        pltpu.make_async_copy(v_hbm, v_s, ld_sem.at[1]),
        pltpu.make_async_copy(q_hbm, q_s, ld_sem.at[2]),
        pltpu.make_async_copy(res_hbm, res_s, ld_sem.at[3]),
        pltpu.make_async_copy(wt, gw.at[me], ld_sem.at[4]),
        pltpu.make_async_copy(kw, gk.at[me], ld_sem.at[5]),
    ]
    for load in loads:
        load.start()
    pl.semaphore_wait(barrier, len(peers))

    def near(i):
        half = lax.div(i + 1, 2)
        return mod(z + half * (1 - 2 * lax.rem(i, 2)), NZ)

    row_step = (0, 3, 1, 2)

    def slot(r, i):
        return at(mod(y + row_step[r], NY), near(i), c)

    def w_rows(src, s, i):
        send(src, gw.at[s], w_ys.at[0, i], w_r.at[1, i], up).start()
        send(src, gw.at[s], w_ys.at[1, i], w_r.at[2, i], down).start()

    def w_pass(src, s, r, i):
        send(src, gw.at[s], w_ps.at[r, i], w_p.at[r, i], partner).start()

    def w_start():
        send(wt, gw.at[me], w_zs.at[0, 0], w_r.at[0, 1], ahead).start()
        send(wt, gw.at[me], w_zs.at[1, 0], w_r.at[0, 2], behind).start()
        w_rows(wt, me, 0)
        w_pass(wt, me, 0, 0)

    def w_along(i):
        s = slot(0, i)
        odd = lax.rem(i, 2)
        arrive(gw.at[s], w_r.at[0, i])

        @pl.when(i <= 5)
        def _():
            target = (at(y, mod(z + 2 * odd - 1, NZ), c), x)
            send(
                gw.at[s], gw.at[s], w_zs.at[1 - odd, lax.div(i + 1, 2)],
                w_r.at[0, i + 2], target,
            ).start()

        w_rows(gw.at[s], s, i)
        w_pass(gw.at[s], s, 0, i)

    def w_across(i):
        below, above = slot(1, i), slot(2, i)
        even = lax.rem(i, 2) == 0
        arrive(gw.at[below], w_r.at[1, i])
        arrive(gw.at[above], w_r.at[2, i])
        s = jnp.where(even, below, above)
        target = (jnp.where(even, up[0], down[0]), x)
        send(gw.at[s], gw.at[s], w_fs.at[i], w_r.at[3, i], target).start()
        w_pass(gw.at[below], below, 1, i)
        w_pass(gw.at[above], above, 2, i)

    def w_last(i):
        s = slot(3, i)
        arrive(gw.at[s], w_r.at[3, i])
        w_pass(gw.at[s], s, 3, i)

    def k_along(src, s, r):
        send(src, gk.at[s], k_zs.at[0, r, 0], k_r.at[r, 1], ahead).start()
        send(src, gk.at[s], k_zs.at[1, r, 0], k_r.at[r, 2], behind).start()
        send(src, gk.at[s], k_ps.at[r, 0], k_p.at[r, 0], partner).start()

    def k_start():
        send(kw, gk.at[me], k_ys.at[0], k_r.at[1, 0], up).start()
        send(kw, gk.at[me], k_ys.at[1], k_r.at[2, 0], down).start()
        k_along(kw, me, 0)

    def k_across():
        below, above = slot(1, 0), slot(2, 0)
        arrive(gk.at[below], k_r.at[1, 0])
        arrive(gk.at[above], k_r.at[2, 0])
        low = gk.at[below, pl.ds(0, 32)]
        top = gk.at[above, pl.ds(32, 32)]
        send(low, low, k_fs.at[0], k_h.at[0], up).start()
        send(top, top, k_fs.at[1], k_h.at[1], down).start()
        k_along(gk.at[below], below, 1)
        k_along(gk.at[above], above, 2)

    def k_last():
        s = slot(3, 0)
        arrive(gk.at[s, pl.ds(0, 32)], k_h.at[0])
        arrive(gk.at[s, pl.ds(32, 32)], k_h.at[1])
        k_along(gk.at[s], s, 3)

    def k_ring(i):
        odd = lax.rem(i, 2)
        for r in range(NY):
            s = slot(r, i)
            arrive(gk.at[s], k_r.at[r, i])

            @pl.when(i <= 5)
            def _():
                target = (at(y, mod(z + 2 * odd - 1, NZ), c), x)
                send(
                    gk.at[s], gk.at[s], k_zs.at[1 - odd, r, lax.div(i + 1, 2)],
                    k_r.at[r, i + 2], target,
                ).start()

            send(gk.at[s], gk.at[s], k_ps.at[r, i], k_p.at[r, i], partner).start()

    w_start()
    for m in range(1, NX):
        target = (me, mod(x + m, NX))
        send(tbl, tb.at[x], t_s.at[m - 1], t_r.at[m - 1], target).start()

    steps_a = lax.broadcasted_iota(jnp.int32, (BLK, BLK), 0)
    steps_b = lax.broadcasted_iota(jnp.int32, (BLK, BLK), 1)
    lower = jnp.where(steps_b <= steps_a, 1.0, 0.0).astype(F32)
    decay = ld[...]
    sums_row = lax.dot_general(decay, lower, NT_DIMS, precision=HIGH, preferred_element_type=F32)
    sums_col = lax.dot_general(lower, decay, NT_DIMS, precision=HIGH, preferred_element_type=F32)
    for h in range(HEADS):
        crow[h] = sums_row[h : h + 1, :]
        wide = jnp.broadcast_to(sums_col[:, h : h + 1], (BLK, HD))
        ccol[h] = wide
        a_s[h] = jnp.broadcast_to(wide[BLK - 1 : BLK, :], (8, HD))

    def head_cols(h):
        return pl.ds(pl.multiple_of(h * HD, HD), HD)

    loads[0].wait()
    loads[1].wait()

    def update(h, carry):
        cb = ccol[h]
        gap = jnp.exp(cb[BLK - 1 : BLK, :] - cb)
        weighted = (k_s[:, head_cols(h)].astype(F32) * gap).astype(BF16)
        u_s[h] = lax.dot_general(
            weighted, v_s[:, head_cols(h)], TN_DIMS, preferred_element_type=F32
        )
        return carry

    lax.fori_loop(0, HEADS, update, 0)
    ub_s[...] = u_s[pl.ds(4 * (1 - c), 4)].astype(BF16)
    send(ub_s, ub_r, s1_s.at[0], s1_r.at[0], partner).start()
    send(a_s, a_r, s1_s.at[1], s1_r.at[1], partner).start()

    def chip_parts():
        own = u_s[pl.ds(4 * c, 4)]
        other = ub_r[...].astype(F32)
        a_own = a_s[pl.ds(4 * c, 4)]
        a_other = a_r[pl.ds(4 * c, 4)]
        first = c == 0
        return (
            jnp.where(first, own, other),
            jnp.where(first, other, own),
            jnp.where(first, a_own, a_other),
            jnp.where(first, a_other, a_own),
        )

    def scan_chip():
        arrive(ub_r, s1_r.at[0])
        arrive(a_r, s1_r.at[1])
        u0, u1, a0, a1 = chip_parts()
        total = jnp.exp(a1)[:, 0:1, :] * u0 + u1
        a_chip = a0 + a1
        rows = lax.broadcasted_iota(jnp.int32, (16, HD), 0)
        for hl in range(4):
            a = jnp.broadcast_to(a_chip[hl, 0:1, :], (16, HD))
            hi = a.astype(BF16).astype(F32)
            mid = (a - hi).astype(BF16).astype(F32)
            low = a - hi - mid
            tile = jnp.where(rows == 0, hi, jnp.where(rows == 1, mid, jnp.where(rows == 2, low, 0.0)))
            for half in range(2):
                st_s[2 * hl + half, 0:64, :] = total[hl, 64 * half : 64 * half + 64, :].astype(BF16)
                st_s[2 * hl + half, 64:80, :] = tile.astype(BF16)
        st_r[z] = st_s[z]
        for m in range(1, NZ):
            zz = mod(z + m, NZ)
            send(st_s.at[zz], st_r.at[z], s2_s.at[m], s2_r.at[m], (at(y, zz, c), x)).start()

    def chip_total(zz):
        message = st_r[zz].astype(F32)
        return message[0:64, :], jnp.sum(message[64:80, :], axis=0, keepdims=True)

    def scan_row():
        for m in range(1, NZ):
            arrive(st_r.at[mod(z - m, NZ)], s2_r.at[m])
        total = jnp.zeros((64, HD), F32)
        a_row = jnp.zeros((1, HD), F32)
        for zz in range(NZ):
            t, a = chip_total(zz)
            total = jnp.exp(a) * total + t
            a_row = a_row + a
        sr_s[0:64, :] = total
        sr_s[64:72, :] = jnp.broadcast_to(a_row, (8, HD))
        sr_r[y] = sr_s[...]
        for m in range(1, NY):
            target = (at(mod(y + m, NY), z, c), x)
            send(sr_s, sr_r.at[y], s3_s.at[m], s3_r.at[m], target).start()

    def scan_back():
        for m in range(1, NY):
            arrive(sr_r.at[mod(y - m, NY)], s3_r.at[m])
        enter = jnp.zeros((64, HD), F32)
        for yy in range(NY):
            moved = jnp.exp(sr_r[yy, 64:65, :]) * enter + sr_r[yy, 0:64, :]
            enter = jnp.where(yy < y, moved, enter)
        for zz in range(NZ):
            se_s[zz] = enter.astype(BF16)
            t, a = chip_total(zz)
            enter = jnp.exp(a) * enter + t
        se_r[z] = se_s[z]
        for m in range(1, NZ):
            zz = mod(z + m, NZ)
            send(se_s.at[zz], se_r.at[z], s4_s.at[m], s4_r.at[m], (at(y, zz, c), x)).start()

    def scan_cores():
        for m in range(1, NZ):
            arrive(se_r.at[mod(z - m, NZ)], s4_r.at[m])
        enter = se_r[...].reshape(4, HD, HD).astype(F32)
        u0, _, a0, _ = chip_parts()
        after = jnp.exp(a0)[:, 0:1, :] * enter + u0
        first = c == 0
        sf_s[...] = jnp.where(first, after, enter).astype(BF16)
        send(sf_s, sf_r, s5_s.at[0], s5_r.at[0], partner).start()
        state[pl.ds(4 * c, 4)] = jnp.where(first, enter, after).astype(BF16)

    loads[2].wait()
    loads[4].wait()
    loads[5].wait()

    tri_a = lax.broadcasted_iota(jnp.int32, (HD, HD), 0)
    tri_b = lax.broadcasted_iota(jnp.int32, (HD, HD), 1)
    seen = tri_b <= tri_a

    def within(h, carry):
        @pl.when(h == 1)
        def _():
            scan_chip()

        @pl.when(h == 4)
        def _():
            scan_row()

        @pl.when(h == 5)
        def _():
            k_start()

        @pl.when(h == 6)
        def _():
            scan_back()

        for tq in range(4):
            rows = pl.ds(tq * HD, HD)
            width = HD * (tq + 1)
            products = lax.dot_general(
                q_s[rows, head_cols(h)], k_s[0:width, head_cols(h)], NT_DIMS,
                preferred_element_type=F32,
            )
            c_here = ccol[h, rows, :]
            blocks = []
            for ts in range(tq + 1):
                gap = c_here - crow[h, :, ts * HD : ts * HD + HD]
                piece = products[:, ts * HD : ts * HD + HD]
                if ts == tq:
                    gap = jnp.where(seen, gap, 0.0)
                    piece = jnp.where(seen, piece, 0.0)
                blocks.append((piece * jnp.exp(gap)).astype(BF16))
            scores = jnp.concatenate(blocks, axis=1) if tq else blocks[0]
            inner[rows, head_cols(h)] = jnp.dot(
                scores, v_s[0:width, head_cols(h)], preferred_element_type=F32
            )

        @pl.when(h >= 1)
        def _():
            w_along(h)

        return carry

    lax.fori_loop(0, HEADS, within, 0)
    scan_cores()
    w_across(0)
    w_across(1)
    arrive(sf_r, s5_r.at[0])
    state[pl.ds(4 * (1 - c), 4)] = sf_r[...]

    def finish(h, carry):
        outer = jnp.dot(q_s[:, head_cols(h)], state[h], preferred_element_type=F32)
        kept = inner[:, head_cols(h)] + outer * jnp.exp(ccol[h])
        scale = lax.rsqrt(jnp.mean(kept * kept, axis=-1, keepdims=True) + 1e-05)
        mixed[:, head_cols(h)] = (kept * scale).astype(BF16)
        return carry

    lax.fori_loop(0, HEADS, finish, 0)
    loads[3].wait()

    def row_of(r):
        step = jnp.where(r == 1, 3, jnp.where(r == 2, 1, jnp.where(r == 3, 2, 0)))
        return mod(y + step, NY)

    def chunk_rows(j):
        return row_of(lax.div(j, 2)) * 16 + lax.rem(j, 2) * 8

    def direction(d):
        return (right, -1) if d == 0 else (left, 1)

    def forward(j, step, d, value):
        rs_s[d, j, step] = value.astype(BF16)
        send(
            rs_s.at[d, j, step], rs_r.at[d, j, step],
            rs_ss.at[d, j, step], rs_rs.at[d, j, step], direction(d)[0],
        ).start()

    def w_ready(r):
        for i in range(NZ):
            s = at(row_of(r), near(i), 1 - c)
            arrive(gw.at[s], w_p.at[r, i])

    def reduce(t, carry):
        @pl.when(t == 0)
        def _():
            w_ready(0)

        @pl.when(t < CH)
        def _():
            weight = gw[pl.ds(chunk_rows(t), 8)].reshape(CW, HEADS * HD)
            product = lax.dot_general(mixed[...], weight, NT_DIMS, preferred_element_type=F32)
            part[t] = product.reshape(NX, PAGE, CW)
            for d in range(2):
                block = mod(x + direction(d)[1], NX)
                forward(t, 0, d, part[t, block, :, d * DW : d * DW + DW])

        for step in (1, 2):

            @pl.when(jnp.logical_and(t >= step, t < CH + step))
            def _():
                j = t - step
                for d in range(2):
                    arrive(rs_r.at[d, j, step - 1], rs_rs.at[d, j, step - 1])
                    block = lax.rem(x + direction(d)[1] * (1 + step) + 2 * NX, NX)
                    own = part[j, block, :, d * DW : d * DW + DW]
                    forward(j, step, d, rs_r[d, j, step - 1].astype(F32) + own)

        @pl.when(t >= 3)
        def _():
            j = t - 3
            for d in range(2):
                arrive(rs_r.at[d, j, 2], rs_rs.at[d, j, 2])
                own = part[j, x, :, d * DW : d * DW + DW]
                cols = pl.ds(pl.multiple_of(chunk_rows(j) * 64 + d * DW, DW), DW)
                hid[:, cols] = rs_r[d, j, 2].astype(F32) + own + res_s[:, cols].astype(F32)

        @pl.when(t == 0)
        def _():
            k_across()
            for i in (2, 3, 4):
                w_across(i)

        @pl.when(t == 1)
        def _():
            k_last()
            for i in (5, 6, 7):
                w_across(i)
            w_ready(1)

        @pl.when(jnp.logical_and(t >= 2, t < 4))
        def _():
            for i in range(4):
                w_last(4 * (t - 2) + i)

        @pl.when(t == 3)
        def _():
            w_ready(2)

        @pl.when(t == 5)
        def _():
            w_ready(3)

        @pl.when(jnp.logical_and(t >= 2, t < 9))
        def _():
            k_ring(t - 1)

        return carry

    lax.fori_loop(0, CH + 3, reduce, 0)

    def square(j, total):
        cols = pl.ds(pl.multiple_of(j * CW, CW), CW)
        value = hid[:, cols]
        return total + jnp.sum(value * value, axis=-1, keepdims=True)

    squares = lax.fori_loop(0, CH, square, jnp.zeros((PAGE, 1), F32))
    scale = lax.rsqrt(squares * (1.0 / D) + 1e-05)

    def normalize(j, carry):
        cols = pl.ds(pl.multiple_of(j * CW, CW), CW)
        norm[:, cols] = (hid[:, cols] * scale * gain[:, cols]).astype(BF16)
        return carry

    lax.fori_loop(0, CH, normalize, 0)

    def k_ready(i, carry):
        for r in range(NY):
            s = at(row_of(r), near(i), 1 - c)
            arrive(gk.at[s], k_p.at[r, i])
        return carry

    lax.fori_loop(0, NZ, k_ready, 0)
    x_left = mod(x - 1, NX)
    x_right = mod(x + 1, NX)
    x_far = mod(x + 2, NX)

    def tile(n):
        return pl.ds(pl.multiple_of(n * TW, TW), TW)

    def project(n, carry):
        @pl.when(n < NT)
        def _():
            weight = gk[:, :, tile(n)].reshape(D, TW)
            value = jnp.dot(norm[...], weight, preferred_element_type=F32)
            pg[x, :, tile(n)] = value.astype(BF16)
            own = pg.at[x, :, tile(n)]
            send(own, own, g_s.at[0, n], g_r.at[0, n], right).start()
            send(own, own, g_s.at[1, n], g_r.at[1, n], left).start()

        @pl.when(n >= 2)
        def _():
            j = n - 2
            arrive(pg.at[x_left, :, tile(j)], g_r.at[0, j])
            arrive(pg.at[x_right, :, tile(j)], g_r.at[1, j])
            early = j < 2
            source = jnp.where(early, x_left, x_right)
            target = (me, jnp.where(early, right[1], left[1]))
            page = pg.at[source, :, tile(j)]
            send(page, page, g_f.at[j], g_r.at[2, j], target).start()

        return carry

    lax.fori_loop(0, NT + 2, project, 0)

    def drain_w(i, carry):
        for d in range(2):
            sent(gw.at[0], w_ys.at[d, i])
        sent(gw.at[0], w_fs.at[i])
        for r in range(NY):
            sent(gw.at[0], w_ps.at[r, i])
            sent(gk.at[0], k_ps.at[r, i])
        return carry

    lax.fori_loop(0, NZ, drain_w, 0)
    for d, count in ((0, 4), (1, 3)):
        for n in range(count):
            sent(gw.at[0], w_zs.at[d, n])
            for r in range(NY):
                sent(gk.at[0], k_zs.at[d, r, n])
    for d in range(2):
        sent(gk.at[0], k_ys.at[d])
        sent(gk.at[0, pl.ds(0, 32)], k_fs.at[d])
    sent(ub_s, s1_s.at[0])
    sent(a_s, s1_s.at[1])
    sent(sf_s, s5_s.at[0])
    for m in range(1, NZ):
        sent(st_s.at[0], s2_s.at[m])
        sent(se_s.at[0], s4_s.at[m])
    for m in range(1, NY):
        sent(sr_s, s3_s.at[m])

    def drain_rs(j, carry):
        for d in range(2):
            for step in range(3):
                sent(rs_s.at[0, 0, 0], rs_ss.at[d, j, step])
        return carry

    lax.fori_loop(0, CH, drain_rs, 0)
    tb[x] = tbl[...]
    for m in range(1, NX):
        arrive(tb.at[mod(x - m, NX)], t_r.at[m - 1])
        sent(tbl, t_s.at[m - 1])
    tables[...] = tb[...]
    for n in range(NT):
        sent(pg.at[0, :, pl.ds(0, TW)], g_s.at[0, n])
        sent(pg.at[0, :, pl.ds(0, TW)], g_s.at[1, n])
        sent(pg.at[0, :, pl.ds(0, TW)], g_f.at[n])
    for n in range(NT):
        arrive(pg.at[x_far, :, tile(n)], g_r.at[2, n])
    pages[...] = pg[...]


def on_device(query_rows, key_rows, value_rows, log_decay, residual, out_weight, norm_gain, kv_weight, block_table):
    vm, dma = pltpu.VMEM, pltpu.SemaphoreType.DMA
    table = jnp.broadcast_to(block_table.reshape(2, 1, 1), (2, 8, HD))
    hbm = pl.BlockSpec(memory_space=pl.ANY)
    vmem = pl.BlockSpec(memory_space=pltpu.VMEM)
    pages, tables = pl.pallas_call(
        kernel,
        out_shape=(
            jax.ShapeDtypeStruct((NX, PAGE, KVW), BF16),
            jax.ShapeDtypeStruct((NX, 2, 8, HD), jnp.int32),
        ),
        in_specs=[hbm, hbm, hbm, hbm, hbm, vmem, hbm, vmem, vmem],
        out_specs=(vmem, vmem),
        scratch_shapes=[
            vm((64, 64, HEADS * HD), BF16),
            vm((64, 64, KVW), BF16),
            vm((BLK, HEADS * HD), BF16),
            vm((BLK, HEADS * HD), BF16),
            vm((BLK, HEADS * HD), BF16),
            vm((PAGE, D), BF16),
            vm((HEADS, 1, BLK), F32),
            vm((HEADS, BLK, HD), F32),
            vm((HEADS, 8, HD), F32),
            vm((HEADS, 8, HD), F32),
            vm((HEADS, HD, HD), F32),
            vm((BLK, HEADS * HD), F32),
            vm((BLK, HEADS * HD), BF16),
            vm((4, HD, HD), BF16),
            vm((4, HD, HD), BF16),
            vm((NZ, 80, HD), BF16),
            vm((NZ, 80, HD), BF16),
            vm((72, HD), F32),
            vm((NY, 72, HD), F32),
            vm((NZ, 64, HD), BF16),
            vm((NZ, 64, HD), BF16),
            vm((4, HD, HD), BF16),
            vm((4, HD, HD), BF16),
            vm((HEADS, HD, HD), BF16),
            vm((CH, NX, PAGE, CW), F32),
            vm((2, CH, 3, PAGE, DW), BF16),
            vm((2, CH, 3, PAGE, DW), BF16),
            vm((PAGE, D), F32),
            vm((PAGE, D), BF16),
            vm((NX, PAGE, KVW), BF16),
            vm((NX, 2, 8, HD), jnp.int32),
            dma((6,)),
            dma((2, 4)), dma((2, NZ)), dma((NZ,)), dma((NY, NZ)), dma((NY, NZ)), dma((NY, NZ)),
            dma((2, NY, 4)), dma((2,)), dma((2,)), dma((NY, NZ)), dma((NY, NZ)), dma((2,)), dma((NY, NZ)),
            dma((2,)), dma((2,)), dma((NZ,)), dma((NZ,)), dma((NY,)), dma((NY,)),
            dma((NZ,)), dma((NZ,)), dma((1,)), dma((1,)),
            dma((2, CH, 3)), dma((2, CH, 3)), dma((2, NT)), dma((NT,)), dma((3, NT)), dma((3,)), dma((3,)),
        ],
        compiler_params=pltpu.CompilerParams(
            collective_id=0, has_side_effects=True, vmem_limit_bytes=63 * 1024 * 1024
        ),
        name="layer",
    )(
        out_weight.T, kv_weight, query_rows, key_rows, value_rows, log_decay,
        residual, norm_gain.reshape(1, D), table,
    )
    mine = tables[:, 0, 0, 0] == lax.axis_index("pool")
    slot = tables[:, 1, 0, 0]
    slots = []
    for s in range(2):
        total = jnp.zeros((PAGE, KVW), BF16)
        for p in range(NX):
            total = jnp.where(jnp.logical_and(mine[p], slot[p] == s), pages[p], total)
        slots.append(total)
    return jnp.stack(slots).reshape(1, 1, 2, PAGE, KVW)


def solution(mesh):
    placed = (
        P("seq", "pool"),
        P("seq", "pool"),
        P("seq", "pool"),
        P("pool", "seq"),
        P(("seq", "pool"), None),
        P("pool", "seq"),
        P(),
        P("seq", None),
        P(("seq", "pool"), None),
    )
    return jax.shard_map(
        on_device,
        mesh=mesh,
        in_specs=placed,
        out_specs=P("seq", "pool", None, None, None),
        check_vma=False,
    )
```

```python
import jax
import jax.numpy as jnp
from jax import lax
from jax.experimental import pallas as pl
from jax.experimental.pallas import tpu as pltpu
from jax.sharding import PartitionSpec as P

NY, NZ, NX = 4, 8, 4
HEADS = 8
HD = 128
BLK = 512
PAGE = 128
D = 4096
KVW = 1024
CH = 8
CW = D // CH
DW = CW // 2
NT = 4
TW = KVW // NT
F32 = jnp.float32
BF16 = jnp.bfloat16
MESH = pl.DeviceIdType.MESH
NT_DIMS = (((1,), (1,)), ((), ()))
TN_DIMS = (((0,), (0,)), ((), ()))
HIGH = lax.Precision.HIGHEST


def kernel(
    wt, kw, q_hbm, k_hbm, v_hbm, ld, res_hbm, gain, tbl,
    cache,
    gw, gk, q_s, k_s, v_s, res_s, crow, ccol, a_s, a_r, u_s, inner, mixed,
    ub_s, ub_r, st_s, st_r, sr_s, sr_r, se_s, se_r, sf_s, sf_r, state,
    part, rs_s, rs_r, hid, norm, pg, tb, tb_s,
    ld_sem, w_zs, w_ys, w_fs, w_ps, w_r, w_p,
    k_zs, k_ys, k_fs, k_ps, k_r, k_h, k_p,
    s1_s, s1_r, s2_s, s2_r, s3_s, s3_r, s4_s, s4_r, s5_s, s5_r,
    rs_ss, rs_rs, g_s, g_f, g_r, t_s, t_r,
):
    me = lax.axis_index("seq")
    x = lax.axis_index("pool")
    y = lax.div(me, 16)
    z = lax.rem(lax.div(me, 2), 8)
    c = lax.rem(me, 2)

    def at(yy, zz, cc):
        return (yy * NZ + zz) * 2 + cc

    def mod(value, size):
        return lax.rem(value + size, size)

    up = (at(mod(y + 1, NY), z, c), x)
    down = (at(mod(y - 1, NY), z, c), x)
    ahead = (at(y, mod(z + 1, NZ), c), x)
    behind = (at(y, mod(z - 1, NZ), c), x)
    partner = (at(y, z, 1 - c), x)
    right = (me, mod(x + 1, NX))
    left = (me, mod(x - 1, NX))

    def send(src, dst, ssem, rsem, device):
        copy = pltpu.make_async_remote_copy(
            src_ref=src, dst_ref=dst, send_sem=ssem, recv_sem=rsem,
            device_id=device, device_id_type=MESH,
        )
        return copy

    def arrive(ref, rsem):
        send(ref, ref, rsem, rsem, partner).wait_recv()

    def sent(ref, ssem):
        send(ref, ref, ssem, ssem, partner).wait_send()

    peers = [partner]
    peers += [(at(y, mod(z + m, NZ), c), x) for m in range(1, NZ)]
    peers += [(at(mod(y + m, NY), z, c), x) for m in range(1, NY)]
    peers += [(me, mod(x + m, NX)) for m in range(1, NX)]
    barrier = pltpu.get_barrier_semaphore()
    for peer in peers:
        pl.semaphore_signal(barrier, inc=1, device_id=peer, device_id_type=MESH)
    loads = [
        pltpu.make_async_copy(k_hbm, k_s, ld_sem.at[0]),
        pltpu.make_async_copy(v_hbm, v_s, ld_sem.at[1]),
        pltpu.make_async_copy(q_hbm, q_s, ld_sem.at[2]),
        pltpu.make_async_copy(res_hbm, res_s, ld_sem.at[3]),
        pltpu.make_async_copy(wt, gw.at[me], ld_sem.at[4]),
        pltpu.make_async_copy(kw, gk.at[me], ld_sem.at[5]),
    ]
    for load in loads:
        load.start()
    pl.semaphore_wait(barrier, len(peers))

    def near(i):
        half = lax.div(i + 1, 2)
        return mod(z + half * (1 - 2 * lax.rem(i, 2)), NZ)

    row_step = (0, 3, 1, 2)

    def slot(r, i):
        return at(mod(y + row_step[r], NY), near(i), c)

    def w_rows(src, s, i):
        send(src, gw.at[s], w_ys.at[0, i], w_r.at[1, i], up).start()
        send(src, gw.at[s], w_ys.at[1, i], w_r.at[2, i], down).start()

    def w_pass(src, s, r, i):
        send(src, gw.at[s], w_ps.at[r, i], w_p.at[r, i], partner).start()

    def w_start():
        send(wt, gw.at[me], w_zs.at[0, 0], w_r.at[0, 1], ahead).start()
        send(wt, gw.at[me], w_zs.at[1, 0], w_r.at[0, 2], behind).start()
        w_rows(wt, me, 0)
        w_pass(wt, me, 0, 0)

    def w_along(i):
        s = slot(0, i)
        odd = lax.rem(i, 2)
        arrive(gw.at[s], w_r.at[0, i])

        @pl.when(i <= 5)
        def _():
            target = (at(y, mod(z + 2 * odd - 1, NZ), c), x)
            send(
                gw.at[s], gw.at[s], w_zs.at[1 - odd, lax.div(i + 1, 2)],
                w_r.at[0, i + 2], target,
            ).start()

        w_rows(gw.at[s], s, i)
        w_pass(gw.at[s], s, 0, i)

    def w_across(i):
        below, above = slot(1, i), slot(2, i)
        even = lax.rem(i, 2) == 0
        arrive(gw.at[below], w_r.at[1, i])
        arrive(gw.at[above], w_r.at[2, i])
        s = jnp.where(even, below, above)
        target = (jnp.where(even, up[0], down[0]), x)
        send(gw.at[s], gw.at[s], w_fs.at[i], w_r.at[3, i], target).start()
        w_pass(gw.at[below], below, 1, i)
        w_pass(gw.at[above], above, 2, i)

    def w_last(i):
        s = slot(3, i)
        arrive(gw.at[s], w_r.at[3, i])
        w_pass(gw.at[s], s, 3, i)

    def k_along(src, s, r):
        send(src, gk.at[s], k_zs.at[0, r, 0], k_r.at[r, 1], ahead).start()
        send(src, gk.at[s], k_zs.at[1, r, 0], k_r.at[r, 2], behind).start()
        send(src, gk.at[s], k_ps.at[r, 0], k_p.at[r, 0], partner).start()

    def k_start():
        send(kw, gk.at[me], k_ys.at[0], k_r.at[1, 0], up).start()
        send(kw, gk.at[me], k_ys.at[1], k_r.at[2, 0], down).start()
        k_along(kw, me, 0)

    def k_across():
        below, above = slot(1, 0), slot(2, 0)
        arrive(gk.at[below], k_r.at[1, 0])
        arrive(gk.at[above], k_r.at[2, 0])
        low = gk.at[below, pl.ds(0, 32)]
        top = gk.at[above, pl.ds(32, 32)]
        send(low, low, k_fs.at[0], k_h.at[0], up).start()
        send(top, top, k_fs.at[1], k_h.at[1], down).start()
        k_along(gk.at[below], below, 1)
        k_along(gk.at[above], above, 2)

    def k_last():
        s = slot(3, 0)
        arrive(gk.at[s, pl.ds(0, 32)], k_h.at[0])
        arrive(gk.at[s, pl.ds(32, 32)], k_h.at[1])
        k_along(gk.at[s], s, 3)

    def k_ring(i):
        odd = lax.rem(i, 2)
        for r in range(NY):
            s = slot(r, i)
            arrive(gk.at[s], k_r.at[r, i])

            @pl.when(i <= 5)
            def _():
                target = (at(y, mod(z + 2 * odd - 1, NZ), c), x)
                send(
                    gk.at[s], gk.at[s], k_zs.at[1 - odd, r, lax.div(i + 1, 2)],
                    k_r.at[r, i + 2], target,
                ).start()

            send(gk.at[s], gk.at[s], k_ps.at[r, i], k_p.at[r, i], partner).start()

    w_start()
    for n in range(2):
        tb_s[n] = jnp.broadcast_to(tbl[0:1, n : n + 1], (8, HD))
    for m in range(1, NX):
        target = (me, mod(x + m, NX))
        send(tb_s, tb.at[x], t_s.at[m - 1], t_r.at[m - 1], target).start()

    steps_a = lax.broadcasted_iota(jnp.int32, (BLK, BLK), 0)
    steps_b = lax.broadcasted_iota(jnp.int32, (BLK, BLK), 1)
    lower = jnp.where(steps_b <= steps_a, 1.0, 0.0).astype(F32)
    decay = ld[...]
    sums_row = lax.dot_general(decay, lower, NT_DIMS, precision=HIGH, preferred_element_type=F32)
    sums_col = lax.dot_general(lower, decay, NT_DIMS, precision=HIGH, preferred_element_type=F32)
    for h in range(HEADS):
        crow[h] = sums_row[h : h + 1, :]
        wide = jnp.broadcast_to(sums_col[:, h : h + 1], (BLK, HD))
        ccol[h] = wide
        a_s[h] = jnp.broadcast_to(wide[BLK - 1 : BLK, :], (8, HD))

    def head_cols(h):
        return pl.ds(pl.multiple_of(h * HD, HD), HD)

    loads[0].wait()
    loads[1].wait()

    def update(h, carry):
        cb = ccol[h]
        gap = jnp.exp(cb[BLK - 1 : BLK, :] - cb)
        weighted = (k_s[:, head_cols(h)].astype(F32) * gap).astype(BF16)
        u_s[h] = lax.dot_general(
            weighted, v_s[:, head_cols(h)], TN_DIMS, preferred_element_type=F32
        )
        return carry

    lax.fori_loop(0, HEADS, update, 0)
    ub_s[...] = u_s[pl.ds(4 * (1 - c), 4)].astype(BF16)
    send(ub_s, ub_r, s1_s.at[0], s1_r.at[0], partner).start()
    send(a_s, a_r, s1_s.at[1], s1_r.at[1], partner).start()

    def chip_parts():
        own = u_s[pl.ds(4 * c, 4)]
        other = ub_r[...].astype(F32)
        a_own = a_s[pl.ds(4 * c, 4)]
        a_other = a_r[pl.ds(4 * c, 4)]
        first = c == 0
        return (
            jnp.where(first, own, other),
            jnp.where(first, other, own),
            jnp.where(first, a_own, a_other),
            jnp.where(first, a_other, a_own),
        )

    def scan_chip():
        arrive(ub_r, s1_r.at[0])
        arrive(a_r, s1_r.at[1])
        u0, u1, a0, a1 = chip_parts()
        total = jnp.exp(a1)[:, 0:1, :] * u0 + u1
        a_chip = a0 + a1
        rows = lax.broadcasted_iota(jnp.int32, (16, HD), 0)
        for hl in range(4):
            a = jnp.broadcast_to(a_chip[hl, 0:1, :], (16, HD))
            hi = a.astype(BF16).astype(F32)
            mid = (a - hi).astype(BF16).astype(F32)
            low = a - hi - mid
            tile = jnp.where(rows == 0, hi, jnp.where(rows == 1, mid, jnp.where(rows == 2, low, 0.0)))
            for half in range(2):
                st_s[2 * hl + half, 0:64, :] = total[hl, 64 * half : 64 * half + 64, :].astype(BF16)
                st_s[2 * hl + half, 64:80, :] = tile.astype(BF16)
        st_r[z] = st_s[z]
        for m in range(1, NZ):
            zz = mod(z + m, NZ)
            send(st_s.at[zz], st_r.at[z], s2_s.at[m], s2_r.at[m], (at(y, zz, c), x)).start()

    def chip_total(zz):
        message = st_r[zz].astype(F32)
        return message[0:64, :], jnp.sum(message[64:80, :], axis=0, keepdims=True)

    def scan_row():
        for m in range(1, NZ):
            arrive(st_r.at[mod(z - m, NZ)], s2_r.at[m])
        total = jnp.zeros((64, HD), F32)
        a_row = jnp.zeros((1, HD), F32)
        for zz in range(NZ):
            t, a = chip_total(zz)
            total = jnp.exp(a) * total + t
            a_row = a_row + a
        sr_s[0:64, :] = total
        sr_s[64:72, :] = jnp.broadcast_to(a_row, (8, HD))
        sr_r[y] = sr_s[...]
        for m in range(1, NY):
            target = (at(mod(y + m, NY), z, c), x)
            send(sr_s, sr_r.at[y], s3_s.at[m], s3_r.at[m], target).start()

    def scan_back():
        for m in range(1, NY):
            arrive(sr_r.at[mod(y - m, NY)], s3_r.at[m])
        enter = jnp.zeros((64, HD), F32)
        for yy in range(NY):
            moved = jnp.exp(sr_r[yy, 64:65, :]) * enter + sr_r[yy, 0:64, :]
            enter = jnp.where(yy < y, moved, enter)
        for zz in range(NZ):
            se_s[zz] = enter.astype(BF16)
            t, a = chip_total(zz)
            enter = jnp.exp(a) * enter + t
        se_r[z] = se_s[z]
        for m in range(1, NZ):
            zz = mod(z + m, NZ)
            send(se_s.at[zz], se_r.at[z], s4_s.at[m], s4_r.at[m], (at(y, zz, c), x)).start()

    def scan_cores():
        for m in range(1, NZ):
            arrive(se_r.at[mod(z - m, NZ)], s4_r.at[m])
        enter = se_r[...].reshape(4, HD, HD).astype(F32)
        u0, _, a0, _ = chip_parts()
        after = jnp.exp(a0)[:, 0:1, :] * enter + u0
        first = c == 0
        sf_s[...] = jnp.where(first, after, enter).astype(BF16)
        send(sf_s, sf_r, s5_s.at[0], s5_r.at[0], partner).start()
        state[pl.ds(4 * c, 4)] = jnp.where(first, enter, after).astype(BF16)

    loads[2].wait()
    loads[4].wait()
    loads[5].wait()

    tri_a = lax.broadcasted_iota(jnp.int32, (HD, HD), 0)
    tri_b = lax.broadcasted_iota(jnp.int32, (HD, HD), 1)
    seen = tri_b <= tri_a

    def within(h, carry):
        @pl.when(h == 1)
        def _():
            scan_chip()

        @pl.when(h == 4)
        def _():
            scan_row()

        @pl.when(h == 5)
        def _():
            k_start()

        @pl.when(h == 6)
        def _():
            scan_back()

        for tq in range(4):
            rows = pl.ds(tq * HD, HD)
            width = HD * (tq + 1)
            products = lax.dot_general(
                q_s[rows, head_cols(h)], k_s[0:width, head_cols(h)], NT_DIMS,
                preferred_element_type=F32,
            )
            c_here = ccol[h, rows, :]
            blocks = []
            for ts in range(tq + 1):
                gap = c_here - crow[h, :, ts * HD : ts * HD + HD]
                piece = products[:, ts * HD : ts * HD + HD]
                if ts == tq:
                    gap = jnp.where(seen, gap, 0.0)
                    piece = jnp.where(seen, piece, 0.0)
                blocks.append((piece * jnp.exp(gap)).astype(BF16))
            scores = jnp.concatenate(blocks, axis=1) if tq else blocks[0]
            inner[rows, head_cols(h)] = jnp.dot(
                scores, v_s[0:width, head_cols(h)], preferred_element_type=F32
            )

        @pl.when(h >= 1)
        def _():
            w_along(h)

        return carry

    lax.fori_loop(0, HEADS, within, 0)
    scan_cores()
    w_across(0)
    w_across(1)
    arrive(sf_r, s5_r.at[0])
    state[pl.ds(4 * (1 - c), 4)] = sf_r[...]

    def finish(h, carry):
        outer = jnp.dot(q_s[:, head_cols(h)], state[h], preferred_element_type=F32)
        kept = inner[:, head_cols(h)] + outer * jnp.exp(ccol[h])
        scale = lax.rsqrt(jnp.mean(kept * kept, axis=-1, keepdims=True) + 1e-05)
        mixed[:, head_cols(h)] = (kept * scale).astype(BF16)
        return carry

    lax.fori_loop(0, HEADS, finish, 0)
    loads[3].wait()

    def row_of(r):
        step = jnp.where(r == 1, 3, jnp.where(r == 2, 1, jnp.where(r == 3, 2, 0)))
        return mod(y + step, NY)

    def chunk_rows(j):
        return row_of(lax.div(j, 2)) * 16 + lax.rem(j, 2) * 8

    def direction(d):
        return (right, -1) if d == 0 else (left, 1)

    def forward(j, step, d, value):
        rs_s[d, j, step] = value.astype(BF16)
        send(
            rs_s.at[d, j, step], rs_r.at[d, j, step],
            rs_ss.at[d, j, step], rs_rs.at[d, j, step], direction(d)[0],
        ).start()

    def w_ready(r):
        for i in range(NZ):
            s = at(row_of(r), near(i), 1 - c)
            arrive(gw.at[s], w_p.at[r, i])

    def reduce(t, carry):
        @pl.when(t == 0)
        def _():
            w_ready(0)

        @pl.when(t < CH)
        def _():
            weight = gw[pl.ds(chunk_rows(t), 8)].reshape(CW, HEADS * HD)
            product = lax.dot_general(mixed[...], weight, NT_DIMS, preferred_element_type=F32)
            part[t] = product.reshape(NX, PAGE, CW)
            for d in range(2):
                block = mod(x + direction(d)[1], NX)
                forward(t, 0, d, part[t, block, :, d * DW : d * DW + DW])

        for step in (1, 2):

            @pl.when(jnp.logical_and(t >= step, t < CH + step))
            def _():
                j = t - step
                for d in range(2):
                    arrive(rs_r.at[d, j, step - 1], rs_rs.at[d, j, step - 1])
                    block = lax.rem(x + direction(d)[1] * (1 + step) + 2 * NX, NX)
                    own = part[j, block, :, d * DW : d * DW + DW]
                    forward(j, step, d, rs_r[d, j, step - 1].astype(F32) + own)

        @pl.when(t >= 3)
        def _():
            j = t - 3
            for d in range(2):
                arrive(rs_r.at[d, j, 2], rs_rs.at[d, j, 2])
                own = part[j, x, :, d * DW : d * DW + DW]
                cols = pl.ds(pl.multiple_of(chunk_rows(j) * 64 + d * DW, DW), DW)
                hid[:, cols] = rs_r[d, j, 2].astype(F32) + own + res_s[:, cols].astype(F32)

        @pl.when(t == 0)
        def _():
            k_across()
            for i in (2, 3, 4):
                w_across(i)

        @pl.when(t == 1)
        def _():
            k_last()
            for i in (5, 6, 7):
                w_across(i)
            w_ready(1)

        @pl.when(jnp.logical_and(t >= 2, t < 4))
        def _():
            for i in range(4):
                w_last(4 * (t - 2) + i)

        @pl.when(t == 3)
        def _():
            w_ready(2)

        @pl.when(t == 5)
        def _():
            w_ready(3)

        @pl.when(jnp.logical_and(t >= 2, t < 9))
        def _():
            k_ring(t - 1)

        return carry

    lax.fori_loop(0, CH + 3, reduce, 0)

    def square(j, total):
        cols = pl.ds(pl.multiple_of(j * CW, CW), CW)
        value = hid[:, cols]
        return total + jnp.sum(value * value, axis=-1, keepdims=True)

    squares = lax.fori_loop(0, CH, square, jnp.zeros((PAGE, 1), F32))
    scale = lax.rsqrt(squares * (1.0 / D) + 1e-05)

    def normalize(j, carry):
        cols = pl.ds(pl.multiple_of(j * CW, CW), CW)
        norm[:, cols] = (hid[:, cols] * scale * gain[:, cols]).astype(BF16)
        return carry

    lax.fori_loop(0, CH, normalize, 0)

    def k_ready(i, carry):
        for r in range(NY):
            s = at(row_of(r), near(i), 1 - c)
            arrive(gk.at[s], k_p.at[r, i])
        return carry

    lax.fori_loop(0, NZ, k_ready, 0)
    x_left = mod(x - 1, NX)
    x_right = mod(x + 1, NX)
    x_far = mod(x + 2, NX)

    def tile(n):
        return pl.ds(pl.multiple_of(n * TW, TW), TW)

    def project(n, carry):
        @pl.when(n < NT)
        def _():
            weight = gk[:, :, tile(n)].reshape(D, TW)
            value = jnp.dot(norm[...], weight, preferred_element_type=F32)
            pg[x, :, tile(n)] = value.astype(BF16)
            own = pg.at[x, :, tile(n)]
            send(own, own, g_s.at[0, n], g_r.at[0, n], right).start()
            send(own, own, g_s.at[1, n], g_r.at[1, n], left).start()

        @pl.when(n >= 2)
        def _():
            j = n - 2
            arrive(pg.at[x_left, :, tile(j)], g_r.at[0, j])
            arrive(pg.at[x_right, :, tile(j)], g_r.at[1, j])
            early = j < 2
            source = jnp.where(early, x_left, x_right)
            target = (me, jnp.where(early, right[1], left[1]))
            page = pg.at[source, :, tile(j)]
            send(page, page, g_f.at[j], g_r.at[2, j], target).start()

        return carry

    lax.fori_loop(0, NT + 2, project, 0)

    def drain_w(i, carry):
        for d in range(2):
            sent(gw.at[0], w_ys.at[d, i])
        sent(gw.at[0], w_fs.at[i])
        for r in range(NY):
            sent(gw.at[0], w_ps.at[r, i])
            sent(gk.at[0], k_ps.at[r, i])
        return carry

    lax.fori_loop(0, NZ, drain_w, 0)
    for d, count in ((0, 4), (1, 3)):
        for n in range(count):
            sent(gw.at[0], w_zs.at[d, n])
            for r in range(NY):
                sent(gk.at[0], k_zs.at[d, r, n])
    for d in range(2):
        sent(gk.at[0], k_ys.at[d])
        sent(gk.at[0, pl.ds(0, 32)], k_fs.at[d])
    sent(ub_s, s1_s.at[0])
    sent(a_s, s1_s.at[1])
    sent(sf_s, s5_s.at[0])
    for m in range(1, NZ):
        sent(st_s.at[0], s2_s.at[m])
        sent(se_s.at[0], s4_s.at[m])
    for m in range(1, NY):
        sent(sr_s, s3_s.at[m])

    def drain_rs(j, carry):
        for d in range(2):
            for step in range(3):
                sent(rs_s.at[0, 0, 0], rs_ss.at[d, j, step])
        return carry

    lax.fori_loop(0, CH, drain_rs, 0)
    tb[x] = tb_s[...]
    for m in range(1, NX):
        arrive(tb.at[mod(x - m, NX)], t_r.at[m - 1])
        sent(tb_s, t_s.at[m - 1])
    for n in range(NT):
        sent(pg.at[0, :, pl.ds(0, TW)], g_s.at[0, n])
        sent(pg.at[0, :, pl.ds(0, TW)], g_s.at[1, n])
        sent(pg.at[0, :, pl.ds(0, TW)], g_f.at[n])
    for n in range(NT):
        arrive(pg.at[x_far, :, tile(n)], g_r.at[2, n])
    here = [tb[p, 0] == x for p in range(NX)]
    for s in range(2):
        total = jnp.zeros((PAGE, KVW), BF16)
        for p in range(NX):
            hit = jnp.logical_and(here[p], tb[p, 1] == s).astype(F32)
            hit = jnp.broadcast_to(hit[0:1, 0:1], (PAGE, KVW))
            total = jnp.where(hit > 0.5, pg[p], total)
        cache[s] = total


def on_device(query_rows, key_rows, value_rows, log_decay, residual, out_weight, norm_gain, kv_weight, block_table):
    vm, dma = pltpu.VMEM, pltpu.SemaphoreType.DMA
    hbm = pl.BlockSpec(memory_space=pl.ANY)
    vmem = pl.BlockSpec(memory_space=pltpu.VMEM)
    cache = pl.pallas_call(
        kernel,
        out_shape=jax.ShapeDtypeStruct((2, PAGE, KVW), BF16),
        in_specs=[hbm, hbm, hbm, hbm, hbm, vmem, hbm, vmem, vmem],
        out_specs=vmem,
        scratch_shapes=[
            vm((64, 64, HEADS * HD), BF16),
            vm((64, 64, KVW), BF16),
            vm((BLK, HEADS * HD), BF16),
            vm((BLK, HEADS * HD), BF16),
            vm((BLK, HEADS * HD), BF16),
            vm((PAGE, D), BF16),
            vm((HEADS, 1, BLK), F32),
            vm((HEADS, BLK, HD), F32),
            vm((HEADS, 8, HD), F32),
            vm((HEADS, 8, HD), F32),
            vm((HEADS, HD, HD), F32),
            vm((BLK, HEADS * HD), F32),
            vm((BLK, HEADS * HD), BF16),
            vm((4, HD, HD), BF16),
            vm((4, HD, HD), BF16),
            vm((NZ, 80, HD), BF16),
            vm((NZ, 80, HD), BF16),
            vm((72, HD), F32),
            vm((NY, 72, HD), F32),
            vm((NZ, 64, HD), BF16),
            vm((NZ, 64, HD), BF16),
            vm((4, HD, HD), BF16),
            vm((4, HD, HD), BF16),
            vm((HEADS, HD, HD), BF16),
            vm((CH, NX, PAGE, CW), F32),
            vm((2, CH, 3, PAGE, DW), BF16),
            vm((2, CH, 3, PAGE, DW), BF16),
            vm((PAGE, D), F32),
            vm((PAGE, D), BF16),
            vm((NX, PAGE, KVW), BF16),
            vm((NX, 2, 8, HD), jnp.int32),
            vm((2, 8, HD), jnp.int32),
            dma((6,)),
            dma((2, 4)), dma((2, NZ)), dma((NZ,)), dma((NY, NZ)), dma((NY, NZ)), dma((NY, NZ)),
            dma((2, NY, 4)), dma((2,)), dma((2,)), dma((NY, NZ)), dma((NY, NZ)), dma((2,)), dma((NY, NZ)),
            dma((2,)), dma((2,)), dma((NZ,)), dma((NZ,)), dma((NY,)), dma((NY,)),
            dma((NZ,)), dma((NZ,)), dma((1,)), dma((1,)),
            dma((2, CH, 3)), dma((2, CH, 3)), dma((2, NT)), dma((NT,)), dma((3, NT)), dma((3,)), dma((3,)),
        ],
        compiler_params=pltpu.CompilerParams(
            collective_id=0, has_side_effects=True, vmem_limit_bytes=63 * 1024 * 1024
        ),
        name="layer",
    )(
        out_weight.T, kv_weight, query_rows, key_rows, value_rows, log_decay,
        residual, norm_gain.reshape(1, D), block_table,
    )
    return cache.reshape(1, 1, 2, PAGE, KVW)


def solution(mesh):
    placed = (
        P("seq", "pool"),
        P("seq", "pool"),
        P("seq", "pool"),
        P("pool", "seq"),
        P(("seq", "pool"), None),
        P("pool", "seq"),
        P(),
        P("seq", None),
        P(("seq", "pool"), None),
    )
    return jax.shard_map(
        on_device,
        mesh=mesh,
        in_specs=placed,
        out_specs=P("seq", "pool", None, None, None),
        check_vma=False,
    )
```

```python
import jax
import jax.numpy as jnp
from jax import lax
from jax.experimental import pallas as pl
from jax.experimental.pallas import tpu as pltpu
from jax.sharding import PartitionSpec as P

NY, NZ, NX = 4, 8, 4
HEADS = 8
HD = 128
BLK = 512
PAGE = 128
D = 4096
KVW = 1024
CH = 8
CW = D // CH
DW = CW // 2
NT = 4
TW = KVW // NT
F32 = jnp.float32
BF16 = jnp.bfloat16
MESH = pl.DeviceIdType.MESH
NT_DIMS = (((1,), (1,)), ((), ()))
TN_DIMS = (((0,), (0,)), ((), ()))
HIGH = lax.Precision.HIGHEST

PLAN = {
    (0, 0): ((1, 0, 0, 1), (2, 0, 0, 2), (3, 0, 1, 0), (4, 0, 2, 0),),
    (1, 0): ((3, 1, 1, 0), (4, 1, 2, 0),),
    (2, 1, 1): ((0, 0, 0, 1), (0, 0, 0, 2), (0, 0, 1, 0), (0, 0, 2, 0), (3, 0, 1, 1), (4, 0, 2, 1),),
    (2, 2, 2): ((2, 0, 0, 4),),
    (2, 4, 2): ((0, 1, 1, 0), (0, 1, 2, 0), (3, 0, 1, 2), (4, 0, 2, 2), (1, 0, 0, 3),),
    (2, 5, 0): ((0, 0, 1, 1), (0, 0, 2, 1), (3, 0, 3, 0), (4, 0, 3, 1), (0, 0, 0, 4), (2, 0, 0, 6),),
    (2, 5, 1): ((0, 0, 1, 2), (0, 0, 2, 2),),
    (2, 5, 2): ((0, 0, 0, 3), (1, 0, 0, 5), (4, 0, 2, 3),),
    (2, 6, 2): ((3, 0, 1, 3),),
    (2, 7, 2): ((0, 0, 3, 0), (0, 0, 3, 1),),
    (3, 0): ((0, 0, 0, 6), (2, 0, 0, 7), (4, 0, 2, 4), (3, 0, 1, 4),),
    (4, 0): ((0, 0, 0, 5), (0, 0, 2, 3), (4, 0, 2, 5), (0, 0, 1, 3), (3, 0, 1, 5), (2, 1, 0, 2), (0, 0, 0, 7), (1, 1, 0, 1), (0, 0, 2, 4), (4, 0, 2, 6), (0, 0, 1, 4), (3, 0, 1, 6), (2, 1, 1, 2), (1, 1, 1, 1), (0, 0, 2, 5), (4, 0, 2, 7), (0, 0, 1, 5), (3, 0, 1, 7), (0, 1, 0, 2), (2, 1, 0, 4),),
    (5, 0): ((0, 1, 0, 1), (1, 1, 0, 3),),
    (6, 0): ((0, 0, 1, 6), (0, 0, 2, 6), (0, 1, 1, 1), (0, 1, 1, 2), (3, 0, 3, 2), (4, 0, 3, 3), (1, 1, 2, 1), (2, 1, 2, 2),),
    (7, 0, 1): ((0, 0, 2, 7),),
    (7, 1, 1): ((0, 0, 1, 7), (0, 1, 0, 4), (3, 0, 3, 4), (4, 0, 3, 5), (2, 1, 0, 6),),
    (7, 2, 0): ((0, 1, 0, 3), (1, 1, 0, 5),),
    (7, 3, 1): ((0, 0, 3, 2), (0, 0, 3, 3), (0, 1, 2, 1), (0, 1, 2, 2), (3, 0, 3, 6), (4, 0, 3, 7), (1, 1, 2, 3), (2, 1, 2, 4),),
    (7, 3, 2): ((0, 0, 3, 4), (0, 0, 3, 5), (0, 1, 0, 6), (3, 2, 1, 0), (4, 2, 2, 0), (2, 1, 1, 4), (0, 1, 0, 5), (1, 1, 0, 7),),
    (7, 4, 2): ((0, 0, 3, 6), (0, 0, 3, 7), (0, 1, 2, 4), (2, 1, 2, 6), (0, 1, 2, 3), (1, 1, 2, 5),),
    (7, 4, 3): ((0, 1, 3, 0),),
    (7, 5, 1): ((0, 1, 0, 7), (0, 1, 1, 4), (1, 1, 3, 1), (2, 1, 3, 2),),
    (7, 5, 3): ((0, 1, 2, 6), (2, 1, 1, 6), (0, 1, 2, 5), (1, 1, 2, 7),),
    (7, 6, 2): ((0, 1, 3, 2), (2, 1, 3, 4), (0, 1, 3, 1), (1, 1, 3, 3),),
    (7, 7, 1): ((0, 1, 1, 6), (0, 1, 2, 7), (2, 1, 1, 7), (1, 1, 1, 3),),
    (7, 7, 3): ((0, 1, 3, 4), (2, 1, 3, 6), (0, 1, 3, 3), (1, 1, 3, 5),),
    (7, 8, 2): ((0, 1, 1, 7), (0, 1, 1, 3), (1, 1, 1, 5),),
    (7, 9, 2): ((0, 1, 3, 6), (2, 1, 3, 7), (0, 1, 3, 5),),
    (7, 10, 0): ((0, 1, 1, 5),),
    (7, 10, 3): ((0, 1, 3, 7),),
}


def kernel(
    wt, kw, q_hbm, k_hbm, v_hbm, ld, res_hbm, gain, tbl,
    cache,
    gw, gk, q_s, k_s, v_s, res_s, crow, ccol, a_s, a_r, u_s, inner, mixed,
    ub_s, ub_r, st_s, st_r, sr_s, sr_r, se_s, se_r, sf_s, sf_r, state,
    part, rs_s, rs_r, hid, norm, pg, tb, tb_s,
    ld_sem, w_zs, w_ys, w_fs, w_ps, w_r, w_p,
    k_zs, k_ys, k_fs, k_ps, k_r, k_h, k_p,
    s1_s, s1_r, s2_s, s2_r, s3_s, s3_r, s4_s, s4_r, s5_s, s5_r,
    rs_ss, rs_rs, g_s, g_f, g_r, t_s, t_r,
):
    me = lax.axis_index("seq")
    x = lax.axis_index("pool")
    y = lax.div(me, 16)
    z = lax.rem(lax.div(me, 2), 8)
    c = lax.rem(me, 2)

    def at(yy, zz, cc):
        return (yy * NZ + zz) * 2 + cc

    def mod(value, size):
        return lax.rem(value + size, size)

    up = (at(mod(y + 1, NY), z, c), x)
    down = (at(mod(y - 1, NY), z, c), x)
    ahead = (at(y, mod(z + 1, NZ), c), x)
    behind = (at(y, mod(z - 1, NZ), c), x)
    partner = (at(y, z, 1 - c), x)
    right = (me, mod(x + 1, NX))
    left = (me, mod(x - 1, NX))

    def send(src, dst, ssem, rsem, device):
        copy = pltpu.make_async_remote_copy(
            src_ref=src, dst_ref=dst, send_sem=ssem, recv_sem=rsem,
            device_id=device, device_id_type=MESH,
        )
        return copy

    def arrive(ref, rsem):
        send(ref, ref, rsem, rsem, partner).wait_recv()

    def sent(ref, ssem):
        send(ref, ref, ssem, ssem, partner).wait_send()

    peers = [partner]
    peers += [(at(y, mod(z + m, NZ), c), x) for m in range(1, NZ)]
    peers += [(at(mod(y + m, NY), z, c), x) for m in range(1, NY)]
    peers += [(me, mod(x + m, NX)) for m in range(1, NX)]
    barrier = pltpu.get_barrier_semaphore()
    for peer in peers:
        pl.semaphore_signal(barrier, inc=1, device_id=peer, device_id_type=MESH)
    loads = [
        pltpu.make_async_copy(k_hbm, k_s, ld_sem.at[0]),
        pltpu.make_async_copy(v_hbm, v_s, ld_sem.at[1]),
        pltpu.make_async_copy(q_hbm, q_s, ld_sem.at[2]),
        pltpu.make_async_copy(res_hbm, res_s, ld_sem.at[3]),
        pltpu.make_async_copy(wt, gw.at[me], ld_sem.at[4]),
        pltpu.make_async_copy(kw, gk.at[me], ld_sem.at[5]),
    ]
    for load in loads:
        load.start()
    steps_a = lax.broadcasted_iota(jnp.int32, (BLK, BLK), 0)
    steps_b = lax.broadcasted_iota(jnp.int32, (BLK, BLK), 1)
    lower = jnp.where(steps_b <= steps_a, 1.0, 0.0).astype(F32)
    decay = ld[...]
    sums_row = lax.dot_general(decay, lower, NT_DIMS, precision=HIGH, preferred_element_type=F32)
    sums_col = lax.dot_general(lower, decay, NT_DIMS, precision=HIGH, preferred_element_type=F32)
    for h in range(HEADS):
        crow[h] = sums_row[h : h + 1, :]
        wide = jnp.broadcast_to(sums_col[:, h : h + 1], (BLK, HD))
        ccol[h] = wide
        a_s[h] = jnp.broadcast_to(wide[BLK - 1 : BLK, :], (8, HD))

    pl.semaphore_wait(barrier, len(peers))

    def near(i):
        half = lax.div(i + 1, 2)
        return mod(z + half * (1 - 2 * lax.rem(i, 2)), NZ)

    row_step = (0, 3, 1, 2)

    def slot(r, i):
        return at(mod(y + row_step[r], NY), near(i), c)

    lines = (None, ahead, behind, up, down)

    def take(kind, r, i):
        if kind == 0:
            s = slot(r, i)
            arrive(gw.at[s], w_r.at[r, i])
            send(gw.at[s], gw.at[s], w_ps.at[r, i], w_p.at[r, i], partner).start()
            return
        s = slot(r, i)
        if r == 3 and i == 0:
            arrive(gk.at[s, pl.ds(0, 32)], k_h.at[0])
            arrive(gk.at[s, pl.ds(32, 32)], k_h.at[1])
        else:
            arrive(gk.at[s], k_r.at[r, i])
        send(gk.at[s], gk.at[s], k_ps.at[r, i], k_p.at[r, i], partner).start()

    def along(i, link):
        back = 0 if i <= 2 else (6 if i == 7 and link == 2 else i - 2)
        index = (i - 1) // 2 if link == 1 else (3 if i == 7 else i // 2 - 1)
        return back, index

    def pass_on(link, kind, r, i):
        target = lines[link]
        if kind == 2:
            s = slot(r, 0)
            rows = gk.at[s, pl.ds(32 * (r - 1), 32)]
            send(rows, rows, k_fs.at[r - 1], k_h.at[r - 1], target).start()
            return
        whole, mine = (gw, wt) if kind == 0 else (gk, kw)
        if link <= 2:
            back, index = along(i, link)
            source = (r, back)
            ssem = w_zs.at[link - 1, index] if kind == 0 else k_zs.at[link - 1, r, index]
        elif kind == 1:
            source, ssem = (0, 0), k_ys.at[link - 3]
        elif r == 3:
            source, ssem = (1 if link == 3 else 2, i), w_fs.at[i]
        else:
            source, ssem = (0, i), w_ys.at[link - 3, i]
        s = slot(*source)
        src = mine if source == (0, 0) else whole.at[s]
        rsem = w_r.at[r, i] if kind == 0 else k_r.at[r, i]
        send(src, whole.at[s], ssem, rsem, target).start()

    def gather(*place):
        for what, kind, r, i in PLAN.get(place, ()):
            if what == 0:
                take(kind, r, i)
            else:
                pass_on(what, kind, r, i)

    def gather_at(step, steps, group, part):
        for n in steps:
            if (group, n, part) in PLAN:

                @pl.when(step == n)
                def _():
                    gather(group, n, part)

    send(wt, gw.at[me], w_ps.at[0, 0], w_p.at[0, 0], partner).start()
    send(kw, gk.at[me], k_ps.at[0, 0], k_p.at[0, 0], partner).start()
    gather(0, 0)
    for n in range(2):
        tb_s[n] = jnp.broadcast_to(tbl[0:1, n : n + 1], (8, HD))
    for m in range(1, NX):
        target = (me, mod(x + m, NX))
        send(tb_s, tb.at[x], t_s.at[m - 1], t_r.at[m - 1], target).start()

    def head_cols(h):
        return pl.ds(pl.multiple_of(h * HD, HD), HD)

    loads[0].wait()
    loads[1].wait()

    def update(h, carry):
        cb = ccol[h]
        gap = jnp.exp(cb[BLK - 1 : BLK, :] - cb)
        weighted = (k_s[:, head_cols(h)].astype(F32) * gap).astype(BF16)
        u_s[h] = lax.dot_general(
            weighted, v_s[:, head_cols(h)], TN_DIMS, preferred_element_type=F32
        )
        return carry

    lax.fori_loop(0, HEADS, update, 0)
    gather(1, 0)
    ub_s[...] = u_s[pl.ds(4 * (1 - c), 4)].astype(BF16)
    send(ub_s, ub_r, s1_s.at[0], s1_r.at[0], partner).start()
    send(a_s, a_r, s1_s.at[1], s1_r.at[1], partner).start()

    def chip_parts():
        own = u_s[pl.ds(4 * c, 4)]
        other = ub_r[...].astype(F32)
        a_own = a_s[pl.ds(4 * c, 4)]
        a_other = a_r[pl.ds(4 * c, 4)]
        first = c == 0
        return (
            jnp.where(first, own, other),
            jnp.where(first, other, own),
            jnp.where(first, a_own, a_other),
            jnp.where(first, a_other, a_own),
        )

    def split(row):
        a = jnp.broadcast_to(row, (16, HD))
        rows = lax.broadcasted_iota(jnp.int32, (16, HD), 0)
        hi = a.astype(BF16).astype(F32)
        mid = (a - hi).astype(BF16).astype(F32)
        low = a - hi - mid
        tile = jnp.where(rows == 0, hi, jnp.where(rows == 1, mid, jnp.where(rows == 2, low, 0.0)))
        return tile.astype(BF16)

    def joined(message):
        value = message.astype(F32)
        return value[0:64, :], jnp.sum(value[64:80, :], axis=0, keepdims=True)

    def scan_chip():
        arrive(ub_r, s1_r.at[0])
        arrive(a_r, s1_r.at[1])
        u0, u1, a0, a1 = chip_parts()
        total = jnp.exp(a1)[:, 0:1, :] * u0 + u1
        a_chip = a0 + a1
        for hl in range(4):
            tile = split(a_chip[hl, 0:1, :])
            for half in range(2):
                st_s[2 * hl + half, 0:64, :] = total[hl, 64 * half : 64 * half + 64, :].astype(BF16)
                st_s[2 * hl + half, 64:80, :] = tile
        st_r[z] = st_s[z]
        for m in range(1, NZ):
            zz = mod(z + m, NZ)
            send(st_s.at[zz], st_r.at[z], s2_s.at[m], s2_r.at[m], (at(y, zz, c), x)).start()

    def chip_total(zz):
        return joined(st_r[zz])

    def scan_row():
        for m in range(1, NZ):
            arrive(st_r.at[mod(z - m, NZ)], s2_r.at[m])
        total = jnp.zeros((64, HD), F32)
        a_row = jnp.zeros((1, HD), F32)
        for zz in range(NZ):
            t, a = chip_total(zz)
            total = jnp.exp(a) * total + t
            a_row = a_row + a
        sr_s[0:64, :] = total.astype(BF16)
        sr_s[64:80, :] = split(a_row)
        sr_r[y] = sr_s[...]
        for m in range(1, NY):
            target = (at(mod(y + m, NY), z, c), x)
            send(sr_s, sr_r.at[y], s3_s.at[m], s3_r.at[m], target).start()

    def scan_back():
        for m in range(1, NY):
            arrive(sr_r.at[mod(y - m, NY)], s3_r.at[m])
        enter = jnp.zeros((64, HD), F32)
        for yy in range(NY):
            t, a = joined(sr_r[yy])
            moved = jnp.exp(a) * enter + t
            enter = jnp.where(yy < y, moved, enter)
        for zz in range(NZ):
            se_s[zz] = enter.astype(BF16)
            t, a = chip_total(zz)
            enter = jnp.exp(a) * enter + t
        se_r[z] = se_s[z]
        for m in range(1, NZ):
            zz = mod(z + m, NZ)
            send(se_s.at[zz], se_r.at[z], s4_s.at[m], s4_r.at[m], (at(y, zz, c), x)).start()

    def scan_cores():
        for m in range(1, NZ):
            arrive(se_r.at[mod(z - m, NZ)], s4_r.at[m])
        enter = se_r[...].reshape(4, HD, HD).astype(F32)
        u0, _, a0, _ = chip_parts()
        after = jnp.exp(a0)[:, 0:1, :] * enter + u0
        first = c == 0
        sf_s[...] = jnp.where(first, after, enter).astype(BF16)
        send(sf_s, sf_r, s5_s.at[0], s5_r.at[0], partner).start()
        state[pl.ds(4 * c, 4)] = jnp.where(first, enter, after).astype(BF16)

    loads[2].wait()
    loads[4].wait()
    loads[5].wait()

    tri_a = lax.broadcasted_iota(jnp.int32, (HD, HD), 0)
    tri_b = lax.broadcasted_iota(jnp.int32, (HD, HD), 1)
    seen = tri_b <= tri_a

    def within(h, carry):
        gather_at(h, range(HEADS), 2, 0)

        @pl.when(h == 1)
        def _():
            scan_chip()

        @pl.when(h == 5)
        def _():
            scan_row()

        gather_at(h, range(HEADS), 2, 1)

        for tq in range(4):
            rows = pl.ds(tq * HD, HD)
            width = HD * (tq + 1)
            products = lax.dot_general(
                q_s[rows, head_cols(h)], k_s[0:width, head_cols(h)], NT_DIMS,
                preferred_element_type=F32,
            )
            c_here = ccol[h, rows, :]
            blocks = []
            for ts in range(tq + 1):
                gap = c_here - crow[h, :, ts * HD : ts * HD + HD]
                piece = products[:, ts * HD : ts * HD + HD]
                if ts == tq:
                    gap = jnp.where(seen, gap, 0.0)
                    piece = jnp.where(seen, piece, 0.0)
                blocks.append((piece * jnp.exp(gap)).astype(BF16))
            scores = jnp.concatenate(blocks, axis=1) if tq else blocks[0]
            inner[rows, head_cols(h)] = jnp.dot(
                scores, v_s[0:width, head_cols(h)], preferred_element_type=F32
            )

        gather_at(h, range(HEADS), 2, 2)
        return carry

    lax.fori_loop(0, HEADS, within, 0)
    gather(3, 0)
    scan_back()
    gather(3, 1)
    gather(4, 0)
    scan_cores()
    gather(4, 1)
    gather(5, 0)
    arrive(sf_r, s5_r.at[0])
    gather(5, 1)
    state[pl.ds(4 * (1 - c), 4)] = sf_r[...]

    def finish(h, carry):
        outer = jnp.dot(q_s[:, head_cols(h)], state[h], preferred_element_type=F32)
        kept = inner[:, head_cols(h)] + outer * jnp.exp(ccol[h])
        scale = lax.rsqrt(jnp.mean(kept * kept, axis=-1, keepdims=True) + 1e-05)
        mixed[:, head_cols(h)] = (kept * scale).astype(BF16)
        return carry

    lax.fori_loop(0, HEADS, finish, 0)
    loads[3].wait()
    gather(6, 0)

    def row_of(r):
        step = jnp.where(r == 1, 3, jnp.where(r == 2, 1, jnp.where(r == 3, 2, 0)))
        return mod(y + step, NY)

    def chunk_rows(j):
        return row_of(lax.div(j, 2)) * 16 + lax.rem(j, 2) * 8

    def direction(d):
        return (right, -1) if d == 0 else (left, 1)

    def forward(j, step, d, value):
        rs_s[d, j, step] = value.astype(BF16)
        send(
            rs_s.at[d, j, step], rs_r.at[d, j, step],
            rs_ss.at[d, j, step], rs_rs.at[d, j, step], direction(d)[0],
        ).start()

    def w_ready(r):
        for i in range(NZ):
            s = at(row_of(r), near(i), 1 - c)
            arrive(gw.at[s], w_p.at[r, i])

    def reduce(t, carry):
        steps = range(CH + 4)
        gather_at(t, steps, 7, 0)
        for r in range(NY):

            @pl.when(t == 2 * r)
            def _():
                w_ready(r)

        @pl.when(t < CH)
        def _():
            weight = gw[pl.ds(chunk_rows(t), 8)].reshape(CW, HEADS * HD)
            product = lax.dot_general(mixed[...], weight, NT_DIMS, preferred_element_type=F32)
            part[t] = product.reshape(NX, PAGE, CW)
            for d in range(2):
                block = mod(x + direction(d)[1], NX)
                forward(t, 0, d, part[t, block, :, d * DW : d * DW + DW])

        gather_at(t, steps, 7, 1)
        for step in (1, 2):

            @pl.when(jnp.logical_and(t >= step + 1, t < CH + step + 1))
            def _():
                j = t - step - 1
                for d in range(2):
                    arrive(rs_r.at[d, j, step - 1], rs_rs.at[d, j, step - 1])
                    block = lax.rem(x + direction(d)[1] * (1 + step) + 2 * NX, NX)
                    own = part[j, block, :, d * DW : d * DW + DW]
                    forward(j, step, d, rs_r[d, j, step - 1].astype(F32) + own)

            gather_at(t, steps, 7, step + 1)

        @pl.when(t >= 4)
        def _():
            j = t - 4
            for d in range(2):
                arrive(rs_r.at[d, j, 2], rs_rs.at[d, j, 2])
                own = part[j, x, :, d * DW : d * DW + DW]
                cols = pl.ds(pl.multiple_of(chunk_rows(j) * 64 + d * DW, DW), DW)
                hid[:, cols] = rs_r[d, j, 2].astype(F32) + own + res_s[:, cols].astype(F32)

        gather_at(t, steps, 7, 4)
        return carry

    lax.fori_loop(0, CH + 4, reduce, 0)

    def square(j, total):
        cols = pl.ds(pl.multiple_of(j * CW, CW), CW)
        value = hid[:, cols]
        return total + jnp.sum(value * value, axis=-1, keepdims=True)

    squares = lax.fori_loop(0, CH, square, jnp.zeros((PAGE, 1), F32))
    scale = lax.rsqrt(squares * (1.0 / D) + 1e-05)

    def normalize(j, carry):
        cols = pl.ds(pl.multiple_of(j * CW, CW), CW)
        norm[:, cols] = (hid[:, cols] * scale * gain[:, cols]).astype(BF16)
        return carry

    lax.fori_loop(0, CH, normalize, 0)

    gather(8, 0)
    gather(9, 0)

    def k_ready(i, carry):
        for r in range(NY):
            s = at(row_of(r), near(i), 1 - c)
            arrive(gk.at[s], k_p.at[r, i])
        return carry

    lax.fori_loop(0, NZ, k_ready, 0)
    x_left = mod(x - 1, NX)
    x_right = mod(x + 1, NX)
    x_far = mod(x + 2, NX)

    def tile(n):
        return pl.ds(pl.multiple_of(n * TW, TW), TW)

    def project(n, carry):
        @pl.when(n < NT)
        def _():
            weight = gk[:, :, tile(n)].reshape(D, TW)
            value = jnp.dot(norm[...], weight, preferred_element_type=F32)
            pg[x, :, tile(n)] = value.astype(BF16)
            own = pg.at[x, :, tile(n)]
            send(own, own, g_s.at[0, n], g_r.at[0, n], right).start()
            send(own, own, g_s.at[1, n], g_r.at[1, n], left).start()

        @pl.when(n >= 2)
        def _():
            j = n - 2
            arrive(pg.at[x_left, :, tile(j)], g_r.at[0, j])
            arrive(pg.at[x_right, :, tile(j)], g_r.at[1, j])
            early = j < 2
            source = jnp.where(early, x_left, x_right)
            target = (me, jnp.where(early, right[1], left[1]))
            page = pg.at[source, :, tile(j)]
            send(page, page, g_f.at[j], g_r.at[2, j], target).start()

        return carry

    lax.fori_loop(0, NT + 2, project, 0)

    def drain_w(i, carry):
        for d in range(2):
            sent(gw.at[0], w_ys.at[d, i])
        sent(gw.at[0], w_fs.at[i])
        for r in range(NY):
            sent(gw.at[0], w_ps.at[r, i])
            sent(gk.at[0], k_ps.at[r, i])
        return carry

    lax.fori_loop(0, NZ, drain_w, 0)
    for n in range(4):
        for d in range(2):
            if n < 3 or d == 1:
                sent(gw.at[0], w_zs.at[d, n])
            for r in range(NY):
                if n < 3 or d == r % 2:
                    sent(gk.at[0], k_zs.at[d, r, n])
    for d in range(2):
        sent(gk.at[0], k_ys.at[d])
        sent(gk.at[0, pl.ds(0, 32)], k_fs.at[d])
    sent(ub_s, s1_s.at[0])
    sent(a_s, s1_s.at[1])
    sent(sf_s, s5_s.at[0])
    for m in range(1, NZ):
        sent(st_s.at[0], s2_s.at[m])
        sent(se_s.at[0], s4_s.at[m])
    for m in range(1, NY):
        sent(sr_s, s3_s.at[m])

    def drain_rs(j, carry):
        for d in range(2):
            for step in range(3):
                sent(rs_s.at[0, 0, 0], rs_ss.at[d, j, step])
        return carry

    lax.fori_loop(0, CH, drain_rs, 0)
    tb[x] = tb_s[...]
    for m in range(1, NX):
        arrive(tb.at[mod(x - m, NX)], t_r.at[m - 1])
        sent(tb_s, t_s.at[m - 1])
    for n in range(NT):
        sent(pg.at[0, :, pl.ds(0, TW)], g_s.at[0, n])
        sent(pg.at[0, :, pl.ds(0, TW)], g_s.at[1, n])
        sent(pg.at[0, :, pl.ds(0, TW)], g_f.at[n])
    for n in range(NT):
        arrive(pg.at[x_far, :, tile(n)], g_r.at[2, n])
    here = [tb[p, 0] == x for p in range(NX)]
    for s in range(2):
        total = jnp.zeros((PAGE, KVW), BF16)
        for p in range(NX):
            hit = jnp.logical_and(here[p], tb[p, 1] == s).astype(F32)
            hit = jnp.broadcast_to(hit[0:1, 0:1], (PAGE, KVW))
            total = jnp.where(hit > 0.5, pg[p], total)
        cache[s] = total


def on_device(query_rows, key_rows, value_rows, log_decay, residual, out_weight, norm_gain, kv_weight, block_table):
    vm, dma = pltpu.VMEM, pltpu.SemaphoreType.DMA
    hbm = pl.BlockSpec(memory_space=pl.ANY)
    vmem = pl.BlockSpec(memory_space=pltpu.VMEM)
    cache = pl.pallas_call(
        kernel,
        out_shape=jax.ShapeDtypeStruct((2, PAGE, KVW), BF16),
        in_specs=[hbm, hbm, hbm, hbm, hbm, vmem, hbm, vmem, vmem],
        out_specs=vmem,
        scratch_shapes=[
            vm((64, 64, HEADS * HD), BF16),
            vm((64, 64, KVW), BF16),
            vm((BLK, HEADS * HD), BF16),
            vm((BLK, HEADS * HD), BF16),
            vm((BLK, HEADS * HD), BF16),
            vm((PAGE, D), BF16),
            vm((HEADS, 1, BLK), F32),
            vm((HEADS, BLK, HD), F32),
            vm((HEADS, 8, HD), F32),
            vm((HEADS, 8, HD), F32),
            vm((HEADS, HD, HD), F32),
            vm((BLK, HEADS * HD), F32),
            vm((BLK, HEADS * HD), BF16),
            vm((4, HD, HD), BF16),
            vm((4, HD, HD), BF16),
            vm((NZ, 80, HD), BF16),
            vm((NZ, 80, HD), BF16),
            vm((80, HD), BF16),
            vm((NY, 80, HD), BF16),
            vm((NZ, 64, HD), BF16),
            vm((NZ, 64, HD), BF16),
            vm((4, HD, HD), BF16),
            vm((4, HD, HD), BF16),
            vm((HEADS, HD, HD), BF16),
            vm((CH, NX, PAGE, CW), F32),
            vm((2, CH, 3, PAGE, DW), BF16),
            vm((2, CH, 3, PAGE, DW), BF16),
            vm((PAGE, D), F32),
            vm((PAGE, D), BF16),
            vm((NX, PAGE, KVW), BF16),
            vm((NX, 2, 8, HD), jnp.int32),
            vm((2, 8, HD), jnp.int32),
            dma((6,)),
            dma((2, 4)), dma((2, NZ)), dma((NZ,)), dma((NY, NZ)), dma((NY, NZ)), dma((NY, NZ)),
            dma((2, NY, 4)), dma((2,)), dma((2,)), dma((NY, NZ)), dma((NY, NZ)), dma((2,)), dma((NY, NZ)),
            dma((2,)), dma((2,)), dma((NZ,)), dma((NZ,)), dma((NY,)), dma((NY,)),
            dma((NZ,)), dma((NZ,)), dma((1,)), dma((1,)),
            dma((2, CH, 3)), dma((2, CH, 3)), dma((2, NT)), dma((NT,)), dma((3, NT)), dma((3,)), dma((3,)),
        ],
        compiler_params=pltpu.CompilerParams(
            collective_id=0, has_side_effects=True, vmem_limit_bytes=63 * 1024 * 1024
        ),
        name="layer",
    )(
        out_weight.T, kv_weight, query_rows, key_rows, value_rows, log_decay,
        residual, norm_gain.reshape(1, D), block_table,
    )
    return cache.reshape(1, 1, 2, PAGE, KVW)


def solution(mesh):
    placed = (
        P("seq", "pool"),
        P("seq", "pool"),
        P("seq", "pool"),
        P("pool", "seq"),
        P(("seq", "pool"), None),
        P("pool", "seq"),
        P(),
        P("seq", None),
        P(("seq", "pool"), None),
    )
    return jax.shard_map(
        on_device,
        mesh=mesh,
        in_specs=placed,
        out_specs=P("seq", "pool", None, None, None),
        check_vma=False,
    )
```

```python
import jax
import jax.numpy as jnp
from jax import lax
from jax.experimental import pallas as pl
from jax.experimental.pallas import tpu as pltpu
from jax.sharding import PartitionSpec as P

NY, NZ, NX = 4, 8, 4
HEADS = 8
HD = 128
BLK = 512
PAGE = 128
D = 4096
KVW = 1024
CH = 8
CW = D // CH
DW = CW // 2
NT = 4
TW = KVW // NT
F32 = jnp.float32
BF16 = jnp.bfloat16
MESH = pl.DeviceIdType.MESH
FAR_Z = (4, 3, 5, 2, 6, 1, 7)
NT_DIMS = (((1,), (1,)), ((), ()))
TN_DIMS = (((0,), (0,)), ((), ()))

PLAN = {
    (0, 0): ((1, 0, 0, 1), (2, 0, 0, 2), (3, 0, 1, 0), (4, 0, 2, 0),),
    (1, 0): ((3, 1, 1, 0), (4, 1, 2, 0),),
    (2, 2, 2): ((0, 0, 0, 1), (0, 0, 0, 2), (0, 0, 1, 0), (0, 0, 2, 0), (2, 0, 0, 4), (3, 0, 1, 1), (4, 0, 2, 1),),
    (2, 5, 0): ((1, 0, 0, 3), (3, 0, 1, 2), (4, 0, 2, 2), (0, 1, 1, 0), (0, 1, 2, 0),),
    (2, 5, 1): ((4, 2, 2, 0),),
    (2, 5, 2): ((0, 0, 1, 1), (0, 0, 2, 1), (3, 2, 1, 0),),
    (2, 6, 2): ((0, 0, 0, 4), (2, 0, 0, 6), (4, 0, 2, 4),),
    (2, 7, 0): ((3, 0, 1, 4), (0, 0, 0, 3), (1, 0, 0, 5), (0, 0, 1, 2), (0, 0, 2, 2),),
    (2, 7, 1): ((4, 0, 2, 3),),
    (2, 7, 2): ((3, 0, 1, 3),),
    (4, 0): ((2, 1, 1, 2), (0, 1, 3, 0), (4, 0, 3, 1), (0, 0, 0, 6), (0, 0, 2, 4), (3, 0, 1, 6), (1, 1, 1, 1), (2, 0, 0, 7), (0, 0, 0, 5), (0, 0, 1, 4), (4, 0, 2, 5), (0, 0, 2, 3), (3, 0, 1, 5), (1, 1, 0, 1), (2, 1, 0, 2),),
    (4, 1): ((0, 0, 1, 3),),
    (5, 0): ((0, 1, 1, 2), (4, 0, 2, 6),),
    (6, 0): ((0, 0, 0, 7), (0, 0, 3, 1), (0, 0, 1, 6), (0, 1, 1, 1), (3, 0, 1, 7), (1, 1, 2, 1), (2, 1, 2, 2),),
    (7, 0, 0): ((4, 0, 2, 7),),
    (7, 0, 1): ((0, 0, 2, 5), (3, 0, 3, 0), (1, 1, 3, 1), (2, 1, 3, 2),),
    (7, 1, 1): ((0, 0, 1, 5), (0, 1, 0, 1), (0, 1, 0, 2),),
    (7, 2, 0): ((4, 0, 3, 3), (0, 0, 2, 6), (3, 0, 3, 2), (1, 1, 0, 3), (2, 1, 1, 4), (0, 0, 1, 7), (0, 1, 2, 1), (0, 1, 2, 2), (4, 0, 3, 5),),
    (7, 2, 1): ((0, 0, 2, 7), (3, 0, 3, 4), (1, 1, 2, 3), (2, 1, 2, 4),),
    (7, 3, 1): ((0, 0, 3, 0), (0, 1, 3, 1), (0, 1, 3, 2), (4, 0, 3, 7),),
    (7, 3, 2): ((0, 0, 3, 3), (3, 0, 3, 6), (1, 1, 3, 3), (2, 1, 3, 4), (0, 0, 3, 2), (0, 1, 0, 3), (0, 1, 1, 4),),
    (7, 4, 1): ((0, 0, 3, 5), (1, 1, 0, 5), (2, 1, 1, 6),),
    (7, 4, 2): ((0, 0, 3, 4), (0, 1, 2, 3), (0, 1, 2, 4),),
    (7, 4, 3): ((0, 0, 3, 7), (1, 1, 2, 5), (2, 1, 2, 6),),
    (7, 5, 1): ((0, 0, 3, 6), (0, 1, 3, 3), (0, 1, 3, 4),),
    (7, 5, 2): ((1, 1, 3, 5), (2, 1, 3, 6),),
    (7, 5, 3): ((0, 1, 0, 5), (0, 1, 1, 6),),
    (7, 6, 2): ((1, 1, 0, 7), (2, 1, 1, 7), (0, 1, 2, 5), (0, 1, 2, 6),),
    (7, 6, 3): ((1, 1, 2, 7), (2, 1, 0, 4),),
    (7, 7, 1): ((0, 1, 3, 5), (0, 1, 3, 6),),
    (7, 7, 2): ((1, 1, 1, 3), (2, 1, 3, 7),),
    (7, 7, 3): ((0, 1, 0, 7), (0, 1, 1, 7),),
    (7, 8, 2): ((0, 1, 2, 7), (0, 1, 0, 4), (2, 1, 0, 6),),
    (7, 9, 2): ((0, 1, 1, 3), (0, 1, 3, 7), (1, 1, 1, 5),),
    (7, 10, 0): ((0, 1, 0, 6),),
    (7, 11, 0): ((0, 1, 1, 5),),
}


def kernel(
    wt, kw, q_hbm, k_hbm, v_hbm, ld, res_hbm, gain, tbl,
    cache,
    gw, gk, q_s, k_s, v_s, res_s, crow, ccol, a_s, a_r, u_s, inner, mixed,
    ub_s, ub_r, st_s, st_r, sr_s, sr_r, se_s, se_r, sf_s, sf_r, state,
    part, rs_s, rs_r, squares, norm, pg, tb, tb_s,
    ld_sem, w_zs, w_ys, w_fs, w_ps, w_r, w_p,
    k_zs, k_ys, k_fs, k_ps, k_r, k_h, k_p,
    s1_s, s1_r, s2_s, s2_r, s3_s, s3_r, s4_s, s4_r, s5_s, s5_r,
    rs_ss, rs_rs, g_s, g_f, g_r, t_s, t_r,
):
    me = lax.axis_index("seq")
    x = lax.axis_index("pool")
    y = lax.div(me, 16)
    z = lax.rem(lax.div(me, 2), 8)
    c = lax.rem(me, 2)

    def at(yy, zz, cc):
        return (yy * NZ + zz) * 2 + cc

    def mod(value, size):
        return lax.rem(value + size, size)

    up = (at(mod(y + 1, NY), z, c), x)
    down = (at(mod(y - 1, NY), z, c), x)
    ahead = (at(y, mod(z + 1, NZ), c), x)
    behind = (at(y, mod(z - 1, NZ), c), x)
    partner = (at(y, z, 1 - c), x)
    right = (me, mod(x + 1, NX))
    left = (me, mod(x - 1, NX))

    def send(src, dst, ssem, rsem, device):
        copy = pltpu.make_async_remote_copy(
            src_ref=src, dst_ref=dst, send_sem=ssem, recv_sem=rsem,
            device_id=device, device_id_type=MESH,
        )
        return copy

    def arrive(ref, rsem):
        send(ref, ref, rsem, rsem, partner).wait_recv()

    def sent(ref, ssem):
        send(ref, ref, ssem, ssem, partner).wait_send()

    peers = [partner]
    peers += [(at(y, mod(z + m, NZ), c), x) for m in range(1, NZ)]
    peers += [(at(mod(y + m, NY), z, c), x) for m in range(1, NY)]
    peers += [(me, mod(x + m, NX)) for m in range(1, NX)]
    barrier = pltpu.get_barrier_semaphore()
    for peer in peers:
        pl.semaphore_signal(barrier, inc=1, device_id=peer, device_id_type=MESH)
    loads = [
        pltpu.make_async_copy(k_hbm, k_s, ld_sem.at[0]),
        pltpu.make_async_copy(v_hbm, v_s, ld_sem.at[1]),
        pltpu.make_async_copy(q_hbm, q_s, ld_sem.at[2]),
        pltpu.make_async_copy(res_hbm, res_s, ld_sem.at[3]),
        pltpu.make_async_copy(wt, gw.at[me], ld_sem.at[4]),
        pltpu.make_async_copy(kw, gk.at[me], ld_sem.at[5]),
    ]
    for load in loads:
        load.start()
    steps_a = lax.broadcasted_iota(jnp.int32, (BLK, BLK), 0)
    steps_b = lax.broadcasted_iota(jnp.int32, (BLK, BLK), 1)
    lower = jnp.where(steps_b <= steps_a, 1.0, 0.0).astype(BF16)
    rest = ld[...]
    sums_row = jnp.zeros((HEADS, BLK), F32)
    sums_col = jnp.zeros((BLK, HEADS), F32)
    for _ in range(3):
        piece = rest.astype(BF16)
        rest = rest - piece.astype(F32)
        sums_row += lax.dot_general(piece, lower, NT_DIMS, preferred_element_type=F32)
        sums_col += lax.dot_general(lower, piece, NT_DIMS, preferred_element_type=F32)
    for h in range(HEADS):
        crow[h] = sums_row[h : h + 1, :]
        wide = jnp.broadcast_to(sums_col[:, h : h + 1], (BLK, HD))
        ccol[h] = wide
        a_s[h] = jnp.broadcast_to(wide[BLK - 1 : BLK, :], (8, HD))

    pl.semaphore_wait(barrier, len(peers))

    def near(i):
        half = lax.div(i + 1, 2)
        return mod(z + half * (1 - 2 * lax.rem(i, 2)), NZ)

    row_step = (0, 3, 1, 2)

    def slot(r, i):
        return at(mod(y + row_step[r], NY), near(i), c)

    lines = (None, ahead, behind, up, down)

    def take(kind, r, i):
        if kind == 0:
            s = slot(r, i)
            arrive(gw.at[s], w_r.at[r, i])
            send(gw.at[s], gw.at[s], w_ps.at[r, i], w_p.at[r, i], partner).start()
            return
        s = slot(r, i)
        if r == 3 and i == 0:
            arrive(gk.at[s, pl.ds(0, 32)], k_h.at[0])
            arrive(gk.at[s, pl.ds(32, 32)], k_h.at[1])
        else:
            arrive(gk.at[s], k_r.at[r, i])
        send(gk.at[s], gk.at[s], k_ps.at[r, i], k_p.at[r, i], partner).start()

    def along(i, link):
        back = 0 if i <= 2 else (6 if i == 7 and link == 2 else i - 2)
        index = (i - 1) // 2 if link == 1 else (3 if i == 7 else i // 2 - 1)
        return back, index

    def pass_on(link, kind, r, i):
        target = lines[link]
        if kind == 2:
            s = slot(r, 0)
            rows = gk.at[s, pl.ds(32 * (r - 1), 32)]
            send(rows, rows, k_fs.at[r - 1], k_h.at[r - 1], target).start()
            return
        whole, mine = (gw, wt) if kind == 0 else (gk, kw)
        if link <= 2:
            back, index = along(i, link)
            source = (r, back)
            ssem = w_zs.at[link - 1, index] if kind == 0 else k_zs.at[link - 1, r, index]
        elif kind == 1:
            source, ssem = (0, 0), k_ys.at[link - 3]
        elif r == 3:
            source, ssem = (1 if link == 3 else 2, i), w_fs.at[i]
        else:
            source, ssem = (0, i), w_ys.at[link - 3, i]
        s = slot(*source)
        src = mine if source == (0, 0) else whole.at[s]
        rsem = w_r.at[r, i] if kind == 0 else k_r.at[r, i]
        send(src, whole.at[s], ssem, rsem, target).start()

    def gather(*place):
        for what, kind, r, i in PLAN.get(place, ()):
            if what == 0:
                take(kind, r, i)
            else:
                pass_on(what, kind, r, i)

    def gather_at(step, steps, group, part):
        for n in steps:
            if (group, n, part) in PLAN:

                @pl.when(step == n)
                def _():
                    gather(group, n, part)

    send(wt, gw.at[me], w_ps.at[0, 0], w_p.at[0, 0], partner).start()
    send(kw, gk.at[me], k_ps.at[0, 0], k_p.at[0, 0], partner).start()
    gather(0, 0)
    for n in range(2):
        tb_s[n] = jnp.broadcast_to(tbl[0:1, n : n + 1], (8, HD))
    for m in range(1, NX):
        target = (me, mod(x + m, NX))
        send(tb_s, tb.at[x], t_s.at[m - 1], t_r.at[m - 1], target).start()

    def head_cols(h):
        return pl.ds(pl.multiple_of(h * HD, HD), HD)

    loads[0].wait()
    loads[1].wait()

    def update(h, carry):
        cb = ccol[h]
        gap = jnp.exp(cb[BLK - 1 : BLK, :] - cb)
        weighted = (k_s[:, head_cols(h)].astype(F32) * gap).astype(BF16)
        u_s[h] = lax.dot_general(
            weighted, v_s[:, head_cols(h)], TN_DIMS, preferred_element_type=F32
        )
        return carry

    lax.fori_loop(0, HEADS, update, 0)
    gather(1, 0)
    ub_s[...] = u_s[pl.ds(4 * (1 - c), 4)].astype(BF16)
    send(ub_s, ub_r, s1_s.at[0], s1_r.at[0], partner).start()
    send(a_s, a_r, s1_s.at[1], s1_r.at[1], partner).start()

    def chip_parts():
        own = u_s[pl.ds(4 * c, 4)]
        other = ub_r[...].astype(F32)
        a_own = a_s[pl.ds(4 * c, 4)]
        a_other = a_r[pl.ds(4 * c, 4)]
        first = c == 0
        return (
            jnp.where(first, own, other),
            jnp.where(first, other, own),
            jnp.where(first, a_own, a_other),
            jnp.where(first, a_other, a_own),
        )

    def split(row):
        a = jnp.broadcast_to(row, (16, HD))
        rows = lax.broadcasted_iota(jnp.int32, (16, HD), 0)
        hi = a.astype(BF16).astype(F32)
        mid = (a - hi).astype(BF16).astype(F32)
        low = a - hi - mid
        tile = jnp.where(rows == 0, hi, jnp.where(rows == 1, mid, jnp.where(rows == 2, low, 0.0)))
        return tile.astype(BF16)

    def joined(message):
        value = message.astype(F32)
        return value[0:64, :], jnp.sum(value[64:80, :], axis=0, keepdims=True)

    def scan_chip():
        arrive(ub_r, s1_r.at[0])
        arrive(a_r, s1_r.at[1])
        u0, u1, a0, a1 = chip_parts()
        total = jnp.exp(a1)[:, 0:1, :] * u0 + u1
        a_chip = a0 + a1
        for hl in range(4):
            tile = split(a_chip[hl, 0:1, :])
            for half in range(2):
                st_s[2 * hl + half, 0:64, :] = total[hl, 64 * half : 64 * half + 64, :].astype(BF16)
                st_s[2 * hl + half, 64:80, :] = tile
        st_r[z] = st_s[z]
        for m in FAR_Z:
            zz = mod(z + m, NZ)
            send(st_s.at[zz], st_r.at[z], s2_s.at[m], s2_r.at[m], (at(y, zz, c), x)).start()

    def chip_total(zz):
        return joined(st_r[zz])

    def scan_row():
        for m in range(1, NZ):
            arrive(st_r.at[mod(z - m, NZ)], s2_r.at[m])
        total = jnp.zeros((64, HD), F32)
        a_row = jnp.zeros((1, HD), F32)
        for zz in range(NZ):
            t, a = chip_total(zz)
            total = jnp.exp(a) * total + t
            a_row = a_row + a
        sr_s[0:64, :] = total.astype(BF16)
        sr_s[64:80, :] = split(a_row)
        sr_r[y] = sr_s[...]
        for m in (2, 1, 3):
            target = (at(mod(y + m, NY), z, c), x)
            send(sr_s, sr_r.at[y], s3_s.at[m], s3_r.at[m], target).start()

    def scan_back():
        for m in range(1, NY):
            arrive(sr_r.at[mod(y - m, NY)], s3_r.at[m])
        enter = jnp.zeros((64, HD), F32)
        for yy in range(NY):
            t, a = joined(sr_r[yy])
            moved = jnp.exp(a) * enter + t
            enter = jnp.where(yy < y, moved, enter)
        for zz in range(NZ):
            se_s[zz] = enter.astype(BF16)
            t, a = chip_total(zz)
            enter = jnp.exp(a) * enter + t
        se_r[z] = se_s[z]
        for m in FAR_Z:
            zz = mod(z + m, NZ)
            send(se_s.at[zz], se_r.at[z], s4_s.at[m], s4_r.at[m], (at(y, zz, c), x)).start()

    def scan_cores():
        for m in range(1, NZ):
            arrive(se_r.at[mod(z - m, NZ)], s4_r.at[m])
        enter = se_r[...].reshape(4, HD, HD).astype(F32)
        u0, _, a0, _ = chip_parts()
        after = jnp.exp(a0)[:, 0:1, :] * enter + u0
        first = c == 0
        sf_s[...] = jnp.where(first, after, enter).astype(BF16)
        send(sf_s, sf_r, s5_s.at[0], s5_r.at[0], partner).start()
        state[pl.ds(4 * c, 4)] = jnp.where(first, enter, after).astype(BF16)

    loads[2].wait()
    loads[4].wait()
    loads[5].wait()

    tri_a = lax.broadcasted_iota(jnp.int32, (HD, HD), 0)
    tri_b = lax.broadcasted_iota(jnp.int32, (HD, HD), 1)
    seen = tri_b <= tri_a

    def within(h, carry):
        gather_at(h, range(HEADS), 2, 0)

        @pl.when(h == 1)
        def _():
            scan_chip()

        @pl.when(h == 5)
        def _():
            scan_row()

        @pl.when(h == 7)
        def _():
            scan_back()

        gather_at(h, range(HEADS), 2, 1)

        for tq in range(4):
            rows = pl.ds(tq * HD, HD)
            width = HD * (tq + 1)
            products = lax.dot_general(
                q_s[rows, head_cols(h)], k_s[0:width, head_cols(h)], NT_DIMS,
                preferred_element_type=F32,
            )
            c_here = ccol[h, rows, :]
            blocks = []
            for ts in range(tq + 1):
                gap = c_here - crow[h, :, ts * HD : ts * HD + HD]
                piece = products[:, ts * HD : ts * HD + HD]
                if ts == tq:
                    gap = jnp.where(seen, gap, 0.0)
                    piece = jnp.where(seen, piece, 0.0)
                blocks.append((piece * jnp.exp(gap)).astype(BF16))
            scores = jnp.concatenate(blocks, axis=1) if tq else blocks[0]
            inner[rows, head_cols(h)] = jnp.dot(
                scores, v_s[0:width, head_cols(h)], preferred_element_type=F32
            )

        ccol[h] = jnp.exp(ccol[h])
        gather_at(h, range(HEADS), 2, 2)
        return carry

    lax.fori_loop(0, HEADS, within, 0)
    gather(4, 0)
    scan_cores()
    gather(4, 1)
    gather(5, 0)
    arrive(sf_r, s5_r.at[0])
    gather(5, 1)
    state[pl.ds(4 * (1 - c), 4)] = sf_r[...]

    def finish(h, carry):
        outer = jnp.dot(q_s[:, head_cols(h)], state[h], preferred_element_type=F32)
        kept = inner[:, head_cols(h)] + outer * ccol[h]
        scale = lax.rsqrt(jnp.mean(kept * kept, axis=-1, keepdims=True) + 1e-05)
        mixed[:, head_cols(h)] = (kept * scale).astype(BF16)
        return carry

    lax.fori_loop(0, HEADS, finish, 0)
    loads[3].wait()
    gather(6, 0)

    def row_of(r):
        step = jnp.where(r == 1, 3, jnp.where(r == 2, 1, jnp.where(r == 3, 2, 0)))
        return mod(y + step, NY)

    def chunk_rows(j):
        return row_of(lax.div(j, 2)) * 16 + lax.rem(j, 2) * 8

    def direction(d):
        return (right, -1) if d == 0 else (left, 1)

    def forward(j, step, d, value):
        rs_s[d, j, step] = value.astype(BF16)
        send(
            rs_s.at[d, j, step], rs_r.at[d, j, step],
            rs_ss.at[d, j, step], rs_rs.at[d, j, step], direction(d)[0],
        ).start()

    def w_ready(r):
        for i in range(NZ):
            s = at(row_of(r), near(i), 1 - c)
            arrive(gw.at[s], w_p.at[r, i])

    def reduce(t, carry):
        steps = range(CH + 4)
        gather_at(t, steps, 7, 0)
        for r in range(NY):

            @pl.when(t == 2 * r)
            def _():
                w_ready(r)

        @pl.when(t < CH)
        def _():
            weight = gw[pl.ds(chunk_rows(t), 8)].reshape(CW, HEADS * HD)
            product = lax.dot_general(mixed[...], weight, NT_DIMS, preferred_element_type=F32)
            part[t] = product.reshape(NX, PAGE, CW)
            for d in range(2):
                block = mod(x + direction(d)[1], NX)
                forward(t, 0, d, part[t, block, :, d * DW : d * DW + DW])

        gather_at(t, steps, 7, 1)
        for step in (1, 2):

            @pl.when(jnp.logical_and(t >= step + 1, t < CH + step + 1))
            def _():
                j = t - step - 1
                for d in range(2):
                    arrive(rs_r.at[d, j, step - 1], rs_rs.at[d, j, step - 1])
                    block = lax.rem(x + direction(d)[1] * (1 + step) + 2 * NX, NX)
                    own = part[j, block, :, d * DW : d * DW + DW]
                    forward(j, step, d, rs_r[d, j, step - 1].astype(F32) + own)

            gather_at(t, steps, 7, step + 1)

        @pl.when(t >= 4)
        def _():
            j = t - 4
            for d in range(2):
                arrive(rs_r.at[d, j, 2], rs_rs.at[d, j, 2])
                own = part[j, x, :, d * DW : d * DW + DW]
                cols = pl.ds(pl.multiple_of(chunk_rows(j) * 64 + d * DW, DW), DW)
                hidden = rs_r[d, j, 2].astype(F32) + own + res_s[:, cols].astype(F32)
                norm[:, cols] = (hidden * gain[:, cols]).astype(BF16)
                square = hidden * hidden
                squares[...] += square[:, :HD] + square[:, HD:]

        gather_at(t, steps, 7, 4)
        return carry

    squares[...] = jnp.zeros_like(squares)
    lax.fori_loop(0, CH + 4, reduce, 0)

    scale = lax.rsqrt(jnp.sum(squares[...], axis=-1, keepdims=True) * (1.0 / D) + 1e-05)
    gather(8, 0)
    gather(9, 0)

    def k_ready(i, carry):
        for r in range(NY):
            s = at(row_of(r), near(i), 1 - c)
            arrive(gk.at[s], k_p.at[r, i])
        return carry

    lax.fori_loop(0, NZ, k_ready, 0)
    x_left = mod(x - 1, NX)
    x_right = mod(x + 1, NX)
    x_far = mod(x + 2, NX)

    def tile(n):
        return pl.ds(pl.multiple_of(n * TW, TW), TW)

    def project(n, carry):
        @pl.when(n < NT)
        def _():
            weight = gk[:, :, tile(n)].reshape(D, TW)
            value = jnp.dot(norm[...], weight, preferred_element_type=F32)
            pg[x, :, tile(n)] = (value * scale).astype(BF16)
            own = pg.at[x, :, tile(n)]
            send(own, own, g_s.at[0, n], g_r.at[0, n], right).start()
            send(own, own, g_s.at[1, n], g_r.at[1, n], left).start()

        @pl.when(n >= 2)
        def _():
            j = n - 2
            arrive(pg.at[x_left, :, tile(j)], g_r.at[0, j])
            arrive(pg.at[x_right, :, tile(j)], g_r.at[1, j])
            early = j < 2
            source = jnp.where(early, x_left, x_right)
            target = (me, jnp.where(early, right[1], left[1]))
            page = pg.at[source, :, tile(j)]
            send(page, page, g_f.at[j], g_r.at[2, j], target).start()

        return carry

    lax.fori_loop(0, NT + 2, project, 0)

    def drain_w(i, carry):
        for d in range(2):
            sent(gw.at[0], w_ys.at[d, i])
        sent(gw.at[0], w_fs.at[i])
        for r in range(NY):
            sent(gw.at[0], w_ps.at[r, i])
            sent(gk.at[0], k_ps.at[r, i])
        return carry

    lax.fori_loop(0, NZ, drain_w, 0)
    for n in range(4):
        for d in range(2):
            if n < 3 or d == 1:
                sent(gw.at[0], w_zs.at[d, n])
            for r in range(NY):
                if n < 3 or d == r % 2:
                    sent(gk.at[0], k_zs.at[d, r, n])
    for d in range(2):
        sent(gk.at[0], k_ys.at[d])
        sent(gk.at[0, pl.ds(0, 32)], k_fs.at[d])
    sent(ub_s, s1_s.at[0])
    sent(a_s, s1_s.at[1])
    sent(sf_s, s5_s.at[0])
    for m in range(1, NZ):
        sent(st_s.at[0], s2_s.at[m])
        sent(se_s.at[0], s4_s.at[m])
    for m in range(1, NY):
        sent(sr_s, s3_s.at[m])

    def drain_rs(j, carry):
        for d in range(2):
            for step in range(3):
                sent(rs_s.at[0, 0, 0], rs_ss.at[d, j, step])
        return carry

    lax.fori_loop(0, CH, drain_rs, 0)
    tb[x] = tb_s[...]
    for m in range(1, NX):
        arrive(tb.at[mod(x - m, NX)], t_r.at[m - 1])
        sent(tb_s, t_s.at[m - 1])
    for n in range(NT):
        sent(pg.at[0, :, pl.ds(0, TW)], g_s.at[0, n])
        sent(pg.at[0, :, pl.ds(0, TW)], g_s.at[1, n])
        sent(pg.at[0, :, pl.ds(0, TW)], g_f.at[n])
    for n in range(NT):
        arrive(pg.at[x_far, :, tile(n)], g_r.at[2, n])
    here = [tb[p, 0] == x for p in range(NX)]
    for s in range(2):
        total = jnp.zeros((PAGE, KVW), BF16)
        for p in range(NX):
            hit = jnp.logical_and(here[p], tb[p, 1] == s).astype(F32)
            hit = jnp.broadcast_to(hit[0:1, 0:1], (PAGE, KVW))
            total = jnp.where(hit > 0.5, pg[p], total)
        cache[s] = total


def on_device(query_rows, key_rows, value_rows, log_decay, residual, out_weight, norm_gain, kv_weight, block_table):
    vm, dma = pltpu.VMEM, pltpu.SemaphoreType.DMA
    hbm = pl.BlockSpec(memory_space=pl.ANY)
    vmem = pl.BlockSpec(memory_space=pltpu.VMEM)
    cache = pl.pallas_call(
        kernel,
        out_shape=jax.ShapeDtypeStruct((2, PAGE, KVW), BF16),
        in_specs=[hbm, hbm, hbm, hbm, hbm, vmem, hbm, vmem, vmem],
        out_specs=vmem,
        scratch_shapes=[
            vm((64, 64, HEADS * HD), BF16),
            vm((64, 64, KVW), BF16),
            vm((BLK, HEADS * HD), BF16),
            vm((BLK, HEADS * HD), BF16),
            vm((BLK, HEADS * HD), BF16),
            vm((PAGE, D), BF16),
            vm((HEADS, 1, BLK), F32),
            vm((HEADS, BLK, HD), F32),
            vm((HEADS, 8, HD), F32),
            vm((HEADS, 8, HD), F32),
            vm((HEADS, HD, HD), F32),
            vm((BLK, HEADS * HD), F32),
            vm((BLK, HEADS * HD), BF16),
            vm((4, HD, HD), BF16),
            vm((4, HD, HD), BF16),
            vm((NZ, 80, HD), BF16),
            vm((NZ, 80, HD), BF16),
            vm((80, HD), BF16),
            vm((NY, 80, HD), BF16),
            vm((NZ, 64, HD), BF16),
            vm((NZ, 64, HD), BF16),
            vm((4, HD, HD), BF16),
            vm((4, HD, HD), BF16),
            vm((HEADS, HD, HD), BF16),
            vm((CH, NX, PAGE, CW), F32),
            vm((2, CH, 3, PAGE, DW), BF16),
            vm((2, CH, 3, PAGE, DW), BF16),
            vm((PAGE, HD), F32),
            vm((PAGE, D), BF16),
            vm((NX, PAGE, KVW), BF16),
            vm((NX, 2, 8, HD), jnp.int32),
            vm((2, 8, HD), jnp.int32),
            dma((6,)),
            dma((2, 4)), dma((2, NZ)), dma((NZ,)), dma((NY, NZ)), dma((NY, NZ)), dma((NY, NZ)),
            dma((2, NY, 4)), dma((2,)), dma((2,)), dma((NY, NZ)), dma((NY, NZ)), dma((2,)), dma((NY, NZ)),
            dma((2,)), dma((2,)), dma((NZ,)), dma((NZ,)), dma((NY,)), dma((NY,)),
            dma((NZ,)), dma((NZ,)), dma((1,)), dma((1,)),
            dma((2, CH, 3)), dma((2, CH, 3)), dma((2, NT)), dma((NT,)), dma((3, NT)), dma((3,)), dma((3,)),
        ],
        compiler_params=pltpu.CompilerParams(
            collective_id=0, has_side_effects=True, vmem_limit_bytes=63 * 1024 * 1024
        ),
        name="layer",
    )(
        out_weight.T, kv_weight, query_rows, key_rows, value_rows, log_decay,
        residual, norm_gain.reshape(1, D), block_table,
    )
    return cache.reshape(1, 1, 2, PAGE, KVW)


def solution(mesh):
    placed = (
        P("seq", "pool"),
        P("seq", "pool"),
        P("seq", "pool"),
        P("pool", "seq"),
        P(("seq", "pool"), None),
        P("pool", "seq"),
        P(),
        P("seq", None),
        P(("seq", "pool"), None),
    )
    return jax.shard_map(
        on_device,
        mesh=mesh,
        in_specs=placed,
        out_specs=P("seq", "pool", None, None, None),
        check_vma=False,
    )
```

```python
import jax
import jax.numpy as jnp
from jax import lax
from jax.experimental import pallas as pl
from jax.experimental.pallas import tpu as pltpu
from jax.sharding import PartitionSpec as P

NY, NZ, NX = 4, 8, 4
HEADS = 8
HD = 128
BLK = 512
PAGE = 128
D = 4096
KVW = 1024
CH = 8
CW = D // CH
DW = CW // 2
LAGS = (2, 4, 6)
NT = 4
TW = KVW // NT
F32 = jnp.float32
BF16 = jnp.bfloat16
MESH = pl.DeviceIdType.MESH
FAR_Z = (4, 3, 5, 2, 6, 1, 7)
NT_DIMS = (((1,), (1,)), ((), ()))
TN_DIMS = (((0,), (0,)), ((), ()))

PLAN = {
    (0, 0): ((1, 0, 0, 1), (2, 0, 0, 2), (3, 0, 1, 0), (4, 0, 2, 0),),
    (1, 0): ((3, 1, 1, 0), (4, 1, 2, 0),),
    (2, 2, 2): ((0, 0, 0, 1), (0, 0, 0, 2), (0, 0, 1, 0), (0, 0, 2, 0), (2, 0, 0, 4), (3, 0, 1, 1), (4, 0, 2, 1),),
    (2, 5, 0): ((1, 0, 0, 3), (3, 0, 1, 2), (4, 0, 2, 2), (0, 1, 1, 0), (0, 1, 2, 0),),
    (2, 5, 1): ((4, 2, 2, 0),),
    (2, 5, 2): ((0, 0, 1, 1), (0, 0, 2, 1), (3, 2, 1, 0),),
    (2, 6, 2): ((0, 0, 0, 4), (2, 0, 0, 6), (4, 0, 2, 4),),
    (2, 7, 0): ((3, 0, 1, 4), (0, 0, 0, 3), (1, 0, 0, 5), (0, 0, 1, 2), (0, 0, 2, 2),),
    (2, 7, 1): ((4, 0, 2, 3),),
    (2, 7, 2): ((3, 0, 1, 3),),
    (4, 0): ((2, 1, 1, 2), (0, 1, 3, 0), (4, 0, 3, 1), (0, 0, 0, 6), (0, 0, 2, 4), (3, 0, 1, 6), (1, 1, 1, 1), (2, 0, 0, 7), (0, 0, 0, 5), (0, 0, 1, 4), (4, 0, 2, 5), (0, 0, 2, 3), (3, 0, 1, 5), (1, 1, 0, 1), (2, 1, 0, 2),),
    (4, 1): ((0, 0, 1, 3),),
    (5, 0): ((0, 1, 1, 2), (4, 0, 2, 6),),
    (6, 0): ((0, 0, 0, 7), (0, 0, 3, 1), (0, 0, 1, 6), (0, 1, 1, 1), (3, 0, 1, 7), (1, 1, 2, 1), (2, 1, 2, 2),),
    (7, 0, 0): ((4, 0, 2, 7),),
    (7, 0, 1): ((0, 0, 2, 5), (3, 0, 3, 0), (1, 1, 3, 1), (2, 1, 3, 2),),
    (7, 1, 1): ((0, 0, 1, 5), (0, 1, 0, 1), (0, 1, 0, 2),),
    (7, 2, 0): ((4, 0, 3, 3), (0, 0, 2, 6), (3, 0, 3, 2), (1, 1, 0, 3), (2, 1, 1, 4), (0, 0, 1, 7), (0, 1, 2, 1), (0, 1, 2, 2), (4, 0, 3, 5),),
    (7, 2, 1): ((0, 0, 2, 7), (3, 0, 3, 4), (1, 1, 2, 3), (2, 1, 2, 4),),
    (7, 3, 1): ((0, 0, 3, 0), (0, 1, 3, 1), (0, 1, 3, 2), (4, 0, 3, 7),),
    (7, 4, 1): ((0, 0, 3, 3), (3, 0, 3, 6), (1, 1, 3, 3), (2, 1, 3, 4),),
    (7, 4, 2): ((0, 0, 3, 2), (0, 1, 0, 3), (0, 1, 1, 4),),
    (7, 5, 1): ((0, 0, 3, 5), (1, 1, 0, 5), (2, 1, 1, 6),),
    (7, 5, 2): ((0, 0, 3, 4), (0, 1, 2, 3), (0, 1, 2, 4),),
    (7, 6, 0): ((0, 0, 3, 7), (1, 1, 2, 5), (2, 1, 2, 6), (0, 0, 3, 6), (0, 1, 3, 3), (0, 1, 3, 4),),
    (7, 6, 2): ((1, 1, 3, 5), (2, 1, 3, 6),),
    (7, 7, 1): ((0, 1, 0, 5), (0, 1, 1, 6),),
    (7, 7, 2): ((1, 1, 0, 7), (2, 1, 1, 7),),
    (7, 7, 3): ((0, 1, 2, 5), (0, 1, 2, 6),),
    (7, 8, 0): ((1, 1, 2, 7), (2, 1, 0, 4),),
    (7, 8, 2): ((0, 1, 3, 5), (0, 1, 3, 6),),
    (7, 8, 3): ((1, 1, 1, 3), (2, 1, 3, 7),),
    (7, 9, 0): ((0, 1, 0, 7), (0, 1, 1, 7),),
    (7, 9, 3): ((0, 1, 2, 7), (0, 1, 0, 4), (2, 1, 0, 6),),
    (7, 10, 3): ((0, 1, 1, 3), (0, 1, 3, 7), (1, 1, 1, 5),),
    (7, 11, 3): ((0, 1, 0, 6),),
    (7, 13, 0): ((0, 1, 1, 5),),
}


def kernel(
    wt, kw, q_hbm, k_hbm, v_hbm, ld, res_hbm, gain, tbl,
    cache,
    gw, gk, q_s, k_s, v_s, res_s, crow, ccol, a_s, a_r, u_s, inner, mixed,
    ub_s, ub_r, st_s, st_r, sr_s, sr_r, se_s, se_r, sf_s, sf_r, state,
    part, rs_s, rs_r, squares, norm, pg, tb, tb_s,
    ld_sem, w_zs, w_ys, w_fs, w_ps, w_r, w_p,
    k_zs, k_ys, k_fs, k_ps, k_r, k_h, k_p,
    s1_s, s1_r, s2_s, s2_r, s3_s, s3_r, s4_s, s4_r, s5_s, s5_r,
    rs_ss, rs_rs, g_s, g_f, g_r, t_s, t_r,
):
    me = lax.axis_index("seq")
    x = lax.axis_index("pool")
    y = lax.div(me, 16)
    z = lax.rem(lax.div(me, 2), 8)
    c = lax.rem(me, 2)

    def at(yy, zz, cc):
        return (yy * NZ + zz) * 2 + cc

    def mod(value, size):
        return lax.rem(value + size, size)

    up = (at(mod(y + 1, NY), z, c), x)
    down = (at(mod(y - 1, NY), z, c), x)
    ahead = (at(y, mod(z + 1, NZ), c), x)
    behind = (at(y, mod(z - 1, NZ), c), x)
    partner = (at(y, z, 1 - c), x)
    right = (me, mod(x + 1, NX))
    left = (me, mod(x - 1, NX))

    def send(src, dst, ssem, rsem, device):
        copy = pltpu.make_async_remote_copy(
            src_ref=src, dst_ref=dst, send_sem=ssem, recv_sem=rsem,
            device_id=device, device_id_type=MESH,
        )
        return copy

    def arrive(ref, rsem):
        send(ref, ref, rsem, rsem, partner).wait_recv()

    def sent(ref, ssem):
        send(ref, ref, ssem, ssem, partner).wait_send()

    peers = [partner]
    peers += [(at(y, mod(z + m, NZ), c), x) for m in range(1, NZ)]
    peers += [(at(mod(y + m, NY), z, c), x) for m in range(1, NY)]
    peers += [(me, mod(x + m, NX)) for m in range(1, NX)]
    barrier = pltpu.get_barrier_semaphore()
    for peer in peers:
        pl.semaphore_signal(barrier, inc=1, device_id=peer, device_id_type=MESH)
    loads = [
        pltpu.make_async_copy(k_hbm, k_s, ld_sem.at[0]),
        pltpu.make_async_copy(v_hbm, v_s, ld_sem.at[1]),
        pltpu.make_async_copy(q_hbm, q_s, ld_sem.at[2]),
        pltpu.make_async_copy(res_hbm, res_s, ld_sem.at[3]),
        pltpu.make_async_copy(wt, gw.at[me], ld_sem.at[4]),
        pltpu.make_async_copy(kw, gk.at[me], ld_sem.at[5]),
    ]
    for load in loads:
        load.start()
    steps_a = lax.broadcasted_iota(jnp.int32, (BLK, BLK), 0)
    steps_b = lax.broadcasted_iota(jnp.int32, (BLK, BLK), 1)
    lower = jnp.where(steps_b <= steps_a, 1.0, 0.0).astype(BF16)
    rest = ld[...]
    sums_row = jnp.zeros((HEADS, BLK), F32)
    sums_col = jnp.zeros((BLK, HEADS), F32)
    for _ in range(3):
        piece = rest.astype(BF16)
        rest = rest - piece.astype(F32)
        sums_row += lax.dot_general(piece, lower, NT_DIMS, preferred_element_type=F32)
        sums_col += lax.dot_general(lower, piece, NT_DIMS, preferred_element_type=F32)
    for h in range(HEADS):
        crow[h] = sums_row[h : h + 1, :]
        wide = jnp.broadcast_to(sums_col[:, h : h + 1], (BLK, HD))
        ccol[h] = wide
        a_s[h] = jnp.broadcast_to(wide[BLK - 1 : BLK, :], (8, HD))

    pl.semaphore_wait(barrier, len(peers))

    def near(i):
        half = lax.div(i + 1, 2)
        return mod(z + half * (1 - 2 * lax.rem(i, 2)), NZ)

    row_step = (0, 3, 1, 2)

    def slot(r, i):
        return at(mod(y + row_step[r], NY), near(i), c)

    lines = (None, ahead, behind, up, down)

    def take(kind, r, i):
        if kind == 0:
            s = slot(r, i)
            arrive(gw.at[s], w_r.at[r, i])
            send(gw.at[s], gw.at[s], w_ps.at[r, i], w_p.at[r, i], partner).start()
            return
        s = slot(r, i)
        if r == 3 and i == 0:
            arrive(gk.at[s, pl.ds(0, 32)], k_h.at[0])
            arrive(gk.at[s, pl.ds(32, 32)], k_h.at[1])
        else:
            arrive(gk.at[s], k_r.at[r, i])
        send(gk.at[s], gk.at[s], k_ps.at[r, i], k_p.at[r, i], partner).start()

    def along(i, link):
        back = 0 if i <= 2 else (6 if i == 7 and link == 2 else i - 2)
        index = (i - 1) // 2 if link == 1 else (3 if i == 7 else i // 2 - 1)
        return back, index

    def pass_on(link, kind, r, i):
        target = lines[link]
        if kind == 2:
            s = slot(r, 0)
            rows = gk.at[s, pl.ds(32 * (r - 1), 32)]
            send(rows, rows, k_fs.at[r - 1], k_h.at[r - 1], target).start()
            return
        whole, mine = (gw, wt) if kind == 0 else (gk, kw)
        if link <= 2:
            back, index = along(i, link)
            source = (r, back)
            ssem = w_zs.at[link - 1, index] if kind == 0 else k_zs.at[link - 1, r, index]
        elif kind == 1:
            source, ssem = (0, 0), k_ys.at[link - 3]
        elif r == 3:
            source, ssem = (1 if link == 3 else 2, i), w_fs.at[i]
        else:
            source, ssem = (0, i), w_ys.at[link - 3, i]
        s = slot(*source)
        src = mine if source == (0, 0) else whole.at[s]
        rsem = w_r.at[r, i] if kind == 0 else k_r.at[r, i]
        send(src, whole.at[s], ssem, rsem, target).start()

    def gather(*place):
        for what, kind, r, i in PLAN.get(place, ()):
            if what == 0:
                take(kind, r, i)
            else:
                pass_on(what, kind, r, i)

    def gather_at(step, steps, group, part):
        for n in steps:
            if (group, n, part) in PLAN:

                @pl.when(step == n)
                def _():
                    gather(group, n, part)

    send(wt, gw.at[me], w_ps.at[0, 0], w_p.at[0, 0], partner).start()
    send(kw, gk.at[me], k_ps.at[0, 0], k_p.at[0, 0], partner).start()
    gather(0, 0)
    for n in range(2):
        tb_s[n] = jnp.broadcast_to(tbl[0:1, n : n + 1], (8, HD))
    for m in range(1, NX):
        target = (me, mod(x + m, NX))
        send(tb_s, tb.at[x], t_s.at[m - 1], t_r.at[m - 1], target).start()

    def head_cols(h):
        return pl.ds(pl.multiple_of(h * HD, HD), HD)

    loads[0].wait()
    loads[1].wait()

    def update(h, carry):
        cb = ccol[h]
        gap = jnp.exp(cb[BLK - 1 : BLK, :] - cb)
        weighted = (k_s[:, head_cols(h)].astype(F32) * gap).astype(BF16)
        u_s[h] = lax.dot_general(
            weighted, v_s[:, head_cols(h)], TN_DIMS, preferred_element_type=F32
        )
        return carry

    lax.fori_loop(0, HEADS, update, 0)
    gather(1, 0)
    ub_s[...] = u_s[pl.ds(4 * (1 - c), 4)].astype(BF16)
    send(ub_s, ub_r, s1_s.at[0], s1_r.at[0], partner).start()
    send(a_s, a_r, s1_s.at[1], s1_r.at[1], partner).start()

    def chip_parts():
        own = u_s[pl.ds(4 * c, 4)]
        other = ub_r[...].astype(F32)
        a_own = a_s[pl.ds(4 * c, 4)]
        a_other = a_r[pl.ds(4 * c, 4)]
        first = c == 0
        return (
            jnp.where(first, own, other),
            jnp.where(first, other, own),
            jnp.where(first, a_own, a_other),
            jnp.where(first, a_other, a_own),
        )

    def split(row):
        a = jnp.broadcast_to(row, (16, HD))
        rows = lax.broadcasted_iota(jnp.int32, (16, HD), 0)
        hi = a.astype(BF16).astype(F32)
        mid = (a - hi).astype(BF16).astype(F32)
        low = a - hi - mid
        tile = jnp.where(rows == 0, hi, jnp.where(rows == 1, mid, jnp.where(rows == 2, low, 0.0)))
        return tile.astype(BF16)

    def joined(message):
        value = message.astype(F32)
        return value[0:64, :], jnp.sum(value[64:80, :], axis=0, keepdims=True)

    def scan_chip():
        arrive(ub_r, s1_r.at[0])
        arrive(a_r, s1_r.at[1])
        u0, u1, a0, a1 = chip_parts()
        total = jnp.exp(a1)[:, 0:1, :] * u0 + u1
        a_chip = a0 + a1
        for hl in range(4):
            tile = split(a_chip[hl, 0:1, :])
            for half in range(2):
                st_s[2 * hl + half, 0:64, :] = total[hl, 64 * half : 64 * half + 64, :].astype(BF16)
                st_s[2 * hl + half, 64:80, :] = tile
        st_r[z] = st_s[z]
        for m in FAR_Z:
            zz = mod(z + m, NZ)
            send(st_s.at[zz], st_r.at[z], s2_s.at[m], s2_r.at[m], (at(y, zz, c), x)).start()

    def chip_total(zz):
        return joined(st_r[zz])

    def scan_row():
        for m in range(1, NZ):
            arrive(st_r.at[mod(z - m, NZ)], s2_r.at[m])
        total = jnp.zeros((64, HD), F32)
        a_row = jnp.zeros((1, HD), F32)
        for zz in range(NZ):
            t, a = chip_total(zz)
            total = jnp.exp(a) * total + t
            a_row = a_row + a
        sr_s[0:64, :] = total.astype(BF16)
        sr_s[64:80, :] = split(a_row)
        sr_r[y] = sr_s[...]
        for m in (2, 1, 3):
            target = (at(mod(y + m, NY), z, c), x)
            send(sr_s, sr_r.at[y], s3_s.at[m], s3_r.at[m], target).start()

    def scan_back():
        for m in range(1, NY):
            arrive(sr_r.at[mod(y - m, NY)], s3_r.at[m])
        enter = jnp.zeros((64, HD), F32)
        for yy in range(NY):
            t, a = joined(sr_r[yy])
            moved = jnp.exp(a) * enter + t
            enter = jnp.where(yy < y, moved, enter)
        for zz in range(NZ):
            se_s[zz] = enter.astype(BF16)
            t, a = chip_total(zz)
            enter = jnp.exp(a) * enter + t
        se_r[z] = se_s[z]
        for m in FAR_Z:
            zz = mod(z + m, NZ)
            send(se_s.at[zz], se_r.at[z], s4_s.at[m], s4_r.at[m], (at(y, zz, c), x)).start()

    def scan_cores():
        for m in range(1, NZ):
            arrive(se_r.at[mod(z - m, NZ)], s4_r.at[m])
        enter = se_r[...].reshape(4, HD, HD).astype(F32)
        u0, _, a0, _ = chip_parts()
        after = jnp.exp(a0)[:, 0:1, :] * enter + u0
        first = c == 0
        sf_s[...] = jnp.where(first, after, enter).astype(BF16)
        send(sf_s, sf_r, s5_s.at[0], s5_r.at[0], partner).start()
        state[pl.ds(4 * c, 4)] = jnp.where(first, enter, after).astype(BF16)

    loads[2].wait()
    loads[4].wait()
    loads[5].wait()

    tri_a = lax.broadcasted_iota(jnp.int32, (HD, HD), 0)
    tri_b = lax.broadcasted_iota(jnp.int32, (HD, HD), 1)
    seen = tri_b <= tri_a

    def within(h, carry):
        gather_at(h, range(HEADS), 2, 0)

        @pl.when(h == 1)
        def _():
            scan_chip()

        @pl.when(h == 5)
        def _():
            scan_row()

        @pl.when(h == 7)
        def _():
            scan_back()

        gather_at(h, range(HEADS), 2, 1)

        for tq in range(4):
            rows = pl.ds(tq * HD, HD)
            width = HD * (tq + 1)
            products = lax.dot_general(
                q_s[rows, head_cols(h)], k_s[0:width, head_cols(h)], NT_DIMS,
                preferred_element_type=F32,
            )
            c_here = ccol[h, rows, :]
            blocks = []
            for ts in range(tq + 1):
                gap = c_here - crow[h, :, ts * HD : ts * HD + HD]
                piece = products[:, ts * HD : ts * HD + HD]
                if ts == tq:
                    gap = jnp.where(seen, gap, 0.0)
                    piece = jnp.where(seen, piece, 0.0)
                blocks.append((piece * jnp.exp(gap)).astype(BF16))
            scores = jnp.concatenate(blocks, axis=1) if tq else blocks[0]
            inner[rows, head_cols(h)] = jnp.dot(
                scores, v_s[0:width, head_cols(h)], preferred_element_type=F32
            )

        ccol[h] = jnp.exp(ccol[h])
        gather_at(h, range(HEADS), 2, 2)
        return carry

    lax.fori_loop(0, HEADS, within, 0)
    gather(4, 0)
    scan_cores()
    gather(4, 1)
    gather(5, 0)
    arrive(sf_r, s5_r.at[0])
    gather(5, 1)
    state[pl.ds(4 * (1 - c), 4)] = sf_r[...]

    def finish(h, carry):
        outer = jnp.dot(q_s[:, head_cols(h)], state[h], preferred_element_type=F32)
        kept = inner[:, head_cols(h)] + outer * ccol[h]
        scale = lax.rsqrt(jnp.mean(kept * kept, axis=-1, keepdims=True) + 1e-05)
        mixed[:, head_cols(h)] = (kept * scale).astype(BF16)
        return carry

    lax.fori_loop(0, HEADS, finish, 0)
    loads[3].wait()
    gather(6, 0)

    def row_of(r):
        step = jnp.where(r == 1, 3, jnp.where(r == 2, 1, jnp.where(r == 3, 2, 0)))
        return mod(y + step, NY)

    def chunk_rows(j):
        return row_of(lax.div(j, 2)) * 16 + lax.rem(j, 2) * 8

    def direction(d):
        return (right, -1) if d == 0 else (left, 1)

    def forward(j, step, d, value):
        rs_s[d, j, step] = value.astype(BF16)
        send(
            rs_s.at[d, j, step], rs_r.at[d, j, step],
            rs_ss.at[d, j, step], rs_rs.at[d, j, step], direction(d)[0],
        ).start()

    def w_ready(r):
        for i in range(NZ):
            s = at(row_of(r), near(i), 1 - c)
            arrive(gw.at[s], w_p.at[r, i])

    def reduce(t, carry):
        steps = range(CH + LAGS[2])
        gather_at(t, steps, 7, 0)
        for r in range(NY):

            @pl.when(t == 2 * r)
            def _():
                w_ready(r)

        @pl.when(t < CH)
        def _():
            weight = gw[pl.ds(chunk_rows(t), 8)].reshape(CW, HEADS * HD)
            product = lax.dot_general(mixed[...], weight, NT_DIMS, preferred_element_type=F32)
            part[t] = product.reshape(NX, PAGE, CW)
            for d in range(2):
                block = mod(x + direction(d)[1], NX)
                forward(t, 0, d, part[t, block, :, d * DW : d * DW + DW])

        gather_at(t, steps, 7, 1)
        for step in (1, 2):

            lag = LAGS[step - 1]

            @pl.when(jnp.logical_and(t >= lag, t < CH + lag))
            def _():
                j = t - lag
                for d in range(2):
                    arrive(rs_r.at[d, j, step - 1], rs_rs.at[d, j, step - 1])
                    block = lax.rem(x + direction(d)[1] * (1 + step) + 2 * NX, NX)
                    own = part[j, block, :, d * DW : d * DW + DW]
                    forward(j, step, d, rs_r[d, j, step - 1].astype(F32) + own)

            gather_at(t, steps, 7, step + 1)

        @pl.when(t >= LAGS[2])
        def _():
            j = t - LAGS[2]
            for d in range(2):
                arrive(rs_r.at[d, j, 2], rs_rs.at[d, j, 2])
                own = part[j, x, :, d * DW : d * DW + DW]
                cols = pl.ds(pl.multiple_of(chunk_rows(j) * 64 + d * DW, DW), DW)
                hidden = rs_r[d, j, 2].astype(F32) + own + res_s[:, cols].astype(F32)
                norm[:, cols] = (hidden * gain[:, cols]).astype(BF16)
                square = hidden * hidden
                squares[...] += square[:, :HD] + square[:, HD:]

        gather_at(t, steps, 7, 4)
        return carry

    squares[...] = jnp.zeros_like(squares)
    lax.fori_loop(0, CH + LAGS[2], reduce, 0)

    scale = lax.rsqrt(jnp.sum(squares[...], axis=-1, keepdims=True) * (1.0 / D) + 1e-05)
    gather(8, 0)
    gather(9, 0)

    def k_ready(i, carry):
        for r in range(NY):
            s = at(row_of(r), near(i), 1 - c)
            arrive(gk.at[s], k_p.at[r, i])
        return carry

    lax.fori_loop(0, NZ, k_ready, 0)
    x_left = mod(x - 1, NX)
    x_right = mod(x + 1, NX)
    x_far = mod(x + 2, NX)

    def tile(n):
        return pl.ds(pl.multiple_of(n * TW, TW), TW)

    def project(n, carry):
        @pl.when(n < NT)
        def _():
            weight = gk[:, :, tile(n)].reshape(D, TW)
            value = jnp.dot(norm[...], weight, preferred_element_type=F32)
            pg[x, :, tile(n)] = (value * scale).astype(BF16)
            own = pg.at[x, :, tile(n)]
            send(own, own, g_s.at[0, n], g_r.at[0, n], right).start()
            send(own, own, g_s.at[1, n], g_r.at[1, n], left).start()

        @pl.when(n >= 2)
        def _():
            j = n - 2
            arrive(pg.at[x_left, :, tile(j)], g_r.at[0, j])
            arrive(pg.at[x_right, :, tile(j)], g_r.at[1, j])
            early = j < 2
            source = jnp.where(early, x_left, x_right)
            target = (me, jnp.where(early, right[1], left[1]))
            page = pg.at[source, :, tile(j)]
            send(page, page, g_f.at[j], g_r.at[2, j], target).start()

        return carry

    lax.fori_loop(0, NT + 2, project, 0)

    def drain_w(i, carry):
        for d in range(2):
            sent(gw.at[0], w_ys.at[d, i])
        sent(gw.at[0], w_fs.at[i])
        for r in range(NY):
            sent(gw.at[0], w_ps.at[r, i])
            sent(gk.at[0], k_ps.at[r, i])
        return carry

    lax.fori_loop(0, NZ, drain_w, 0)
    for n in range(4):
        for d in range(2):
            if n < 3 or d == 1:
                sent(gw.at[0], w_zs.at[d, n])
            for r in range(NY):
                if n < 3 or d == r % 2:
                    sent(gk.at[0], k_zs.at[d, r, n])
    for d in range(2):
        sent(gk.at[0], k_ys.at[d])
        sent(gk.at[0, pl.ds(0, 32)], k_fs.at[d])
    sent(ub_s, s1_s.at[0])
    sent(a_s, s1_s.at[1])
    sent(sf_s, s5_s.at[0])
    for m in range(1, NZ):
        sent(st_s.at[0], s2_s.at[m])
        sent(se_s.at[0], s4_s.at[m])
    for m in range(1, NY):
        sent(sr_s, s3_s.at[m])

    def drain_rs(j, carry):
        for d in range(2):
            for step in range(3):
                sent(rs_s.at[0, 0, 0], rs_ss.at[d, j, step])
        return carry

    lax.fori_loop(0, CH, drain_rs, 0)
    tb[x] = tb_s[...]
    for m in range(1, NX):
        arrive(tb.at[mod(x - m, NX)], t_r.at[m - 1])
        sent(tb_s, t_s.at[m - 1])
    for n in range(NT):
        sent(pg.at[0, :, pl.ds(0, TW)], g_s.at[0, n])
        sent(pg.at[0, :, pl.ds(0, TW)], g_s.at[1, n])
        sent(pg.at[0, :, pl.ds(0, TW)], g_f.at[n])
    for n in range(NT):
        arrive(pg.at[x_far, :, tile(n)], g_r.at[2, n])
    here = [tb[p, 0] == x for p in range(NX)]
    for s in range(2):
        total = jnp.zeros((PAGE, KVW), BF16)
        for p in range(NX):
            hit = jnp.logical_and(here[p], tb[p, 1] == s).astype(F32)
            hit = jnp.broadcast_to(hit[0:1, 0:1], (PAGE, KVW))
            total = jnp.where(hit > 0.5, pg[p], total)
        cache[s] = total


def on_device(query_rows, key_rows, value_rows, log_decay, residual, out_weight, norm_gain, kv_weight, block_table):
    vm, dma = pltpu.VMEM, pltpu.SemaphoreType.DMA
    hbm = pl.BlockSpec(memory_space=pl.ANY)
    vmem = pl.BlockSpec(memory_space=pltpu.VMEM)
    cache = pl.pallas_call(
        kernel,
        out_shape=jax.ShapeDtypeStruct((2, PAGE, KVW), BF16),
        in_specs=[hbm, hbm, hbm, hbm, hbm, vmem, hbm, vmem, vmem],
        out_specs=vmem,
        scratch_shapes=[
            vm((64, 64, HEADS * HD), BF16),
            vm((64, 64, KVW), BF16),
            vm((BLK, HEADS * HD), BF16),
            vm((BLK, HEADS * HD), BF16),
            vm((BLK, HEADS * HD), BF16),
            vm((PAGE, D), BF16),
            vm((HEADS, 1, BLK), F32),
            vm((HEADS, BLK, HD), F32),
            vm((HEADS, 8, HD), F32),
            vm((HEADS, 8, HD), F32),
            vm((HEADS, HD, HD), F32),
            vm((BLK, HEADS * HD), F32),
            vm((BLK, HEADS * HD), BF16),
            vm((4, HD, HD), BF16),
            vm((4, HD, HD), BF16),
            vm((NZ, 80, HD), BF16),
            vm((NZ, 80, HD), BF16),
            vm((80, HD), BF16),
            vm((NY, 80, HD), BF16),
            vm((NZ, 64, HD), BF16),
            vm((NZ, 64, HD), BF16),
            vm((4, HD, HD), BF16),
            vm((4, HD, HD), BF16),
            vm((HEADS, HD, HD), BF16),
            vm((CH, NX, PAGE, CW), F32),
            vm((2, CH, 3, PAGE, DW), BF16),
            vm((2, CH, 3, PAGE, DW), BF16),
            vm((PAGE, HD), F32),
            vm((PAGE, D), BF16),
            vm((NX, PAGE, KVW), BF16),
            vm((NX, 2, 8, HD), jnp.int32),
            vm((2, 8, HD), jnp.int32),
            dma((6,)),
            dma((2, 4)), dma((2, NZ)), dma((NZ,)), dma((NY, NZ)), dma((NY, NZ)), dma((NY, NZ)),
            dma((2, NY, 4)), dma((2,)), dma((2,)), dma((NY, NZ)), dma((NY, NZ)), dma((2,)), dma((NY, NZ)),
            dma((2,)), dma((2,)), dma((NZ,)), dma((NZ,)), dma((NY,)), dma((NY,)),
            dma((NZ,)), dma((NZ,)), dma((1,)), dma((1,)),
            dma((2, CH, 3)), dma((2, CH, 3)), dma((2, NT)), dma((NT,)), dma((3, NT)), dma((3,)), dma((3,)),
        ],
        compiler_params=pltpu.CompilerParams(
            collective_id=0, has_side_effects=True, vmem_limit_bytes=63 * 1024 * 1024
        ),
        name="layer",
    )(
        out_weight.T, kv_weight, query_rows, key_rows, value_rows, log_decay,
        residual, norm_gain.reshape(1, D), block_table,
    )
    return cache.reshape(1, 1, 2, PAGE, KVW)


def solution(mesh):
    placed = (
        P("seq", "pool"),
        P("seq", "pool"),
        P("seq", "pool"),
        P("pool", "seq"),
        P(("seq", "pool"), None),
        P("pool", "seq"),
        P(),
        P("seq", None),
        P(("seq", "pool"), None),
    )
    return jax.shard_map(
        on_device,
        mesh=mesh,
        in_specs=placed,
        out_specs=P("seq", "pool", None, None, None),
        check_vma=False,
    )
```

```python
import jax
import jax.numpy as jnp
from jax import lax
from jax.experimental import pallas as pl
from jax.experimental.pallas import tpu as pltpu
from jax.sharding import PartitionSpec as P

NY, NZ, NX = 4, 8, 4
HEADS = 8
HD = 128
BLK = 512
PAGE = 128
D = 4096
KVW = 1024
CH = 8
CW = D // CH
DW = CW // 2
LAGS = (2, 4, 6)
NT = 4
TW = KVW // NT
F32 = jnp.float32
BF16 = jnp.bfloat16
MESH = pl.DeviceIdType.MESH
FAR_Z = (4, 3, 5, 2, 6, 1, 7)
NT_DIMS = (((1,), (1,)), ((), ()))
TN_DIMS = (((0,), (0,)), ((), ()))

PLAN = {
    (0, 0): ((1, 0, 0, 1), (2, 0, 0, 2), (3, 0, 1, 0), (4, 0, 2, 0),),
    (1, 0): ((3, 1, 1, 0), (4, 1, 2, 0),),
    (2, 2, 2): ((0, 0, 0, 1), (0, 0, 0, 2), (0, 0, 1, 0), (0, 0, 2, 0), (2, 0, 0, 4), (3, 0, 1, 1), (4, 0, 2, 1),),
    (2, 5, 0): ((1, 0, 0, 3), (3, 0, 1, 2), (4, 0, 2, 2), (0, 1, 1, 0), (0, 1, 2, 0),),
    (2, 5, 1): ((4, 2, 2, 0),),
    (2, 5, 2): ((0, 0, 1, 1), (0, 0, 2, 1), (3, 2, 1, 0),),
    (2, 6, 2): ((0, 0, 0, 4), (2, 0, 0, 6), (4, 0, 2, 4),),
    (2, 7, 0): ((3, 0, 1, 4), (0, 0, 0, 3), (1, 0, 0, 5), (0, 0, 1, 2), (0, 0, 2, 2),),
    (2, 7, 1): ((4, 0, 2, 3),),
    (2, 7, 2): ((3, 0, 1, 3),),
    (4, 0): ((2, 1, 1, 2), (0, 1, 3, 0), (4, 0, 3, 1), (0, 0, 0, 6), (0, 0, 2, 4), (3, 0, 1, 6), (1, 1, 1, 1), (2, 0, 0, 7), (0, 0, 0, 5), (0, 0, 1, 4), (4, 0, 2, 5), (0, 0, 2, 3), (3, 0, 1, 5), (1, 1, 0, 1), (2, 1, 0, 2),),
    (4, 1): ((0, 0, 1, 3),),
    (5, 0): ((0, 1, 1, 2), (4, 0, 2, 6),),
    (6, 0): ((0, 0, 0, 7), (0, 0, 3, 1), (0, 0, 1, 6), (0, 1, 1, 1), (3, 0, 1, 7), (1, 1, 2, 1), (2, 1, 2, 2),),
    (7, 0, 0): ((4, 0, 2, 7),),
    (7, 0, 1): ((0, 0, 2, 5), (3, 0, 3, 0), (1, 1, 3, 1), (2, 1, 3, 2),),
    (7, 1, 1): ((0, 0, 1, 5), (0, 1, 0, 1), (0, 1, 0, 2),),
    (7, 2, 0): ((4, 0, 3, 3), (0, 0, 2, 6), (3, 0, 3, 2), (1, 1, 0, 3), (2, 1, 1, 4), (0, 0, 1, 7), (0, 1, 2, 1), (0, 1, 2, 2), (4, 0, 3, 5),),
    (7, 2, 1): ((0, 0, 2, 7), (3, 0, 3, 4), (1, 1, 2, 3), (2, 1, 2, 4),),
    (7, 3, 1): ((0, 0, 3, 0), (0, 1, 3, 1), (0, 1, 3, 2), (4, 0, 3, 7),),
    (7, 4, 1): ((0, 0, 3, 3), (3, 0, 3, 6), (1, 1, 3, 3), (2, 1, 3, 4),),
    (7, 4, 2): ((0, 0, 3, 2), (0, 1, 0, 3), (0, 1, 1, 4),),
    (7, 5, 1): ((0, 0, 3, 5), (1, 1, 0, 5), (2, 1, 1, 6),),
    (7, 5, 2): ((0, 0, 3, 4), (0, 1, 2, 3), (0, 1, 2, 4),),
    (7, 6, 0): ((0, 0, 3, 7), (1, 1, 2, 5), (2, 1, 2, 6), (0, 0, 3, 6), (0, 1, 3, 3), (0, 1, 3, 4),),
    (7, 6, 2): ((1, 1, 3, 5), (2, 1, 3, 6),),
    (7, 7, 1): ((0, 1, 0, 5), (0, 1, 1, 6),),
    (7, 7, 2): ((1, 1, 0, 7), (2, 1, 1, 7),),
    (7, 7, 3): ((0, 1, 2, 5), (0, 1, 2, 6),),
    (7, 8, 0): ((1, 1, 2, 7), (2, 1, 0, 4),),
    (7, 8, 2): ((0, 1, 3, 5), (0, 1, 3, 6),),
    (7, 8, 3): ((1, 1, 1, 3), (2, 1, 3, 7),),
    (7, 9, 0): ((0, 1, 0, 7), (0, 1, 1, 7),),
    (7, 9, 3): ((0, 1, 2, 7), (0, 1, 0, 4), (2, 1, 0, 6),),
    (7, 10, 3): ((0, 1, 1, 3), (0, 1, 3, 7), (1, 1, 1, 5),),
    (7, 11, 3): ((0, 1, 0, 6),),
    (7, 13, 0): ((0, 1, 1, 5),),
}


def kernel(
    wt, kw, q_hbm, k_hbm, v_hbm, ld, res_hbm, gain, tbl,
    cache,
    gw, gk, q_s, k_s, v_s, res_s, crow, ccol, a_s, a_r, u_s, inner, mixed,
    ub_s, ub_r, st_s, st_r, sr_s, sr_r, se_s, se_r, sf_s, sf_r, state,
    part, rs_s, rs_r, squares, norm, pg, tb, tb_s,
    ld_sem, w_zs, w_ys, w_fs, w_ps, w_r, w_p,
    k_zs, k_ys, k_fs, k_ps, k_r, k_h, k_p,
    s1_s, s1_r, s2_s, s2_r, s3_s, s3_r, s4_s, s4_r, s5_s, s5_r,
    rs_ss, rs_rs, g_s, g_f, g_r, t_s, t_r,
):
    me = lax.axis_index("seq")
    x = lax.axis_index("pool")
    y = lax.div(me, 16)
    z = lax.rem(lax.div(me, 2), 8)
    c = lax.rem(me, 2)

    def at(yy, zz, cc):
        return (yy * NZ + zz) * 2 + cc

    def mod(value, size):
        return lax.rem(value + size, size)

    up = (at(mod(y + 1, NY), z, c), x)
    down = (at(mod(y - 1, NY), z, c), x)
    ahead = (at(y, mod(z + 1, NZ), c), x)
    behind = (at(y, mod(z - 1, NZ), c), x)
    partner = (at(y, z, 1 - c), x)
    right = (me, mod(x + 1, NX))
    left = (me, mod(x - 1, NX))

    def send(src, dst, ssem, rsem, device):
        copy = pltpu.make_async_remote_copy(
            src_ref=src, dst_ref=dst, send_sem=ssem, recv_sem=rsem,
            device_id=device, device_id_type=MESH,
        )
        return copy

    def arrive(ref, rsem):
        send(ref, ref, rsem, rsem, partner).wait_recv()

    def sent(ref, ssem):
        send(ref, ref, ssem, ssem, partner).wait_send()

    peers = [partner]
    peers += [(at(y, mod(z + m, NZ), c), x) for m in range(1, NZ)]
    peers += [(at(mod(y + m, NY), z, c), x) for m in range(1, NY)]
    peers += [(me, mod(x + m, NX)) for m in range(1, NX)]
    barrier = pltpu.get_barrier_semaphore()
    for peer in peers:
        pl.semaphore_signal(barrier, inc=1, device_id=peer, device_id_type=MESH)
    loads = [
        pltpu.make_async_copy(k_hbm, k_s, ld_sem.at[0]),
        pltpu.make_async_copy(v_hbm, v_s, ld_sem.at[1]),
        pltpu.make_async_copy(q_hbm, q_s, ld_sem.at[2]),
        pltpu.make_async_copy(res_hbm, res_s, ld_sem.at[3]),
        pltpu.make_async_copy(wt, gw.at[me], ld_sem.at[4]),
        pltpu.make_async_copy(kw, gk.at[me], ld_sem.at[5]),
    ]
    for load in loads:
        load.start()
    steps_a = lax.broadcasted_iota(jnp.int32, (BLK, BLK), 0)
    steps_b = lax.broadcasted_iota(jnp.int32, (BLK, BLK), 1)
    lower = jnp.where(steps_b <= steps_a, 1.0, 0.0).astype(BF16)
    rest = ld[...]
    sums_row = jnp.zeros((HEADS, BLK), F32)
    sums_col = jnp.zeros((BLK, HEADS), F32)
    for _ in range(3):
        piece = rest.astype(BF16)
        rest = rest - piece.astype(F32)
        sums_row += lax.dot_general(piece, lower, NT_DIMS, preferred_element_type=F32)
        sums_col += lax.dot_general(lower, piece, NT_DIMS, preferred_element_type=F32)
    for h in range(HEADS):
        crow[h] = sums_row[h : h + 1, :]
        wide = jnp.broadcast_to(sums_col[:, h : h + 1], (BLK, HD))
        ccol[h] = wide
        a_s[h] = jnp.broadcast_to(wide[BLK - 1 : BLK, :], (8, HD))

    pl.semaphore_wait(barrier, len(peers))

    def near(i):
        half = lax.div(i + 1, 2)
        return mod(z + half * (1 - 2 * lax.rem(i, 2)), NZ)

    row_step = (0, 3, 1, 2)

    def slot(r, i):
        return at(mod(y + row_step[r], NY), near(i), c)

    lines = (None, ahead, behind, up, down)

    def take(kind, r, i):
        if kind == 0:
            s = slot(r, i)
            arrive(gw.at[s], w_r.at[r, i])
            send(gw.at[s], gw.at[s], w_ps.at[r, i], w_p.at[r, i], partner).start()
            return
        s = slot(r, i)
        if r == 3 and i == 0:
            arrive(gk.at[s, pl.ds(0, 32)], k_h.at[0])
            arrive(gk.at[s, pl.ds(32, 32)], k_h.at[1])
        else:
            arrive(gk.at[s], k_r.at[r, i])
        send(gk.at[s], gk.at[s], k_ps.at[r, i], k_p.at[r, i], partner).start()

    def along(i, link):
        back = 0 if i <= 2 else (6 if i == 7 and link == 2 else i - 2)
        index = (i - 1) // 2 if link == 1 else (3 if i == 7 else i // 2 - 1)
        return back, index

    def pass_on(link, kind, r, i):
        target = lines[link]
        if kind == 2:
            s = slot(r, 0)
            rows = gk.at[s, pl.ds(32 * (r - 1), 32)]
            send(rows, rows, k_fs.at[r - 1], k_h.at[r - 1], target).start()
            return
        whole, mine = (gw, wt) if kind == 0 else (gk, kw)
        if link <= 2:
            back, index = along(i, link)
            source = (r, back)
            ssem = w_zs.at[link - 1, index] if kind == 0 else k_zs.at[link - 1, r, index]
        elif kind == 1:
            source, ssem = (0, 0), k_ys.at[link - 3]
        elif r == 3:
            source, ssem = (1 if link == 3 else 2, i), w_fs.at[i]
        else:
            source, ssem = (0, i), w_ys.at[link - 3, i]
        s = slot(*source)
        src = mine if source == (0, 0) else whole.at[s]
        rsem = w_r.at[r, i] if kind == 0 else k_r.at[r, i]
        send(src, whole.at[s], ssem, rsem, target).start()

    def gather(*place):
        for what, kind, r, i in PLAN.get(place, ()):
            if what == 0:
                take(kind, r, i)
            else:
                pass_on(what, kind, r, i)

    def gather_at(step, steps, group, part):
        for n in steps:
            if (group, n, part) in PLAN:

                @pl.when(step == n)
                def _():
                    gather(group, n, part)

    send(wt, gw.at[me], w_ps.at[0, 0], w_p.at[0, 0], partner).start()
    send(kw, gk.at[me], k_ps.at[0, 0], k_p.at[0, 0], partner).start()
    gather(0, 0)
    for n in range(2):
        tb_s[n] = jnp.broadcast_to(tbl[0:1, n : n + 1], (8, HD))
    for m in range(1, NX):
        target = (me, mod(x + m, NX))
        send(tb_s, tb.at[x], t_s.at[m - 1], t_r.at[m - 1], target).start()

    def head_cols(h):
        return pl.ds(pl.multiple_of(h * HD, HD), HD)

    loads[0].wait()
    loads[1].wait()

    def update(h, carry):
        cb = ccol[h]
        gap = jnp.exp(cb[BLK - 1 : BLK, :] - cb)
        weighted = (k_s[:, head_cols(h)].astype(F32) * gap).astype(BF16)
        u_s[h] = lax.dot_general(
            weighted, v_s[:, head_cols(h)], TN_DIMS, preferred_element_type=F32
        )
        return carry

    lax.fori_loop(0, HEADS, update, 0)
    gather(1, 0)
    ub_s[...] = u_s[pl.ds(4 * (1 - c), 4)].astype(BF16)
    send(ub_s, ub_r, s1_s.at[0], s1_r.at[0], partner).start()
    send(a_s, a_r, s1_s.at[1], s1_r.at[1], partner).start()

    def chip_parts():
        own = u_s[pl.ds(4 * c, 4)]
        other = ub_r[...].astype(F32)
        a_own = a_s[pl.ds(4 * c, 4)]
        a_other = a_r[pl.ds(4 * c, 4)]
        first = c == 0
        return (
            jnp.where(first, own, other),
            jnp.where(first, other, own),
            jnp.where(first, a_own, a_other),
            jnp.where(first, a_other, a_own),
        )

    def split(row):
        a = jnp.broadcast_to(row, (16, HD))
        rows = lax.broadcasted_iota(jnp.int32, (16, HD), 0)
        hi = a.astype(BF16).astype(F32)
        mid = (a - hi).astype(BF16).astype(F32)
        low = a - hi - mid
        tile = jnp.where(rows == 0, hi, jnp.where(rows == 1, mid, jnp.where(rows == 2, low, 0.0)))
        return tile.astype(BF16)

    def joined(message):
        value = message.astype(F32)
        return value[0:64, :], jnp.sum(value[64:80, :], axis=0, keepdims=True)

    def scan_chip():
        arrive(ub_r, s1_r.at[0])
        arrive(a_r, s1_r.at[1])
        u0, u1, a0, a1 = chip_parts()
        total = jnp.exp(a1)[:, 0:1, :] * u0 + u1
        a_chip = a0 + a1
        for hl in range(4):
            tile = split(a_chip[hl, 0:1, :])
            for half in range(2):
                st_s[2 * hl + half, 0:64, :] = total[hl, 64 * half : 64 * half + 64, :].astype(BF16)
                st_s[2 * hl + half, 64:80, :] = tile
        st_r[z] = st_s[z]
        for m in FAR_Z:
            zz = mod(z + m, NZ)
            send(st_s.at[zz], st_r.at[z], s2_s.at[m], s2_r.at[m], (at(y, zz, c), x)).start()

    def chip_total(zz):
        return joined(st_r[zz])

    def scan_row():
        for m in range(1, NZ):
            arrive(st_r.at[mod(z - m, NZ)], s2_r.at[m])
        total = jnp.zeros((64, HD), F32)
        a_row = jnp.zeros((1, HD), F32)
        for zz in range(NZ):
            t, a = chip_total(zz)
            total = jnp.exp(a) * total + t
            a_row = a_row + a
        sr_s[0:64, :] = total.astype(BF16)
        sr_s[64:80, :] = split(a_row)
        sr_r[y] = sr_s[...]
        for m in (2, 1, 3):
            target = (at(mod(y + m, NY), z, c), x)
            send(sr_s, sr_r.at[y], s3_s.at[m], s3_r.at[m], target).start()

    def scan_back():
        for m in range(1, NY):
            arrive(sr_r.at[mod(y - m, NY)], s3_r.at[m])
        enter = jnp.zeros((64, HD), F32)
        for yy in range(NY):
            t, a = joined(sr_r[yy])
            moved = jnp.exp(a) * enter + t
            enter = jnp.where(yy < y, moved, enter)
        for zz in range(NZ):
            se_s[zz] = enter.astype(BF16)
            t, a = chip_total(zz)
            enter = jnp.exp(a) * enter + t
        se_r[z] = se_s[z]
        for m in FAR_Z:
            zz = mod(z + m, NZ)
            send(se_s.at[zz], se_r.at[z], s4_s.at[m], s4_r.at[m], (at(y, zz, c), x)).start()

    def scan_cores():
        for m in range(1, NZ):
            arrive(se_r.at[mod(z - m, NZ)], s4_r.at[m])
        enter = se_r[...].reshape(4, HD, HD).astype(F32)
        u0, _, a0, _ = chip_parts()
        after = jnp.exp(a0)[:, 0:1, :] * enter + u0
        first = c == 0
        sf_s[...] = jnp.where(first, after, enter).astype(BF16)
        send(sf_s, sf_r, s5_s.at[0], s5_r.at[0], partner).start()
        state[pl.ds(4 * c, 4)] = jnp.where(first, enter, after).astype(BF16)

    loads[2].wait()
    loads[4].wait()
    loads[5].wait()

    tri_a = lax.broadcasted_iota(jnp.int32, (HD, HD), 0)
    tri_b = lax.broadcasted_iota(jnp.int32, (HD, HD), 1)
    seen = tri_b <= tri_a

    def within(h, carry):
        gather_at(h, range(HEADS), 2, 0)

        @pl.when(h == 1)
        def _():
            scan_chip()

        @pl.when(h == 5)
        def _():
            scan_row()

        @pl.when(h == 7)
        def _():
            scan_back()

        gather_at(h, range(HEADS), 2, 1)

        for tq in range(4):
            rows = pl.ds(tq * HD, HD)
            width = HD * (tq + 1)
            products = lax.dot_general(
                q_s[rows, head_cols(h)], k_s[0:width, head_cols(h)], NT_DIMS,
                preferred_element_type=F32,
            )
            c_here = ccol[h, rows, :]
            blocks = []
            for ts in range(tq + 1):
                gap = c_here - crow[h, :, ts * HD : ts * HD + HD]
                piece = products[:, ts * HD : ts * HD + HD]
                if ts == tq:
                    gap = jnp.where(seen, gap, 0.0)
                    piece = jnp.where(seen, piece, 0.0)
                blocks.append((piece * jnp.exp(gap)).astype(BF16))
            scores = jnp.concatenate(blocks, axis=1) if tq else blocks[0]
            inner[rows, head_cols(h)] = jnp.dot(
                scores, v_s[0:width, head_cols(h)], preferred_element_type=F32
            )

        ccol[h] = jnp.exp(ccol[h])
        gather_at(h, range(HEADS), 2, 2)
        return carry

    lax.fori_loop(0, HEADS, within, 0)
    gather(4, 0)
    scan_cores()
    gather(4, 1)
    gather(5, 0)
    arrive(sf_r, s5_r.at[0])
    gather(5, 1)
    state[pl.ds(4 * (1 - c), 4)] = sf_r[...]

    def finish(h, carry):
        outer = jnp.dot(q_s[:, head_cols(h)], state[h], preferred_element_type=F32)
        kept = inner[:, head_cols(h)] + outer * ccol[h]
        scale = lax.rsqrt(jnp.mean(kept * kept, axis=-1, keepdims=True) + 1e-05)
        mixed[:, head_cols(h)] = (kept * scale).astype(BF16)
        return carry

    lax.fori_loop(0, HEADS, finish, 0)
    loads[3].wait()
    gather(6, 0)

    def row_of(r):
        step = jnp.where(r == 1, 3, jnp.where(r == 2, 1, jnp.where(r == 3, 2, 0)))
        return mod(y + step, NY)

    def chunk_rows(j):
        return row_of(lax.div(j, 2)) * 16 + lax.rem(j, 2) * 8

    def direction(d):
        return (right, -1) if d == 0 else (left, 1)

    def forward(j, step, d, value):
        rs_s[d, j, step] = value.astype(BF16)
        send(
            rs_s.at[d, j, step], rs_r.at[d, j, step],
            rs_ss.at[d, j, step], rs_rs.at[d, j, step], direction(d)[0],
        ).start()

    def w_ready(r):
        for i in range(NZ):
            s = at(row_of(r), near(i), 1 - c)
            arrive(gw.at[s], w_p.at[r, i])

    def reduce(t, carry):
        steps = range(CH + LAGS[2])
        gather_at(t, steps, 7, 0)
        for r in range(NY):

            @pl.when(t == 2 * r)
            def _():
                w_ready(r)

        @pl.when(t < CH)
        def _():
            weight = gw[pl.ds(chunk_rows(t), 8)].reshape(CW, HEADS * HD)
            product = lax.dot_general(mixed[...], weight, NT_DIMS, preferred_element_type=F32)
            part[t] = product.reshape(NX, PAGE, CW)
            for d in range(2):
                block = mod(x + direction(d)[1], NX)
                forward(t, 0, d, part[t, block, :, d * DW : d * DW + DW])

        gather_at(t, steps, 7, 1)
        for step in (1, 2):

            lag = LAGS[step - 1]

            @pl.when(jnp.logical_and(t >= lag, t < CH + lag))
            def _():
                j = t - lag
                for d in range(2):
                    arrive(rs_r.at[d, j, step - 1], rs_rs.at[d, j, step - 1])
                    block = lax.rem(x + direction(d)[1] * (1 + step) + 2 * NX, NX)
                    own = part[j, block, :, d * DW : d * DW + DW]
                    forward(j, step, d, rs_r[d, j, step - 1].astype(F32) + own)

            gather_at(t, steps, 7, step + 1)

        @pl.when(t >= LAGS[2])
        def _():
            j = t - LAGS[2]
            for d in range(2):
                arrive(rs_r.at[d, j, 2], rs_rs.at[d, j, 2])
                own = part[j, x, :, d * DW : d * DW + DW]
                cols = pl.ds(pl.multiple_of(chunk_rows(j) * 64 + d * DW, DW), DW)
                hidden = rs_r[d, j, 2].astype(F32) + own + res_s[:, cols].astype(F32)
                norm[:, cols] = (hidden * gain[:, cols]).astype(BF16)
                square = hidden * hidden
                squares[...] += square[:, :HD] + square[:, HD:]

        gather_at(t, steps, 7, 4)
        return carry

    squares[...] = jnp.zeros_like(squares)
    lax.fori_loop(0, CH + LAGS[2], reduce, 0)

    scale = lax.rsqrt(jnp.sum(squares[...], axis=-1, keepdims=True) * (1.0 / D) + 1e-05)
    gather(8, 0)
    gather(9, 0)

    def k_ready(i, carry):
        for r in range(NY):
            s = at(row_of(r), near(i), 1 - c)
            arrive(gk.at[s], k_p.at[r, i])
        return carry

    lax.fori_loop(0, NZ, k_ready, 0)
    x_left = mod(x - 1, NX)
    x_right = mod(x + 1, NX)
    x_far = mod(x + 2, NX)

    def tile(n):
        return pl.ds(pl.multiple_of(n * TW, TW), TW)

    def project(n, carry):
        @pl.when(n < NT)
        def _():
            weight = gk[:, :, tile(n)].reshape(D, TW)
            value = jnp.dot(norm[...], weight, preferred_element_type=F32)
            pg[x, :, tile(n)] = (value * scale).astype(BF16)
            own = pg.at[x, :, tile(n)]
            send(own, own, g_s.at[0, n], g_r.at[0, n], right).start()
            send(own, own, g_s.at[1, n], g_r.at[1, n], left).start()

        @pl.when(n >= 2)
        def _():
            j = n - 2
            arrive(pg.at[x_left, :, tile(j)], g_r.at[0, j])
            arrive(pg.at[x_right, :, tile(j)], g_r.at[1, j])
            early = j < 2
            source = jnp.where(early, x_left, x_right)
            target = (me, jnp.where(early, right[1], left[1]))
            page = pg.at[source, :, tile(j)]
            send(page, page, g_f.at[j], g_r.at[2, j], target).start()

        return carry

    lax.fori_loop(0, NT + 2, project, 0)

    def drain_w(i, carry):
        for d in range(2):
            sent(gw.at[0], w_ys.at[d, i])
        sent(gw.at[0], w_fs.at[i])
        for r in range(NY):
            sent(gw.at[0], w_ps.at[r, i])
            sent(gk.at[0], k_ps.at[r, i])
        return carry

    lax.fori_loop(0, NZ, drain_w, 0)
    for n in range(4):
        for d in range(2):
            if n < 3 or d == 1:
                sent(gw.at[0], w_zs.at[d, n])
            for r in range(NY):
                if n < 3 or d == r % 2:
                    sent(gk.at[0], k_zs.at[d, r, n])
    for d in range(2):
        sent(gk.at[0], k_ys.at[d])
        sent(gk.at[0, pl.ds(0, 32)], k_fs.at[d])
    sent(ub_s, s1_s.at[0])
    sent(a_s, s1_s.at[1])
    sent(sf_s, s5_s.at[0])
    for m in range(1, NZ):
        sent(st_s.at[0], s2_s.at[m])
        sent(se_s.at[0], s4_s.at[m])
    for m in range(1, NY):
        sent(sr_s, s3_s.at[m])

    def drain_rs(j, carry):
        for d in range(2):
            for step in range(3):
                sent(rs_s.at[0, 0, 0], rs_ss.at[d, j, step])
        return carry

    lax.fori_loop(0, CH, drain_rs, 0)
    tb[x] = tb_s[...]
    for m in range(1, NX):
        arrive(tb.at[mod(x - m, NX)], t_r.at[m - 1])
        sent(tb_s, t_s.at[m - 1])
    def holds(s, p):
        hit = jnp.logical_and(tb[p, 0] == x, tb[p, 1] == s).astype(F32)
        return jnp.broadcast_to(hit[0:1, 0:1], (PAGE, KVW)) > 0.5

    for s in range(2):
        total = jnp.zeros((PAGE, KVW), BF16)
        for p in (x, x_left, x_right):
            total = jnp.where(holds(s, p), pg[p], total)
        cache[s] = total
    for n in range(NT):
        sent(pg.at[0, :, pl.ds(0, TW)], g_s.at[0, n])
        sent(pg.at[0, :, pl.ds(0, TW)], g_s.at[1, n])
        sent(pg.at[0, :, pl.ds(0, TW)], g_f.at[n])
    for n in range(NT):
        arrive(pg.at[x_far, :, tile(n)], g_r.at[2, n])
    for s in range(2):
        cache[s] = jnp.where(holds(s, x_far), pg[x_far], cache[s])


def on_device(query_rows, key_rows, value_rows, log_decay, residual, out_weight, norm_gain, kv_weight, block_table):
    vm, dma = pltpu.VMEM, pltpu.SemaphoreType.DMA
    hbm = pl.BlockSpec(memory_space=pl.ANY)
    vmem = pl.BlockSpec(memory_space=pltpu.VMEM)
    cache = pl.pallas_call(
        kernel,
        out_shape=jax.ShapeDtypeStruct((2, PAGE, KVW), BF16),
        in_specs=[hbm, hbm, hbm, hbm, hbm, vmem, hbm, vmem, vmem],
        out_specs=vmem,
        scratch_shapes=[
            vm((64, 64, HEADS * HD), BF16),
            vm((64, 64, KVW), BF16),
            vm((BLK, HEADS * HD), BF16),
            vm((BLK, HEADS * HD), BF16),
            vm((BLK, HEADS * HD), BF16),
            vm((PAGE, D), BF16),
            vm((HEADS, 1, BLK), F32),
            vm((HEADS, BLK, HD), F32),
            vm((HEADS, 8, HD), F32),
            vm((HEADS, 8, HD), F32),
            vm((HEADS, HD, HD), F32),
            vm((BLK, HEADS * HD), F32),
            vm((BLK, HEADS * HD), BF16),
            vm((4, HD, HD), BF16),
            vm((4, HD, HD), BF16),
            vm((NZ, 80, HD), BF16),
            vm((NZ, 80, HD), BF16),
            vm((80, HD), BF16),
            vm((NY, 80, HD), BF16),
            vm((NZ, 64, HD), BF16),
            vm((NZ, 64, HD), BF16),
            vm((4, HD, HD), BF16),
            vm((4, HD, HD), BF16),
            vm((HEADS, HD, HD), BF16),
            vm((CH, NX, PAGE, CW), F32),
            vm((2, CH, 3, PAGE, DW), BF16),
            vm((2, CH, 3, PAGE, DW), BF16),
            vm((PAGE, HD), F32),
            vm((PAGE, D), BF16),
            vm((NX, PAGE, KVW), BF16),
            vm((NX, 2, 8, HD), jnp.int32),
            vm((2, 8, HD), jnp.int32),
            dma((6,)),
            dma((2, 4)), dma((2, NZ)), dma((NZ,)), dma((NY, NZ)), dma((NY, NZ)), dma((NY, NZ)),
            dma((2, NY, 4)), dma((2,)), dma((2,)), dma((NY, NZ)), dma((NY, NZ)), dma((2,)), dma((NY, NZ)),
            dma((2,)), dma((2,)), dma((NZ,)), dma((NZ,)), dma((NY,)), dma((NY,)),
            dma((NZ,)), dma((NZ,)), dma((1,)), dma((1,)),
            dma((2, CH, 3)), dma((2, CH, 3)), dma((2, NT)), dma((NT,)), dma((3, NT)), dma((3,)), dma((3,)),
        ],
        compiler_params=pltpu.CompilerParams(
            collective_id=0, has_side_effects=True, vmem_limit_bytes=63 * 1024 * 1024
        ),
        name="layer",
    )(
        out_weight.T, kv_weight, query_rows, key_rows, value_rows, log_decay,
        residual, norm_gain.reshape(1, D), block_table,
    )
    return cache.reshape(1, 1, 2, PAGE, KVW)


def solution(mesh):
    placed = (
        P("seq", "pool"),
        P("seq", "pool"),
        P("seq", "pool"),
        P("pool", "seq"),
        P(("seq", "pool"), None),
        P("pool", "seq"),
        P(),
        P("seq", None),
        P(("seq", "pool"), None),
    )
    return jax.shard_map(
        on_device,
        mesh=mesh,
        in_specs=placed,
        out_specs=P("seq", "pool", None, None, None),
        check_vma=False,
    )
```

```python
import jax
import jax.numpy as jnp
from jax import lax
from jax.experimental import pallas as pl
from jax.experimental.pallas import tpu as pltpu
from jax.sharding import PartitionSpec as P

NY, NZ, NX = 4, 8, 4
HEADS = 8
HD = 128
BLK = 512
PAGE = 128
D = 4096
KVW = 1024
CH = 8
CW = D // CH
DW = CW // 2
LAGS = (2, 4, 6)
NT = 4
TW = KVW // NT
F32 = jnp.float32
BF16 = jnp.bfloat16
MESH = pl.DeviceIdType.MESH
FAR_Z = (4, 3, 5, 2, 6, 1, 7)
NT_DIMS = (((1,), (1,)), ((), ()))
TN_DIMS = (((0,), (0,)), ((), ()))

PLAN = {
    (0, 0): ((1, 0, 0, 1), (2, 0, 0, 2), (3, 0, 1, 0), (4, 0, 2, 0),),
    (1, 0): ((3, 1, 1, 0), (4, 1, 2, 0),),
    (2, 2, 2): ((0, 0, 0, 1), (0, 0, 0, 2), (0, 0, 1, 0), (0, 0, 2, 0), (2, 0, 0, 4), (3, 0, 1, 1), (4, 0, 2, 1),),
    (2, 5, 0): ((1, 0, 0, 3), (3, 0, 1, 2), (4, 0, 2, 2), (0, 1, 1, 0), (0, 1, 2, 0),),
    (2, 5, 1): ((4, 2, 2, 0),),
    (2, 5, 2): ((0, 0, 1, 1), (0, 0, 2, 1), (3, 2, 1, 0),),
    (2, 6, 2): ((0, 0, 0, 4), (2, 0, 0, 6), (4, 0, 2, 4),),
    (2, 7, 0): ((3, 0, 1, 4), (0, 0, 0, 3), (1, 0, 0, 5), (0, 0, 1, 2), (0, 0, 2, 2),),
    (2, 7, 1): ((4, 0, 2, 3),),
    (2, 7, 2): ((3, 0, 1, 3),),
    (4, 0): ((2, 1, 1, 2), (0, 1, 3, 0), (4, 0, 3, 1), (0, 0, 0, 6), (0, 0, 2, 4), (3, 0, 1, 6), (1, 1, 1, 1), (2, 0, 0, 7), (0, 0, 0, 5), (0, 0, 1, 4), (4, 0, 2, 5), (0, 0, 2, 3), (3, 0, 1, 5), (1, 1, 0, 1), (2, 1, 0, 2),),
    (4, 1): ((0, 0, 1, 3),),
    (5, 0): ((0, 1, 1, 2), (4, 0, 2, 6),),
    (6, 0): ((0, 0, 0, 7), (0, 0, 3, 1), (0, 0, 1, 6), (0, 1, 1, 1), (3, 0, 1, 7), (1, 1, 2, 1), (2, 1, 2, 2),),
    (7, 0, 0): ((4, 0, 2, 7),),
    (7, 0, 1): ((0, 0, 2, 5), (3, 0, 3, 0), (1, 1, 3, 1), (2, 1, 3, 2),),
    (7, 1, 1): ((0, 0, 1, 5), (0, 1, 0, 1), (0, 1, 0, 2),),
    (7, 2, 0): ((4, 0, 3, 3), (0, 0, 2, 6), (3, 0, 3, 2), (1, 1, 0, 3), (2, 1, 1, 4), (0, 0, 1, 7), (0, 1, 2, 1), (0, 1, 2, 2), (4, 0, 3, 5),),
    (7, 2, 1): ((0, 0, 2, 7), (3, 0, 3, 4), (1, 1, 2, 3), (2, 1, 2, 4),),
    (7, 3, 1): ((0, 0, 3, 0), (0, 1, 3, 1), (0, 1, 3, 2), (4, 0, 3, 7),),
    (7, 4, 1): ((0, 0, 3, 3), (3, 0, 3, 6), (1, 1, 3, 3), (2, 1, 3, 4),),
    (7, 4, 2): ((0, 0, 3, 2), (0, 1, 0, 3), (0, 1, 1, 4),),
    (7, 5, 1): ((0, 0, 3, 5), (1, 1, 0, 5), (2, 1, 1, 6),),
    (7, 5, 2): ((0, 0, 3, 4), (0, 1, 2, 3), (0, 1, 2, 4),),
    (7, 6, 0): ((0, 0, 3, 7), (1, 1, 2, 5), (2, 1, 2, 6), (0, 0, 3, 6), (0, 1, 3, 3), (0, 1, 3, 4),),
    (7, 6, 2): ((1, 1, 3, 5), (2, 1, 3, 6),),
    (7, 7, 1): ((0, 1, 0, 5), (0, 1, 1, 6),),
    (7, 7, 2): ((1, 1, 0, 7), (2, 1, 1, 7),),
    (7, 7, 3): ((0, 1, 2, 5), (0, 1, 2, 6),),
    (7, 8, 0): ((1, 1, 2, 7), (2, 1, 0, 4),),
    (7, 8, 2): ((0, 1, 3, 5), (0, 1, 3, 6),),
    (7, 8, 3): ((1, 1, 1, 3), (2, 1, 3, 7),),
    (7, 9, 0): ((0, 1, 0, 7), (0, 1, 1, 7),),
    (7, 9, 3): ((0, 1, 2, 7), (0, 1, 0, 4), (2, 1, 0, 6),),
    (7, 10, 3): ((0, 1, 1, 3), (0, 1, 3, 7), (1, 1, 1, 5),),
    (7, 11, 3): ((0, 1, 0, 6),),
    (7, 13, 0): ((0, 1, 1, 5),),
}


def kernel(
    wt, kw, q_hbm, k_hbm, v_hbm, ld, res_hbm, gain, tbl,
    cache,
    gw, gk, q_s, k_s, v_s, res_s, crow, ccol, a_s, a_r, u_s, inner, mixed,
    ub_s, ub_r, st_s, st_r, sr_s, sr_r, se_s, se_r, sf_s, sf_r, state,
    part, rs_s, rs_r, squares, norm, pg, tb, tb_s,
    ld_sem, w_zs, w_ys, w_fs, w_ps, w_r, w_p,
    k_zs, k_ys, k_fs, k_ps, k_r, k_h, k_p,
    s1_s, s1_r, s2_s, s2_r, s3_s, s3_r, s4_s, s4_r, s5_s, s5_r,
    rs_ss, rs_rs, g_s, g_f, g_r, t_s, t_r,
):
    me = lax.axis_index("seq")
    x = lax.axis_index("pool")
    y = lax.div(me, 16)
    z = lax.rem(lax.div(me, 2), 8)
    c = lax.rem(me, 2)

    def at(yy, zz, cc):
        return (yy * NZ + zz) * 2 + cc

    def mod(value, size):
        return lax.rem(value + size, size)

    up = (at(mod(y + 1, NY), z, c), x)
    down = (at(mod(y - 1, NY), z, c), x)
    ahead = (at(y, mod(z + 1, NZ), c), x)
    behind = (at(y, mod(z - 1, NZ), c), x)
    partner = (at(y, z, 1 - c), x)
    right = (me, mod(x + 1, NX))
    left = (me, mod(x - 1, NX))

    def send(src, dst, ssem, rsem, device):
        copy = pltpu.make_async_remote_copy(
            src_ref=src, dst_ref=dst, send_sem=ssem, recv_sem=rsem,
            device_id=device, device_id_type=MESH,
        )
        return copy

    def arrive(ref, rsem):
        send(ref, ref, rsem, rsem, partner).wait_recv()

    def sent(ref, ssem):
        send(ref, ref, ssem, ssem, partner).wait_send()

    peers = [partner]
    peers += [(at(y, mod(z + m, NZ), c), x) for m in range(1, NZ)]
    peers += [(at(mod(y + m, NY), z, c), x) for m in range(1, NY)]
    peers += [(me, mod(x + m, NX)) for m in range(1, NX)]
    barrier = pltpu.get_barrier_semaphore()
    for peer in peers:
        pl.semaphore_signal(barrier, inc=1, device_id=peer, device_id_type=MESH)
    loads = [
        pltpu.make_async_copy(k_hbm, k_s, ld_sem.at[0]),
        pltpu.make_async_copy(v_hbm, v_s, ld_sem.at[1]),
        pltpu.make_async_copy(q_hbm, q_s, ld_sem.at[2]),
        pltpu.make_async_copy(res_hbm, res_s, ld_sem.at[3]),
        pltpu.make_async_copy(wt, gw.at[me], ld_sem.at[4]),
        pltpu.make_async_copy(kw, gk.at[me], ld_sem.at[5]),
    ]
    for load in loads:
        load.start()
    steps_a = lax.broadcasted_iota(jnp.int32, (BLK, BLK), 0)
    steps_b = lax.broadcasted_iota(jnp.int32, (BLK, BLK), 1)
    lower = jnp.where(steps_b <= steps_a, 1.0, 0.0).astype(BF16)
    rest = ld[...]
    sums_row = jnp.zeros((HEADS, BLK), F32)
    sums_col = jnp.zeros((BLK, HEADS), F32)
    for _ in range(3):
        piece = rest.astype(BF16)
        rest = rest - piece.astype(F32)
        sums_row += lax.dot_general(piece, lower, NT_DIMS, preferred_element_type=F32)
        sums_col += lax.dot_general(lower, piece, NT_DIMS, preferred_element_type=F32)
    for h in range(HEADS):
        crow[h] = sums_row[h : h + 1, :]
        wide = jnp.broadcast_to(sums_col[:, h : h + 1], (BLK, HD))
        ccol[h] = wide
        a_s[h] = jnp.broadcast_to(wide[BLK - 1 : BLK, :], (8, HD))

    pl.semaphore_wait(barrier, len(peers))

    def near(i):
        half = lax.div(i + 1, 2)
        return mod(z + half * (1 - 2 * lax.rem(i, 2)), NZ)

    row_step = (0, 3, 1, 2)

    def slot(r, i):
        return at(mod(y + row_step[r], NY), near(i), c)

    lines = (None, ahead, behind, up, down)

    def take(kind, r, i):
        if kind == 0:
            s = slot(r, i)
            arrive(gw.at[s], w_r.at[r, i])
            send(gw.at[s], gw.at[s], w_ps.at[r, i], w_p.at[r, i], partner).start()
            return
        s = slot(r, i)
        if r == 3 and i == 0:
            arrive(gk.at[s, pl.ds(0, 32)], k_h.at[0])
            arrive(gk.at[s, pl.ds(32, 32)], k_h.at[1])
        else:
            arrive(gk.at[s], k_r.at[r, i])
        send(gk.at[s], gk.at[s], k_ps.at[r, i], k_p.at[r, i], partner).start()

    def along(i, link):
        back = 0 if i <= 2 else (6 if i == 7 and link == 2 else i - 2)
        index = (i - 1) // 2 if link == 1 else (3 if i == 7 else i // 2 - 1)
        return back, index

    def pass_on(link, kind, r, i):
        target = lines[link]
        if kind == 2:
            s = slot(r, 0)
            rows = gk.at[s, pl.ds(32 * (r - 1), 32)]
            send(rows, rows, k_fs.at[r - 1], k_h.at[r - 1], target).start()
            return
        whole, mine = (gw, wt) if kind == 0 else (gk, kw)
        if link <= 2:
            back, index = along(i, link)
            source = (r, back)
            ssem = w_zs.at[link - 1, index] if kind == 0 else k_zs.at[link - 1, r, index]
        elif kind == 1:
            source, ssem = (0, 0), k_ys.at[link - 3]
        elif r == 3:
            source, ssem = (1 if link == 3 else 2, i), w_fs.at[i]
        else:
            source, ssem = (0, i), w_ys.at[link - 3, i]
        s = slot(*source)
        src = mine if source == (0, 0) else whole.at[s]
        rsem = w_r.at[r, i] if kind == 0 else k_r.at[r, i]
        send(src, whole.at[s], ssem, rsem, target).start()

    def gather(*place):
        for what, kind, r, i in PLAN.get(place, ()):
            if what == 0:
                take(kind, r, i)
            else:
                pass_on(what, kind, r, i)

    def gather_at(step, steps, group, part):
        for n in steps:
            if (group, n, part) in PLAN:

                @pl.when(step == n)
                def _():
                    gather(group, n, part)

    send(wt, gw.at[me], w_ps.at[0, 0], w_p.at[0, 0], partner).start()
    send(kw, gk.at[me], k_ps.at[0, 0], k_p.at[0, 0], partner).start()
    gather(0, 0)
    for n in range(2):
        tb_s[n] = jnp.broadcast_to(tbl[0:1, n : n + 1], (8, HD))
    for m in range(1, NX):
        target = (me, mod(x + m, NX))
        send(tb_s, tb.at[x], t_s.at[m - 1], t_r.at[m - 1], target).start()

    def head_cols(h):
        return pl.ds(pl.multiple_of(h * HD, HD), HD)

    loads[0].wait()
    loads[1].wait()

    def update(n, carry):
        h = lax.rem(n + 4 * (1 - c), HEADS)
        cb = ccol[h]
        gap = jnp.exp(cb[BLK - 1 : BLK, :] - cb)
        weighted = (k_s[:, head_cols(h)].astype(F32) * gap).astype(BF16)
        u_s[h] = lax.dot_general(
            weighted, v_s[:, head_cols(h)], TN_DIMS, preferred_element_type=F32
        )
        return carry

    lax.fori_loop(0, 4, update, 0)
    ub_s[...] = u_s[pl.ds(4 * (1 - c), 4)].astype(BF16)
    send(ub_s, ub_r, s1_s.at[0], s1_r.at[0], partner).start()
    send(a_s, a_r, s1_s.at[1], s1_r.at[1], partner).start()
    lax.fori_loop(4, HEADS, update, 0)
    gather(1, 0)

    def chip_parts():
        own = u_s[pl.ds(4 * c, 4)]
        other = ub_r[...].astype(F32)
        a_own = a_s[pl.ds(4 * c, 4)]
        a_other = a_r[pl.ds(4 * c, 4)]
        first = c == 0
        return (
            jnp.where(first, own, other),
            jnp.where(first, other, own),
            jnp.where(first, a_own, a_other),
            jnp.where(first, a_other, a_own),
        )

    def split(row):
        a = jnp.broadcast_to(row, (16, HD))
        rows = lax.broadcasted_iota(jnp.int32, (16, HD), 0)
        hi = a.astype(BF16).astype(F32)
        mid = (a - hi).astype(BF16).astype(F32)
        low = a - hi - mid
        tile = jnp.where(rows == 0, hi, jnp.where(rows == 1, mid, jnp.where(rows == 2, low, 0.0)))
        return tile.astype(BF16)

    def joined(message):
        value = message.astype(F32)
        return value[0:64, :], jnp.sum(value[64:80, :], axis=0, keepdims=True)

    def scan_chip():
        arrive(ub_r, s1_r.at[0])
        arrive(a_r, s1_r.at[1])
        u0, u1, a0, a1 = chip_parts()
        total = jnp.exp(a1)[:, 0:1, :] * u0 + u1
        a_chip = a0 + a1
        for hl in range(4):
            tile = split(a_chip[hl, 0:1, :])
            for half in range(2):
                st_s[2 * hl + half, 0:64, :] = total[hl, 64 * half : 64 * half + 64, :].astype(BF16)
                st_s[2 * hl + half, 64:80, :] = tile
        st_r[z] = st_s[z]
        for m in FAR_Z:
            zz = mod(z + m, NZ)
            send(st_s.at[zz], st_r.at[z], s2_s.at[m], s2_r.at[m], (at(y, zz, c), x)).start()

    def chip_total(zz):
        return joined(st_r[zz])

    def scan_row():
        for m in range(1, NZ):
            arrive(st_r.at[mod(z - m, NZ)], s2_r.at[m])
        total = jnp.zeros((64, HD), F32)
        a_row = jnp.zeros((1, HD), F32)
        for zz in range(NZ):
            t, a = chip_total(zz)
            total = jnp.exp(a) * total + t
            a_row = a_row + a
        sr_s[0:64, :] = total.astype(BF16)
        sr_s[64:80, :] = split(a_row)
        sr_r[y] = sr_s[...]
        for m in (2, 1, 3):
            target = (at(mod(y + m, NY), z, c), x)
            send(sr_s, sr_r.at[y], s3_s.at[m], s3_r.at[m], target).start()

    def scan_back():
        for m in range(1, NY):
            arrive(sr_r.at[mod(y - m, NY)], s3_r.at[m])
        enter = jnp.zeros((64, HD), F32)
        for yy in range(NY):
            t, a = joined(sr_r[yy])
            moved = jnp.exp(a) * enter + t
            enter = jnp.where(yy < y, moved, enter)
        for zz in range(NZ):
            se_s[zz] = enter.astype(BF16)
            t, a = chip_total(zz)
            enter = jnp.exp(a) * enter + t
        se_r[z] = se_s[z]
        for m in FAR_Z:
            zz = mod(z + m, NZ)
            send(se_s.at[zz], se_r.at[z], s4_s.at[m], s4_r.at[m], (at(y, zz, c), x)).start()

    def scan_cores():
        for m in range(1, NZ):
            arrive(se_r.at[mod(z - m, NZ)], s4_r.at[m])
        enter = se_r[...].reshape(4, HD, HD).astype(F32)
        u0, _, a0, _ = chip_parts()
        after = jnp.exp(a0)[:, 0:1, :] * enter + u0
        first = c == 0
        sf_s[...] = jnp.where(first, after, enter).astype(BF16)
        send(sf_s, sf_r, s5_s.at[0], s5_r.at[0], partner).start()
        state[pl.ds(4 * c, 4)] = jnp.where(first, enter, after).astype(BF16)

    loads[2].wait()
    loads[4].wait()
    loads[5].wait()

    tri_a = lax.broadcasted_iota(jnp.int32, (HD, HD), 0)
    tri_b = lax.broadcasted_iota(jnp.int32, (HD, HD), 1)
    seen = tri_b <= tri_a

    def within(h, carry):
        gather_at(h, range(HEADS), 2, 0)

        @pl.when(h == 1)
        def _():
            scan_chip()

        @pl.when(h == 5)
        def _():
            scan_row()

        @pl.when(h == 7)
        def _():
            scan_back()

        gather_at(h, range(HEADS), 2, 1)

        for tq in range(4):
            rows = pl.ds(tq * HD, HD)
            width = HD * (tq + 1)
            products = lax.dot_general(
                q_s[rows, head_cols(h)], k_s[0:width, head_cols(h)], NT_DIMS,
                preferred_element_type=F32,
            )
            c_here = ccol[h, rows, :]
            blocks = []
            for ts in range(tq + 1):
                gap = c_here - crow[h, :, ts * HD : ts * HD + HD]
                piece = products[:, ts * HD : ts * HD + HD]
                if ts == tq:
                    gap = jnp.where(seen, gap, 0.0)
                    piece = jnp.where(seen, piece, 0.0)
                blocks.append((piece * jnp.exp(gap)).astype(BF16))
            scores = jnp.concatenate(blocks, axis=1) if tq else blocks[0]
            inner[rows, head_cols(h)] = jnp.dot(
                scores, v_s[0:width, head_cols(h)], preferred_element_type=F32
            )

        ccol[h] = jnp.exp(ccol[h])
        gather_at(h, range(HEADS), 2, 2)
        return carry

    lax.fori_loop(0, HEADS, within, 0)
    gather(4, 0)
    scan_cores()
    gather(4, 1)
    gather(5, 0)
    arrive(sf_r, s5_r.at[0])
    gather(5, 1)
    state[pl.ds(4 * (1 - c), 4)] = sf_r[...]

    def finish(h, carry):
        outer = jnp.dot(q_s[:, head_cols(h)], state[h], preferred_element_type=F32)
        kept = inner[:, head_cols(h)] + outer * ccol[h]
        scale = lax.rsqrt(jnp.mean(kept * kept, axis=-1, keepdims=True) + 1e-05)
        mixed[:, head_cols(h)] = (kept * scale).astype(BF16)
        return carry

    lax.fori_loop(0, HEADS, finish, 0)
    loads[3].wait()
    gather(6, 0)

    def row_of(r):
        step = jnp.where(r == 1, 3, jnp.where(r == 2, 1, jnp.where(r == 3, 2, 0)))
        return mod(y + step, NY)

    def chunk_rows(j):
        return row_of(lax.div(j, 2)) * 16 + lax.rem(j, 2) * 8

    def direction(d):
        return (right, -1) if d == 0 else (left, 1)

    def forward(j, step, d, value):
        rs_s[d, j, step] = value.astype(BF16)
        send(
            rs_s.at[d, j, step], rs_r.at[d, j, step],
            rs_ss.at[d, j, step], rs_rs.at[d, j, step], direction(d)[0],
        ).start()

    def w_ready(r):
        for i in range(NZ):
            s = at(row_of(r), near(i), 1 - c)
            arrive(gw.at[s], w_p.at[r, i])

    def reduce(t, carry):
        steps = range(CH + LAGS[2])
        gather_at(t, steps, 7, 0)
        for r in range(NY):

            @pl.when(t == 2 * r)
            def _():
                w_ready(r)

        @pl.when(t < CH)
        def _():
            weight = gw[pl.ds(chunk_rows(t), 8)].reshape(CW, HEADS * HD)
            product = lax.dot_general(mixed[...], weight, NT_DIMS, preferred_element_type=F32)
            part[t] = product.reshape(NX, PAGE, CW)
            for d in range(2):
                block = mod(x + direction(d)[1], NX)
                forward(t, 0, d, part[t, block, :, d * DW : d * DW + DW])

        gather_at(t, steps, 7, 1)
        for step in (1, 2):

            lag = LAGS[step - 1]

            @pl.when(jnp.logical_and(t >= lag, t < CH + lag))
            def _():
                j = t - lag
                for d in range(2):
                    arrive(rs_r.at[d, j, step - 1], rs_rs.at[d, j, step - 1])
                    block = lax.rem(x + direction(d)[1] * (1 + step) + 2 * NX, NX)
                    own = part[j, block, :, d * DW : d * DW + DW]
                    forward(j, step, d, rs_r[d, j, step - 1].astype(F32) + own)

            gather_at(t, steps, 7, step + 1)

        @pl.when(t >= LAGS[2])
        def _():
            j = t - LAGS[2]
            for d in range(2):
                arrive(rs_r.at[d, j, 2], rs_rs.at[d, j, 2])
                own = part[j, x, :, d * DW : d * DW + DW]
                cols = pl.ds(pl.multiple_of(chunk_rows(j) * 64 + d * DW, DW), DW)
                hidden = rs_r[d, j, 2].astype(F32) + own + res_s[:, cols].astype(F32)
                norm[:, cols] = (hidden * gain[:, cols]).astype(BF16)
                square = hidden * hidden
                squares[...] += square[:, :HD] + square[:, HD:]

        gather_at(t, steps, 7, 4)
        return carry

    squares[...] = jnp.zeros_like(squares)
    lax.fori_loop(0, CH + LAGS[2], reduce, 0)

    scale = lax.rsqrt(jnp.sum(squares[...], axis=-1, keepdims=True) * (1.0 / D) + 1e-05)
    gather(8, 0)
    gather(9, 0)

    def k_ready(i, carry):
        for r in range(NY):
            s = at(row_of(r), near(i), 1 - c)
            arrive(gk.at[s], k_p.at[r, i])
        return carry

    lax.fori_loop(0, NZ, k_ready, 0)
    x_left = mod(x - 1, NX)
    x_right = mod(x + 1, NX)
    x_far = mod(x + 2, NX)

    def tile(n):
        return pl.ds(pl.multiple_of(n * TW, TW), TW)

    def project(n, carry):
        @pl.when(n < NT)
        def _():
            weight = gk[:, :, tile(n)].reshape(D, TW)
            value = jnp.dot(norm[...], weight, preferred_element_type=F32)
            pg[x, :, tile(n)] = (value * scale).astype(BF16)
            own = pg.at[x, :, tile(n)]
            send(own, own, g_s.at[0, n], g_r.at[0, n], right).start()
            send(own, own, g_s.at[1, n], g_r.at[1, n], left).start()

        @pl.when(n >= 2)
        def _():
            j = n - 2
            arrive(pg.at[x_left, :, tile(j)], g_r.at[0, j])
            arrive(pg.at[x_right, :, tile(j)], g_r.at[1, j])
            early = j < 2
            source = jnp.where(early, x_left, x_right)
            target = (me, jnp.where(early, right[1], left[1]))
            page = pg.at[source, :, tile(j)]
            send(page, page, g_f.at[j], g_r.at[2, j], target).start()

        return carry

    lax.fori_loop(0, NT + 2, project, 0)

    def drain_w(i, carry):
        for d in range(2):
            sent(gw.at[0], w_ys.at[d, i])
        sent(gw.at[0], w_fs.at[i])
        for r in range(NY):
            sent(gw.at[0], w_ps.at[r, i])
            sent(gk.at[0], k_ps.at[r, i])
        return carry

    lax.fori_loop(0, NZ, drain_w, 0)
    for n in range(4):
        for d in range(2):
            if n < 3 or d == 1:
                sent(gw.at[0], w_zs.at[d, n])
            for r in range(NY):
                if n < 3 or d == r % 2:
                    sent(gk.at[0], k_zs.at[d, r, n])
    for d in range(2):
        sent(gk.at[0], k_ys.at[d])
        sent(gk.at[0, pl.ds(0, 32)], k_fs.at[d])
    sent(ub_s, s1_s.at[0])
    sent(a_s, s1_s.at[1])
    sent(sf_s, s5_s.at[0])
    for m in range(1, NZ):
        sent(st_s.at[0], s2_s.at[m])
        sent(se_s.at[0], s4_s.at[m])
    for m in range(1, NY):
        sent(sr_s, s3_s.at[m])

    def drain_rs(j, carry):
        for d in range(2):
            for step in range(3):
                sent(rs_s.at[0, 0, 0], rs_ss.at[d, j, step])
        return carry

    lax.fori_loop(0, CH, drain_rs, 0)
    tb[x] = tb_s[...]
    for m in range(1, NX):
        arrive(tb.at[mod(x - m, NX)], t_r.at[m - 1])
        sent(tb_s, t_s.at[m - 1])
    def holds(s, p):
        hit = jnp.logical_and(tb[p, 0] == x, tb[p, 1] == s).astype(F32)
        return jnp.broadcast_to(hit[0:1, 0:1], (PAGE, KVW)) > 0.5

    for s in range(2):
        total = jnp.zeros((PAGE, KVW), BF16)
        for p in (x, x_left, x_right):
            total = jnp.where(holds(s, p), pg[p], total)
        cache[s] = total
    for n in range(NT):
        sent(pg.at[0, :, pl.ds(0, TW)], g_s.at[0, n])
        sent(pg.at[0, :, pl.ds(0, TW)], g_s.at[1, n])
        sent(pg.at[0, :, pl.ds(0, TW)], g_f.at[n])
    for n in range(NT):
        arrive(pg.at[x_far, :, tile(n)], g_r.at[2, n])
    for s in range(2):
        cache[s] = jnp.where(holds(s, x_far), pg[x_far], cache[s])


def on_device(query_rows, key_rows, value_rows, log_decay, residual, out_weight, norm_gain, kv_weight, block_table):
    vm, dma = pltpu.VMEM, pltpu.SemaphoreType.DMA
    hbm = pl.BlockSpec(memory_space=pl.ANY)
    vmem = pl.BlockSpec(memory_space=pltpu.VMEM)
    cache = pl.pallas_call(
        kernel,
        out_shape=jax.ShapeDtypeStruct((2, PAGE, KVW), BF16),
        in_specs=[hbm, hbm, hbm, hbm, hbm, vmem, hbm, vmem, vmem],
        out_specs=vmem,
        scratch_shapes=[
            vm((64, 64, HEADS * HD), BF16),
            vm((64, 64, KVW), BF16),
            vm((BLK, HEADS * HD), BF16),
            vm((BLK, HEADS * HD), BF16),
            vm((BLK, HEADS * HD), BF16),
            vm((PAGE, D), BF16),
            vm((HEADS, 1, BLK), F32),
            vm((HEADS, BLK, HD), F32),
            vm((HEADS, 8, HD), F32),
            vm((HEADS, 8, HD), F32),
            vm((HEADS, HD, HD), F32),
            vm((BLK, HEADS * HD), F32),
            vm((BLK, HEADS * HD), BF16),
            vm((4, HD, HD), BF16),
            vm((4, HD, HD), BF16),
            vm((NZ, 80, HD), BF16),
            vm((NZ, 80, HD), BF16),
            vm((80, HD), BF16),
            vm((NY, 80, HD), BF16),
            vm((NZ, 64, HD), BF16),
            vm((NZ, 64, HD), BF16),
            vm((4, HD, HD), BF16),
            vm((4, HD, HD), BF16),
            vm((HEADS, HD, HD), BF16),
            vm((CH, NX, PAGE, CW), F32),
            vm((2, CH, 3, PAGE, DW), BF16),
            vm((2, CH, 3, PAGE, DW), BF16),
            vm((PAGE, HD), F32),
            vm((PAGE, D), BF16),
            vm((NX, PAGE, KVW), BF16),
            vm((NX, 2, 8, HD), jnp.int32),
            vm((2, 8, HD), jnp.int32),
            dma((6,)),
            dma((2, 4)), dma((2, NZ)), dma((NZ,)), dma((NY, NZ)), dma((NY, NZ)), dma((NY, NZ)),
            dma((2, NY, 4)), dma((2,)), dma((2,)), dma((NY, NZ)), dma((NY, NZ)), dma((2,)), dma((NY, NZ)),
            dma((2,)), dma((2,)), dma((NZ,)), dma((NZ,)), dma((NY,)), dma((NY,)),
            dma((NZ,)), dma((NZ,)), dma((1,)), dma((1,)),
            dma((2, CH, 3)), dma((2, CH, 3)), dma((2, NT)), dma((NT,)), dma((3, NT)), dma((3,)), dma((3,)),
        ],
        compiler_params=pltpu.CompilerParams(
            collective_id=0, has_side_effects=True, vmem_limit_bytes=63 * 1024 * 1024
        ),
        name="layer",
    )(
        out_weight.T, kv_weight, query_rows, key_rows, value_rows, log_decay,
        residual, norm_gain.reshape(1, D), block_table,
    )
    return cache.reshape(1, 1, 2, PAGE, KVW)


def solution(mesh):
    placed = (
        P("seq", "pool"),
        P("seq", "pool"),
        P("seq", "pool"),
        P("pool", "seq"),
        P(("seq", "pool"), None),
        P("pool", "seq"),
        P(),
        P("seq", None),
        P(("seq", "pool"), None),
    )
    return jax.shard_map(
        on_device,
        mesh=mesh,
        in_specs=placed,
        out_specs=P("seq", "pool", None, None, None),
        check_vma=False,
    )
```
